128 devices in a mesh: space: 16 (over y_lo, x, core), tm: 8 (over z, y_hi).
Axes of the slice: x: 4, y: 4 (y_hi: 2, y_lo: 2; y = y_hi * 2 + y_lo), z: 4, core: 2. Of those that a mesh axis runs over, the one named last changes fastest.
Arguments:
- tokens: bfloat16 [16, 32, 64, 768], P('space', 'tm'), may hold values from -6 to 6
- grad_out: bfloat16 [16, 32, 64, 768], P('space', 'tm'), may hold values from -48 to 48
- w_qkv: bfloat16 [768, 1152], replicated, may hold values from -0.21875 to 0.21875
- w_out: bfloat16 [384, 768], replicated, may hold values from -0.3125 to 0.3125
- brain_mask: int32 [16], replicated, may hold values from 0 to 1, as said below
- block_table: int32 [16], replicated, may hold values from 0 to 15, each once
Outputs:
- token_grads: bfloat16 [16, 32, 64, 768], P('space', 'tm')
- qkv_grads: float32 [768, 1152], replicated
- out_grads: float32 [384, 768], replicated
The draws below stay inside these ranges and needn't reach their ends.
Inputs may be any that keep to these rules, and one draw needn't show every extreme that they name: `brain_mask`: 1 marks a block inside the brain; between 8 and 12 of the 16 blocks are marked. Slot s holds block block_table[s]; every block appears once.
All inputs are finite; a program needn't handle non-finite values.
Results may differ from the reference program's by a relative error of at most 0.015.
The reference program's roundings to bfloat16 on the way (of `projected`, `grad_attended`, `weights_low`, `attended`, `grad_scores` and `grad_query`) count: a program that leaves them out, or rounds other values in their place, can miss the bound.
Values may be sent and summed in bfloat16 or wider, within the bound.
A program may use at most 192 MiB of HBM per device.

```python
import jax
import jax.numpy as jnp
from jax import lax

D = 768
HEADS = 6
HD = 64
SIDE = 4
BP = 64
RAD_S = 3
RAD_T = 2
BLOCKS = 16
FRAMES = 32
HW = 384


def draw_brain_mask(key, part):
    marked_count = jax.random.randint(jax.random.fold_in(key, 11), (), 8, 13)
    shuffled = jax.random.permutation(jax.random.fold_in(key, 12), BLOCKS)
    return (shuffled < marked_count).astype(jnp.int32)


def block_levels(key, extent, split, smallest, top_value):
    level = 1.0
    for position, parts in split:
        draws = jax.random.uniform(jax.random.fold_in(jax.random.fold_in(key, 6), position), (parts,), jnp.float32, smallest / len(split), top_value / len(split))
        level = level * jnp.repeat(jnp.exp(draws), extent[position] // parts).reshape((-1,) + (1,) * (len(extent) - 1 - position))
    return level


def gaussian(rng, extent, scale, limit, shards=(), kind=jnp.bfloat16):
    result = jax.random.normal(rng, extent, jnp.float32) * scale
    if len(shards) > 0:
        result = block_levels(rng, extent, shards, -0.22, 0.18) * result
    return jnp.clip(result, min=-limit, max=limit).astype(kind)


def setup_inputs(seed: int = 0) -> dict:
    splits = jax.random.split(jax.random.key(seed), 7)
    return {
        "tokens": gaussian(splits[0], (BLOCKS, FRAMES, BP, D), 1.0, 6.0, ((0, 16), (1, 8))),
        "grad_out": gaussian(splits[1], (BLOCKS, FRAMES, BP, D), 8.0, 48.0, ((0, 16), (1, 8))),
        "w_qkv": gaussian(splits[2], (D, 3 * HW), D ** -0.5, 0.21875),
        "w_out": gaussian(splits[3], (HW, D), HW ** -0.5, 0.3125),
        "brain_mask": draw_brain_mask(jax.random.fold_in(splits[6], 71), 0),
        "block_table": jax.random.permutation(splits[5], BLOCKS).astype(jnp.int32),
    }


NEIGHBOURS = ((-1, -1), (-1, 0), (-1, 1), (0, -1), (0, 0), (0, 1), (1, -1), (1, 0), (1, 1))

def lookup_many(values, indices):
    positions = jnp.arange(values.shape[0], dtype=jnp.int32)
    picked = jnp.where(indices[:, None] == positions[None, :], values[None, :], 0)
    return lax.optimization_barrier(jnp.sum(picked, axis=1)).astype(jnp.int32)

def inverse_table(block_table):
    positions = jnp.arange(block_table.shape[0], dtype=jnp.int32)
    picked = jnp.where(block_table[:, None] == positions[None, :], positions[:, None], 0)
    return lax.optimization_barrier(jnp.sum(picked, axis=0)).astype(jnp.int32)

def neighbour_blocks(block_number, brain_mask):
    offsets = jnp.array(NEIGHBOURS, dtype=jnp.int32)
    near_row = block_number // SIDE + offsets[:, 0]
    near_col = block_number % SIDE + offsets[:, 1]
    inside = (near_row >= 0) & (near_row < SIDE) & (near_col >= 0) & (near_col < SIDE)
    nearby = (jnp.clip(near_row, 0, SIDE - 1) * SIDE + jnp.clip(near_col, 0, SIDE - 1)).astype(jnp.int32)
    usable = inside & (lookup_many(brain_mask, nearby) == 1)
    return (nearby, usable)

def token_places(blocks, first_frame, frame_count):
    patches = jnp.arange(BP, dtype=jnp.int32)
    frames = first_frame + jnp.arange(frame_count, dtype=jnp.int32)
    grid_shape = (blocks.shape[0], frame_count, BP)
    place_x = jnp.broadcast_to((blocks // SIDE)[:, None, None] * 4 + (patches // 16)[None, None, :], grid_shape)
    place_y = jnp.broadcast_to((blocks % SIDE)[:, None, None] * 4 + (patches // 4 % 4)[None, None, :], grid_shape)
    place_t = jnp.broadcast_to(frames[None, :, None], grid_shape)
    return (place_x.reshape(-1), place_y.reshape(-1), place_t.reshape(-1))

def window_allowed(row_places, col_places):
    near_x = jnp.abs(row_places[0][:, None] - col_places[0][None, :]) <= RAD_S
    near_y = jnp.abs(row_places[1][:, None] - col_places[1][None, :]) <= RAD_S
    near_t = jnp.abs(row_places[2][:, None] - col_places[2][None, :]) <= RAD_T
    return near_x & near_y & near_t

def key_usable(usable, first_frame, frame_count, frames_total):
    frames = first_frame + jnp.arange(frame_count, dtype=jnp.int32)
    inside = (frames >= 0) & (frames < frames_total)
    full = usable[:, None, None] & inside[None, :, None] & jnp.ones((1, 1, BP), dtype=jnp.bool_)
    return full.reshape(-1)

def tile_grad(query_rows, grad_rows, key_rows, allowed, brain_flag):
    row_count = query_rows.shape[0]
    key_count = key_rows.shape[0]
    features = query_rows.shape[1]
    scaling = HD ** (-0.5)
    query_heads = query_rows.reshape(row_count, HEADS, HD).astype(jnp.float32)
    grad_heads = grad_rows.reshape(row_count, HEADS, HD).astype(jnp.float32)
    key_heads = key_rows[:, :features].reshape(key_count, HEADS, HD).astype(jnp.float32)
    value_heads = key_rows[:, features:].reshape(key_count, HEADS, HD).astype(jnp.float32)
    scores = scaling * jnp.einsum('rhd,khd->hrk', query_heads, key_heads)
    exp_scores = jnp.where(allowed[None], jnp.exp(scores), 0.0)
    totals = lax.optimization_barrier(jnp.sum(exp_scores, axis=2)) + (1.0 - brain_flag)
    softmax_weights = exp_scores / totals[:, :, None]
    weights_low = lax.optimization_barrier(softmax_weights.astype(jnp.bfloat16)).astype(jnp.float32)
    attended = (jnp.einsum('hrk,khd->rhd', weights_low, value_heads) * brain_flag).astype(jnp.bfloat16)
    attended_wide = lax.optimization_barrier(attended).astype(jnp.float32)
    deltas = lax.optimization_barrier(jnp.sum(grad_heads * attended_wide, axis=2))
    grad_weights = jnp.einsum('rhd,khd->hrk', grad_heads, value_heads)
    grad_scores = (softmax_weights * (grad_weights - deltas.T[:, :, None])).astype(jnp.bfloat16)
    grad_scores = lax.optimization_barrier(grad_scores).astype(jnp.float32)
    grad_query = scaling * jnp.einsum('hrk,khd->rhd', grad_scores, key_heads) * brain_flag
    grad_key = scaling * jnp.einsum('hrk,rhd->khd', grad_scores, query_heads) * brain_flag
    grad_value = jnp.einsum('hrk,rhd->khd', weights_low, grad_heads) * brain_flag
    return (grad_query.reshape(row_count, features), attended.reshape(row_count, features), grad_key.reshape(key_count, features), grad_value.reshape(key_count, features))

def reference(tokens, grad_out, w_qkv, w_out, brain_mask, block_table):
    features = HEADS * HD
    key_span = 2 + 2 * RAD_T
    tile_count = FRAMES // 2
    flat_tokens = tokens.reshape(-1, D)
    projected = jnp.dot(flat_tokens, w_qkv, preferred_element_type=jnp.float32).astype(jnp.bfloat16)
    projected = projected.reshape(BLOCKS, FRAMES, BP, 3 * features)
    queries = projected[..., :features]
    key_values = projected[..., features:]
    flat_grad = grad_out.reshape(-1, D)
    grad_attended = jnp.dot(flat_grad, w_out.T, preferred_element_type=jnp.float32).astype(jnp.bfloat16)
    grad_attended = grad_attended.reshape(BLOCKS, FRAMES, BP, features)
    padded = jnp.pad(key_values, ((0, 0), (RAD_T, RAD_T), (0, 0), (0, 0)))
    slot_of_block = inverse_table(block_table)
    zero_index = jnp.int32(0)

    def one_tile(summed, step_index):
        slot_index = (step_index // tile_count).astype(jnp.int32)
        tile_index = (step_index % tile_count).astype(jnp.int32)
        block_number = lookup_many(block_table, slot_index[None])[0]
        brain_flag = lookup_many(brain_mask, block_number[None])[0].astype(jnp.float32)
        nearby, usable = neighbour_blocks(block_number, brain_mask)
        near_slots = lookup_many(slot_of_block, nearby)
        first_frame = (2 * tile_index).astype(jnp.int32)
        query_rows = lax.dynamic_slice(queries, (slot_index, first_frame, zero_index, zero_index), (1, 2, BP, features)).reshape(-1, features)
        grad_rows = lax.dynamic_slice(grad_attended, (slot_index, first_frame, zero_index, zero_index), (1, 2, BP, features)).reshape(-1, features)
        frame_window = lax.dynamic_slice_in_dim(padded, first_frame, key_span, 1)
        key_rows = jnp.take(frame_window, near_slots, axis=0).reshape(-1, 2 * features)
        row_places = token_places(block_number[None], first_frame, 2)
        col_places = token_places(nearby, first_frame - RAD_T, key_span)
        allowed = window_allowed(row_places, col_places)
        allowed = allowed & key_usable(usable, first_frame - RAD_T, key_span, FRAMES)[None, :]
        grad_query, attended, grad_key, grad_value = tile_grad(query_rows, grad_rows, key_rows, allowed, brain_flag)
        near_frames = first_frame + jnp.arange(key_span, dtype=jnp.int32)
        update = jnp.concatenate([grad_key, grad_value], axis=1).reshape(9, key_span, BP, 2 * features)
        summed = summed.at[near_slots[:, None], near_frames[None, :]].add(update)
        return (summed, (grad_query, attended))
    start = jnp.zeros((BLOCKS, FRAMES + 2 * RAD_T, BP, 2 * features), jnp.float32)
    summed, (query_tiles, attended_tiles) = lax.scan(one_tile, start, jnp.arange(BLOCKS * tile_count, dtype=jnp.int32))
    grad_query = query_tiles.reshape(BLOCKS, FRAMES, BP, features).astype(jnp.bfloat16)
    attended = attended_tiles.reshape(BLOCKS, FRAMES, BP, features)
    key_grads = summed[:, RAD_T:RAD_T + FRAMES].astype(jnp.bfloat16)
    grads = jnp.concatenate([grad_query, key_grads], axis=3).reshape(-1, 3 * features)
    token_grads = jnp.dot(grads, w_qkv.T, preferred_element_type=jnp.float32).astype(jnp.bfloat16).reshape(tokens.shape)
    qkv_grads = jnp.dot(flat_tokens.T, grads, preferred_element_type=jnp.float32)
    out_grads = jnp.dot(attended.reshape(-1, features).T, flat_grad, preferred_element_type=jnp.float32)
    return (token_grads, qkv_grads, out_grads)
```

```python
import functools

import numpy as np
import jax
import jax.numpy as jnp
from jax import lax
from jax.experimental import pallas as pl
from jax.experimental.pallas import tpu as pltpu
from jax.sharding import PartitionSpec as P

D = 768
HEADS = 6
HD = 64
SIDE = 4
BP = 64
RAD_S = 3
RAD_T = 2
HW = HEADS * HD
LF = 4
KF = 6
KR = KF * BP
QR = 2 * BP
WORKERS = 2 * HEADS
ANY = pl.ANY


def where_lane(low, high):
    lane = lax.broadcasted_iota(jnp.int32, low.shape, low.ndim - 1)
    return jnp.where(lane < HD, low, high)


def project_kernel(tok_ref, gout_ref, wqkv_ref, wout_ref, out_ref):
    proj = jnp.dot(tok_ref[...], wqkv_ref[...], preferred_element_type=jnp.float32)
    gatt = lax.dot_general(
        gout_ref[...], wout_ref[...], (((1,), (1,)), ((), ())),
        preferred_element_type=jnp.float32,
    )

    def pair(low, high):
        first = where_lane(low, pltpu.roll(high, HD, 1)).astype(jnp.bfloat16)
        second = where_lane(pltpu.roll(low, HD, 1), high).astype(jnp.bfloat16)
        return first.reshape(LF, BP, 128), second.reshape(LF, BP, 128)

    for i in range(HEADS // 2):
        at = 128 * i
        keys = pair(proj[:, HW + at : HW + at + 128], proj[:, 2 * HW + at : 2 * HW + at + 128])
        queries = pair(proj[:, at : at + 128], gatt[:, at : at + 128])
        for j in range(2):
            out_ref[2 * i + j, 0:2] = queries[j][0:2]
            out_ref[2 * i + j, 2:6] = keys[j]
            out_ref[2 * i + j, 6:8] = queries[j][2:4]


def project(tokens, grad_out, w_qkv, w_out):
    vmem = pl.BlockSpec(memory_space=pltpu.VMEM)
    return pl.pallas_call(
        project_kernel,
        out_shape=jax.ShapeDtypeStruct((HEADS, 8, BP, 128), jnp.bfloat16),
        in_specs=[vmem] * 4,
        out_specs=vmem,
        compiler_params=pltpu.CompilerParams(vmem_limit_bytes=40 << 20),
        name="project",
    )(tokens, grad_out, w_qkv, w_out)


def spread_kernel(tm_size, src, main, halo, ssem, hsem, rsem, rhsem):
    me = lax.axis_index("space")
    t = lax.axis_index("tm")
    after = lax.rem(t + 1, tm_size)
    before = lax.rem(t + tm_size - 1, tm_size)

    def main_copy(w):
        return pltpu.make_async_remote_copy(
            src_ref=src.at[w // 2, pl.ds(2 * (w % 2), 6)],
            dst_ref=main.at[me],
            send_sem=ssem.at[w],
            recv_sem=rsem,
            device_id={"space": w, "tm": t},
            device_id_type=pl.DeviceIdType.MESH,
        )

    def halo_copy(h, half):
        return pltpu.make_async_remote_copy(
            src_ref=src.at[h, pl.ds(4 - 2 * half, 2)],
            dst_ref=halo.at[me],
            send_sem=hsem.at[2 * h + half],
            recv_sem=rhsem,
            device_id={"space": 2 * h + half, "tm": before if half else after},
            device_id_type=pl.DeviceIdType.MESH,
        )

    def send(i, carry):
        w = lax.rem(i + me, WORKERS)

        @pl.when(w != me)
        def _():
            main_copy(w).start()

        @pl.when(w == me)
        def _():
            pltpu.make_async_copy(
                src.at[w // 2, pl.ds(2 * (w % 2), 6)], main.at[me], rsem
            ).start()

        return carry

    def send_halo(i, carry):
        h = lax.rem(i + me // 2, HEADS)
        halo_copy(h, 0).start()
        halo_copy(h, 1).start()
        return carry

    lax.fori_loop(0, HEADS, send_halo, 0)
    lax.fori_loop(0, WORKERS, send, 0)

    def finish(w, carry):
        @pl.when(w != me)
        def _():
            main_copy(w).wait_send()

        return carry

    def finish_halo(h, carry):
        halo_copy(h, 0).wait_send()
        halo_copy(h, 1).wait_send()
        return carry

    @pl.when(me < WORKERS)
    def _():
        pltpu.make_async_copy(halo, halo, rhsem).wait()
        pltpu.make_async_copy(main, main, rsem).wait()

    lax.fori_loop(0, HEADS, finish_halo, 0)
    lax.fori_loop(0, WORKERS, finish, 0)


def spread(packed, slots, tm_size):
    any_spec = pl.BlockSpec(memory_space=ANY)
    return pl.pallas_call(
        functools.partial(spread_kernel, tm_size),
        out_shape=(
            jax.ShapeDtypeStruct((slots, 6, BP, 128), jnp.bfloat16),
            jax.ShapeDtypeStruct((slots, 2, BP, 128), jnp.bfloat16),
        ),
        in_specs=[any_spec],
        out_specs=(any_spec, any_spec),
        scratch_shapes=[
            pltpu.SemaphoreType.DMA((WORKERS,)),
            pltpu.SemaphoreType.DMA((WORKERS,)),
            pltpu.SemaphoreType.DMA,
            pltpu.SemaphoreType.DMA,
        ],
        compiler_params=pltpu.CompilerParams(has_side_effects=True),
        name="spread",
    )(packed)


def collect_kernel(slots, tm_size, main, halo, got, got_halo, ssem, hsem, rsem, rhsem):
    me = lax.axis_index("space")
    t = lax.axis_index("tm")
    head = me // 2
    half = me % 2
    other = lax.rem(t + tm_size + 2 * half - 1, tm_size)

    def main_copy(s):
        return pltpu.make_async_remote_copy(
            src_ref=main.at[s],
            dst_ref=got.at[half, head],
            send_sem=ssem.at[s],
            recv_sem=rsem,
            device_id={"space": s, "tm": t},
            device_id_type=pl.DeviceIdType.MESH,
        )

    def halo_copy(s):
        return pltpu.make_async_remote_copy(
            src_ref=halo.at[s],
            dst_ref=got_halo.at[half, head],
            send_sem=hsem.at[s],
            recv_sem=rhsem,
            device_id={"space": s, "tm": other},
            device_id_type=pl.DeviceIdType.MESH,
        )

    def send(i, carry):
        s = lax.rem(i + me, slots)

        @pl.when(s != me)
        def _():
            main_copy(s).start()

        @pl.when(s == me)
        def _():
            pltpu.make_async_copy(main.at[s], got.at[half, head], rsem).start()

        return carry

    def send_halo(i, carry):
        halo_copy(lax.rem(i + me, slots)).start()
        return carry

    def finish(s, carry):
        @pl.when(s != me)
        def _():
            main_copy(s).wait_send()

        return carry

    def finish_halo(s, carry):
        halo_copy(s).wait_send()
        return carry

    @pl.when(me < WORKERS)
    def _():
        lax.fori_loop(0, slots, send_halo, 0)
        lax.fori_loop(0, slots, send, 0)

    pltpu.make_async_copy(got_halo, got_halo, rhsem).wait()
    pltpu.make_async_copy(got, got, rsem).wait()

    @pl.when(me < WORKERS)
    def _():
        lax.fori_loop(0, slots, finish_halo, 0)
        lax.fori_loop(0, slots, finish, 0)


def collect(main, halo, slots, tm_size):
    any_spec = pl.BlockSpec(memory_space=ANY)
    return pl.pallas_call(
        functools.partial(collect_kernel, slots, tm_size),
        out_shape=(
            jax.ShapeDtypeStruct((2, HEADS, 6, BP, 128), jnp.bfloat16),
            jax.ShapeDtypeStruct((2, HEADS, 2, BP, 128), jnp.bfloat16),
        ),
        in_specs=[any_spec, any_spec],
        out_specs=(any_spec, any_spec),
        scratch_shapes=[
            pltpu.SemaphoreType.DMA((slots,)),
            pltpu.SemaphoreType.DMA((slots,)),
            pltpu.SemaphoreType.DMA,
            pltpu.SemaphoreType.DMA,
        ],
        compiler_params=pltpu.CompilerParams(has_side_effects=True),
        name="collect",
    )(main, halo)


def window_bias():
    patch = np.arange(BP)
    px, py = patch // 16, patch // 4 % 4
    out = np.zeros((9, KF, BP, 2, BP), np.float32)
    for n in range(9):
        dr, dc = n // 3 - 1, n % 3 - 1
        near_x = np.abs(px[:, None] + 4 * dr - px[None, :]) <= RAD_S
        near_y = np.abs(py[:, None] + 4 * dc - py[None, :]) <= RAD_S
        for j in range(KF):
            for i in range(2):
                near = near_x & near_y & (abs(j - RAD_T - i) <= RAD_T)
                out[n, j, :, i, :] = np.where(near, 0.0, -np.inf)
    return out.reshape(9, KR, QR)


def attend_kernel(
    tm_size, table, mask, main, halo, bias_hbm, out_main, out_halo,
    kv, kvt, q, bias, acc, scores, dots, low, res_q, res_kv, slot_of, near_slot, near_off, sem,
):
    me = lax.axis_index("space")
    t = lax.axis_index("tm")
    half = me % 2
    slots = kv.shape[0]
    scaling = HD ** (-0.5)

    @pl.when(me < WORKERS)
    def _():
        loads = [
            pltpu.make_async_copy(
                main.at[:, pl.ds(2 - 2 * half, 4)], kv.at[:, pl.ds(2 - 2 * half, 4)], sem.at[0]
            ),
            pltpu.make_async_copy(halo, kv.at[:, pl.ds(4 * half, 2)], sem.at[1]),
            pltpu.make_async_copy(main.at[:, pl.ds(4 * half, 2)], q, sem.at[2]),
            pltpu.make_async_copy(bias_hbm, bias, sem.at[3]),
        ]
        for load in loads:
            load.start()
        acc[...] = jnp.zeros_like(acc)
        res_q[...] = jnp.zeros_like(res_q)

        def place(s, carry):
            slot_of[table[s]] = s
            return carry

        lax.fori_loop(0, slots, place, 0)
        for load in loads:
            load.wait()

        @pl.when((t == 0) & (half == 0))
        def _():
            bias[:, 0 : 2 * BP, :] = jnp.full((9, 2 * BP, QR), -jnp.inf, jnp.float32)

        @pl.when((t == tm_size - 1) & (half == 1))
        def _():
            bias[:, 4 * BP : 6 * BP, :] = jnp.full((9, 2 * BP, QR), -jnp.inf, jnp.float32)

        def flip(s, carry):
            kvt[s] = kv[s].reshape(KR, 128).T
            return carry

        lax.fori_loop(0, slots, flip, 0)

        def one_block(g, carry):
            @pl.when(mask[g] == 1)
            def _():
                slot = slot_of[g]
                row = g // SIDE
                col = g % SIDE
                count = jnp.int32(0)
                for n in range(9):
                    nr = row + (n // 3 - 1)
                    nc = col + (n % 3 - 1)
                    inside = (nr >= 0) & (nr < SIDE) & (nc >= 0) & (nc < SIDE)
                    nb = jnp.clip(nr, 0, SIDE - 1) * SIDE + jnp.clip(nc, 0, SIDE - 1)
                    valid = inside & (mask[nb] == 1)
                    near_slot[count] = slot_of[nb]
                    near_off[count] = n
                    count = count + valid.astype(jnp.int32)

                rows = q[slot].reshape(QR, 128)
                cols = rows.T
                zero = jnp.zeros_like(cols)
                first = lax.broadcasted_iota(jnp.int32, cols.shape, 0) < HD
                left = lax.broadcasted_iota(jnp.int32, cols.shape, 1) < HD
                rhs_a = jnp.concatenate(
                    [jnp.where(first, cols, zero), jnp.where(first, zero, cols)], axis=1
                )
                rhs_d = jnp.concatenate(
                    [jnp.where(left, rows, zero), jnp.where(left, zero, rows)], axis=0
                )

                def score(k, total):
                    keys = kv[near_slot[k]].reshape(KR, 128)
                    both = jnp.dot(keys, rhs_a, preferred_element_type=jnp.float32)
                    e = jnp.exp(both[:, :QR] * scaling + bias[near_off[k]])
                    scores[k] = e
                    dots[k] = both[:, QR:]
                    return total + jnp.sum(e.reshape(KR // 8, 8, QR), axis=0)

                total = lax.fori_loop(0, count, score, jnp.zeros((8, QR), jnp.float32))
                inverse = 1.0 / jnp.sum(total, axis=0, keepdims=True)

                def weigh(k, out):
                    w = (scores[k] * inverse).astype(jnp.bfloat16)
                    low[k] = w
                    return out + jnp.dot(
                        kvt[near_slot[k], HD:, :], w, preferred_element_type=jnp.float32
                    )

                att = lax.fori_loop(0, count, weigh, jnp.zeros((HD, QR), jnp.float32))
                att = att.astype(jnp.bfloat16).astype(jnp.float32)
                delta = jnp.sum(cols[HD:].astype(jnp.float32) * att, axis=0, keepdims=True)

                def spread_grad(k, out):
                    ds = (scores[k] * inverse * (dots[k] - delta)).astype(jnp.bfloat16)
                    lhs = jnp.concatenate([ds, low[k]], axis=1)
                    acc[near_slot[k]] += jnp.dot(lhs, rhs_d, preferred_element_type=jnp.float32)
                    return out + jnp.dot(
                        kvt[near_slot[k], :HD, :], ds, preferred_element_type=jnp.float32
                    )

                dq = lax.fori_loop(0, count, spread_grad, jnp.zeros((HD, QR), jnp.float32))
                both = jnp.concatenate([dq * scaling, att], axis=0).T
                res_q[slot] = both.astype(jnp.bfloat16).reshape(2, BP, 128)

            return carry

        lax.fori_loop(0, slots, one_block, 0)

        def finish(s, carry):
            total = acc[s]
            res_kv[s] = where_lane(total * scaling, total).astype(jnp.bfloat16).reshape(KF, BP, 128)
            return carry

        lax.fori_loop(0, slots, finish, 0)
        stores = [
            pltpu.make_async_copy(
                res_kv.at[:, pl.ds(2 - 2 * half, 4)], out_main.at[:, pl.ds(2 - 2 * half, 4)], sem.at[0]
            ),
            pltpu.make_async_copy(res_kv.at[:, pl.ds(4 * half, 2)], out_halo, sem.at[1]),
            pltpu.make_async_copy(res_q, out_main.at[:, pl.ds(4 * half, 2)], sem.at[2]),
        ]
        for store in stores:
            store.start()
        for store in stores:
            store.wait()


def attend(block_table, brain_mask, main, halo, tm_size):
    slots = main.shape[0]
    any_spec = pl.BlockSpec(memory_space=ANY)
    smem = pl.BlockSpec(memory_space=pltpu.SMEM)
    return pl.pallas_call(
        functools.partial(attend_kernel, tm_size),
        out_shape=(
            jax.ShapeDtypeStruct((slots, 6, BP, 128), jnp.bfloat16),
            jax.ShapeDtypeStruct((slots, 2, BP, 128), jnp.bfloat16),
        ),
        in_specs=[smem, smem, any_spec, any_spec, any_spec],
        out_specs=(any_spec, any_spec),
        scratch_shapes=[
            pltpu.VMEM((slots, KF, BP, 128), jnp.bfloat16),
            pltpu.VMEM((slots, 128, KR), jnp.bfloat16),
            pltpu.VMEM((slots, 2, BP, 128), jnp.bfloat16),
            pltpu.VMEM((9, KR, QR), jnp.float32),
            pltpu.VMEM((slots, KR, 128), jnp.float32),
            pltpu.VMEM((9, KR, QR), jnp.float32),
            pltpu.VMEM((9, KR, QR), jnp.float32),
            pltpu.VMEM((9, KR, QR), jnp.bfloat16),
            pltpu.VMEM((slots, 2, BP, 128), jnp.bfloat16),
            pltpu.VMEM((slots, KF, BP, 128), jnp.bfloat16),
            pltpu.SMEM((16,), jnp.int32),
            pltpu.SMEM((16,), jnp.int32),
            pltpu.SMEM((16,), jnp.int32),
            pltpu.SemaphoreType.DMA((4,)),
        ],
        compiler_params=pltpu.CompilerParams(vmem_limit_bytes=56 << 20),
        name="attend",
    )(block_table, brain_mask, main, halo, jnp.asarray(window_bias()))


def last_kernel(got_ref, halo_ref, tok_ref, gout_ref, wqkv_ref, tg_ref, terms_ref, grads, att):
    def pair(a, b):
        low = where_lane(a, pltpu.roll(b, HD, 1))
        high = where_lane(pltpu.roll(a, HD, 1), b)
        return low.astype(jnp.bfloat16), high.astype(jnp.bfloat16)

    for i in range(HEADS // 2):
        at = 128 * i
        kvs, qas = [], []
        for h in (2 * i, 2 * i + 1):
            first = got_ref[0, h].astype(jnp.float32)
            second = got_ref[1, h].astype(jnp.float32)
            edge = jnp.concatenate([halo_ref[1, h], halo_ref[0, h]], axis=0).astype(jnp.float32)
            kvs.append((first[2:6] + second[0:4] + edge).reshape(LF * BP, 128))
            qas.append(jnp.concatenate([first[0:2], second[4:6]], axis=0).reshape(LF * BP, 128))
        dk, dv = pair(*kvs)
        dq, da = pair(*qas)
        grads[:, at : at + 128] = dq
        grads[:, HW + at : HW + at + 128] = dk
        grads[:, 2 * HW + at : 2 * HW + at + 128] = dv
        att[:, at : at + 128] = da
    tg_ref[...] = lax.dot_general(
        grads[...], wqkv_ref[...], (((1,), (1,)), ((), ())), preferred_element_type=jnp.float32
    ).astype(jnp.bfloat16)
    tok_t = tok_ref[...].T
    att_t = att[...].T
    for i in range(9):
        terms_ref[768 * i : 768 * (i + 1), :] = jnp.dot(
            tok_t, grads[:, 128 * i : 128 * (i + 1)], preferred_element_type=jnp.float32
        ).astype(terms_ref.dtype)
    for i in range(6):
        terms_ref[6912 + 384 * i : 6912 + 384 * (i + 1), :] = jnp.dot(
            att_t, gout_ref[:, 128 * i : 128 * (i + 1)], preferred_element_type=jnp.float32
        ).astype(terms_ref.dtype)


def last(got, got_halo, tokens, grad_out, w_qkv):
    vmem = pl.BlockSpec(memory_space=pltpu.VMEM)
    return pl.pallas_call(
        last_kernel,
        out_shape=(
            jax.ShapeDtypeStruct((LF * BP, D), jnp.bfloat16),
            jax.ShapeDtypeStruct((9216, 128), jnp.float32),
        ),
        in_specs=[vmem] * 5,
        out_specs=(vmem, vmem),
        scratch_shapes=[
            pltpu.VMEM((LF * BP, 3 * HW), jnp.bfloat16),
            pltpu.VMEM((LF * BP, HW), jnp.bfloat16),
        ],
        compiler_params=pltpu.CompilerParams(vmem_limit_bytes=40 << 20),
        name="last",
    )(got, got_halo, tokens, grad_out, w_qkv)


def shards(tokens, grad_out, w_qkv, w_out, brain_mask, block_table):
    slots = lax.axis_size("space")
    tm_size = lax.axis_size("tm")
    flat_tokens = tokens.reshape(-1, D)
    flat_grad = grad_out.reshape(-1, D)
    packed = project(flat_tokens, flat_grad, w_qkv, w_out)
    main, halo = spread(packed, slots, tm_size)
    main, halo = attend(block_table, brain_mask, main, halo, tm_size)
    got, got_halo = collect(main, halo, slots, tm_size)
    token_grads, terms = last(got, got_halo, flat_tokens, flat_grad, w_qkv)
    terms = lax.psum(terms, ("space", "tm"))
    qkv_grads = terms[:6912].reshape(9, D, 128).transpose(1, 0, 2).reshape(D, 3 * HW)
    out_grads = terms[6912:].reshape(6, HW, 128).transpose(1, 0, 2).reshape(HW, D)
    return (token_grads.reshape(tokens.shape), qkv_grads, out_grads)


def solution(mesh):
    in_specs = (P("space", "tm", None, None), P("space", "tm", None, None), P(), P(), P(), P())
    out_specs = (P("space", "tm", None, None), P(), P())
    return jax.shard_map(shards, mesh=mesh, in_specs=in_specs, out_specs=out_specs, check_vma=False)
```

```python
import functools

import numpy as np
import jax
import jax.numpy as jnp
from jax import lax
from jax.experimental import pallas as pl
from jax.experimental.pallas import tpu as pltpu
from jax.sharding import PartitionSpec as P

D = 768
HEADS = 6
HD = 64
SIDE = 4
BP = 64
RAD_S = 3
RAD_T = 2
HW = HEADS * HD
LF = 4
KF = 6
KR = KF * BP
QR = 2 * BP
WORKERS = 2 * HEADS
ANY = pl.ANY


def where_lane(low, high):
    lane = lax.broadcasted_iota(jnp.int32, low.shape, low.ndim - 1)
    return jnp.where(lane < HD, low, high)


def project_kernel(tok_ref, gout_ref, wqkv_ref, wout_ref, out_ref):
    proj = jnp.dot(tok_ref[...], wqkv_ref[...], preferred_element_type=jnp.float32)
    gatt = lax.dot_general(
        gout_ref[...], wout_ref[...], (((1,), (1,)), ((), ())),
        preferred_element_type=jnp.float32,
    )

    def pair(low, high):
        first = where_lane(low, pltpu.roll(high, HD, 1)).astype(jnp.bfloat16)
        second = where_lane(pltpu.roll(low, HD, 1), high).astype(jnp.bfloat16)
        return first.reshape(LF, BP, 128), second.reshape(LF, BP, 128)

    for i in range(HEADS // 2):
        at = 128 * i
        keys = pair(proj[:, HW + at : HW + at + 128], proj[:, 2 * HW + at : 2 * HW + at + 128])
        queries = pair(proj[:, at : at + 128], gatt[:, at : at + 128])
        for j in range(2):
            out_ref[2 * i + j, 0:2] = queries[j][0:2]
            out_ref[2 * i + j, 2:6] = keys[j]
            out_ref[2 * i + j, 6:8] = queries[j][2:4]


def project(tokens, grad_out, w_qkv, w_out):
    vmem = pl.BlockSpec(memory_space=pltpu.VMEM)
    return pl.pallas_call(
        project_kernel,
        out_shape=jax.ShapeDtypeStruct((HEADS, 8, BP, 128), jnp.bfloat16),
        in_specs=[vmem] * 4,
        out_specs=vmem,
        compiler_params=pltpu.CompilerParams(vmem_limit_bytes=40 << 20),
        name="project",
    )(tokens, grad_out, w_qkv, w_out)


def spread_kernel(tm_size, src, main, halo, ssem, hsem, rsem, rhsem):
    me = lax.axis_index("space")
    t = lax.axis_index("tm")
    after = lax.rem(t + 1, tm_size)
    before = lax.rem(t + tm_size - 1, tm_size)

    def main_copy(w):
        return pltpu.make_async_remote_copy(
            src_ref=src.at[w // 2, pl.ds(2 * (w % 2), 6)],
            dst_ref=main.at[me],
            send_sem=ssem.at[w],
            recv_sem=rsem,
            device_id={"space": w, "tm": t},
            device_id_type=pl.DeviceIdType.MESH,
        )

    def halo_copy(h, half):
        return pltpu.make_async_remote_copy(
            src_ref=src.at[h, pl.ds(4 - 2 * half, 2)],
            dst_ref=halo.at[me],
            send_sem=hsem.at[2 * h + half],
            recv_sem=rhsem,
            device_id={"space": 2 * h + half, "tm": before if half else after},
            device_id_type=pl.DeviceIdType.MESH,
        )

    def send(i, carry):
        w = lax.rem(i + me, WORKERS)

        @pl.when(w != me)
        def _():
            main_copy(w).start()

        @pl.when(w == me)
        def _():
            pltpu.make_async_copy(
                src.at[w // 2, pl.ds(2 * (w % 2), 6)], main.at[me], rsem
            ).start()

        return carry

    def send_halo(i, carry):
        h = lax.rem(i + me // 2, HEADS)
        halo_copy(h, 0).start()
        halo_copy(h, 1).start()
        return carry

    lax.fori_loop(0, HEADS, send_halo, 0)
    lax.fori_loop(0, WORKERS, send, 0)

    def finish(w, carry):
        @pl.when(w != me)
        def _():
            main_copy(w).wait_send()

        return carry

    def finish_halo(h, carry):
        halo_copy(h, 0).wait_send()
        halo_copy(h, 1).wait_send()
        return carry

    @pl.when(me < WORKERS)
    def _():
        pltpu.make_async_copy(halo, halo, rhsem).wait()
        pltpu.make_async_copy(main, main, rsem).wait()

    lax.fori_loop(0, HEADS, finish_halo, 0)
    lax.fori_loop(0, WORKERS, finish, 0)


def spread(packed, slots, tm_size):
    any_spec = pl.BlockSpec(memory_space=ANY)
    return pl.pallas_call(
        functools.partial(spread_kernel, tm_size),
        out_shape=(
            jax.ShapeDtypeStruct((slots, 6, BP, 128), jnp.bfloat16),
            jax.ShapeDtypeStruct((slots, 2, BP, 128), jnp.bfloat16),
        ),
        in_specs=[any_spec],
        out_specs=(any_spec, any_spec),
        scratch_shapes=[
            pltpu.SemaphoreType.DMA((WORKERS,)),
            pltpu.SemaphoreType.DMA((WORKERS,)),
            pltpu.SemaphoreType.DMA,
            pltpu.SemaphoreType.DMA,
        ],
        compiler_params=pltpu.CompilerParams(has_side_effects=True),
        name="spread",
    )(packed)


def collect_kernel(slots, tm_size, main, halo, got, got_halo, ssem, hsem, rsem, rhsem):
    me = lax.axis_index("space")
    t = lax.axis_index("tm")
    head = me // 2
    half = me % 2
    other = lax.rem(t + tm_size + 2 * half - 1, tm_size)

    def main_copy(s):
        return pltpu.make_async_remote_copy(
            src_ref=main.at[s],
            dst_ref=got.at[half, head],
            send_sem=ssem.at[s],
            recv_sem=rsem,
            device_id={"space": s, "tm": t},
            device_id_type=pl.DeviceIdType.MESH,
        )

    def halo_copy(s):
        return pltpu.make_async_remote_copy(
            src_ref=halo.at[s],
            dst_ref=got_halo.at[half, head],
            send_sem=hsem.at[s],
            recv_sem=rhsem,
            device_id={"space": s, "tm": other},
            device_id_type=pl.DeviceIdType.MESH,
        )

    def send(i, carry):
        s = lax.rem(i + me, slots)

        @pl.when(s != me)
        def _():
            main_copy(s).start()

        @pl.when(s == me)
        def _():
            pltpu.make_async_copy(main.at[s], got.at[half, head], rsem).start()

        return carry

    def send_halo(i, carry):
        halo_copy(lax.rem(i + me, slots)).start()
        return carry

    def finish(s, carry):
        @pl.when(s != me)
        def _():
            main_copy(s).wait_send()

        return carry

    def finish_halo(s, carry):
        halo_copy(s).wait_send()
        return carry

    @pl.when(me < WORKERS)
    def _():
        lax.fori_loop(0, slots, send_halo, 0)
        lax.fori_loop(0, slots, send, 0)

    pltpu.make_async_copy(got_halo, got_halo, rhsem).wait()
    pltpu.make_async_copy(got, got, rsem).wait()

    @pl.when(me < WORKERS)
    def _():
        lax.fori_loop(0, slots, finish_halo, 0)
        lax.fori_loop(0, slots, finish, 0)


def collect(main, halo, slots, tm_size):
    any_spec = pl.BlockSpec(memory_space=ANY)
    return pl.pallas_call(
        functools.partial(collect_kernel, slots, tm_size),
        out_shape=(
            jax.ShapeDtypeStruct((2, HEADS, 6, BP, 128), jnp.bfloat16),
            jax.ShapeDtypeStruct((2, HEADS, 2, BP, 128), jnp.bfloat16),
        ),
        in_specs=[any_spec, any_spec],
        out_specs=(any_spec, any_spec),
        scratch_shapes=[
            pltpu.SemaphoreType.DMA((slots,)),
            pltpu.SemaphoreType.DMA((slots,)),
            pltpu.SemaphoreType.DMA,
            pltpu.SemaphoreType.DMA,
        ],
        compiler_params=pltpu.CompilerParams(has_side_effects=True),
        name="collect",
    )(main, halo)


def window_bias():
    patch = np.arange(BP)
    px, py = patch // 16, patch // 4 % 4
    out = np.zeros((9, KF, BP, 2, BP), np.float32)
    for n in range(9):
        dr, dc = n // 3 - 1, n % 3 - 1
        near_x = np.abs(px[:, None] + 4 * dr - px[None, :]) <= RAD_S
        near_y = np.abs(py[:, None] + 4 * dc - py[None, :]) <= RAD_S
        for j in range(KF):
            for i in range(2):
                near = near_x & near_y & (abs(j - RAD_T - i) <= RAD_T)
                out[n, j, :, i, :] = np.where(near, 0.0, -np.inf)
    return out.reshape(9, KR, QR)


def attend_kernel(
    tm_size, table, mask, main, halo, bias_hbm, out_main, out_halo,
    kv, kvt, q, bias, acc, scores, dots, low, res_q, res_kv, slot_of, near_slot, near_off, sem,
):
    me = lax.axis_index("space")
    t = lax.axis_index("tm")
    half = me % 2
    slots = kv.shape[0]
    scaling = HD ** (-0.5)

    @pl.when(me < WORKERS)
    def _():
        loads = [
            pltpu.make_async_copy(
                main.at[:, pl.ds(2 - 2 * half, 4)], kv.at[:, pl.ds(2 - 2 * half, 4)], sem.at[0]
            ),
            pltpu.make_async_copy(halo, kv.at[:, pl.ds(4 * half, 2)], sem.at[1]),
            pltpu.make_async_copy(main.at[:, pl.ds(4 * half, 2)], q, sem.at[2]),
            pltpu.make_async_copy(bias_hbm, bias, sem.at[3]),
        ]
        for load in loads:
            load.start()
        acc[...] = jnp.zeros_like(acc)
        res_q[...] = jnp.zeros_like(res_q)

        def place(s, carry):
            slot_of[table[s]] = s
            return carry

        lax.fori_loop(0, slots, place, 0)
        for load in loads:
            load.wait()

        @pl.when((t == 0) & (half == 0))
        def _():
            bias[:, 0 : 2 * BP, :] = jnp.full((9, 2 * BP, QR), -jnp.inf, jnp.float32)

        @pl.when((t == tm_size - 1) & (half == 1))
        def _():
            bias[:, 4 * BP : 6 * BP, :] = jnp.full((9, 2 * BP, QR), -jnp.inf, jnp.float32)

        def flip(s, carry):
            kvt[s] = kv[s].reshape(KR, 128).T
            return carry

        lax.fori_loop(0, slots, flip, 0)

        def one_block(g, carry):
            @pl.when(mask[g] == 1)
            def _():
                slot = slot_of[g]
                row = g // SIDE
                col = g % SIDE
                count = jnp.int32(0)
                for n in range(9):
                    nr = row + (n // 3 - 1)
                    nc = col + (n % 3 - 1)
                    inside = (nr >= 0) & (nr < SIDE) & (nc >= 0) & (nc < SIDE)
                    nb = jnp.clip(nr, 0, SIDE - 1) * SIDE + jnp.clip(nc, 0, SIDE - 1)
                    valid = inside & (mask[nb] == 1)
                    near_slot[count] = slot_of[nb]
                    near_off[count] = n
                    count = count + valid.astype(jnp.int32)

                rows = q[slot].reshape(QR, 128)
                cols = rows.T
                zero = jnp.zeros_like(cols)
                first = lax.broadcasted_iota(jnp.int32, cols.shape, 0) < HD
                left = lax.broadcasted_iota(jnp.int32, cols.shape, 1) < HD
                rhs_a = jnp.concatenate(
                    [jnp.where(first, cols, zero), jnp.where(first, zero, cols)], axis=1
                )
                rhs_d = jnp.concatenate(
                    [jnp.where(left, rows, zero), jnp.where(left, zero, rows)], axis=0
                )

                def score(k, total):
                    keys = kv[near_slot[k]].reshape(KR, 128)
                    both = jnp.dot(keys, rhs_a, preferred_element_type=jnp.float32)
                    e = jnp.exp(both[:, :QR] * scaling + bias[near_off[k]])
                    scores[k] = e
                    dots[k] = both[:, QR:]
                    return total + jnp.sum(e.reshape(KR // 8, 8, QR), axis=0)

                total = lax.fori_loop(0, count, score, jnp.zeros((8, QR), jnp.float32))
                inverse = 1.0 / jnp.sum(total, axis=0, keepdims=True)

                def weigh(k, out):
                    w = (scores[k] * inverse).astype(jnp.bfloat16)
                    low[k] = w
                    return out + jnp.dot(
                        kvt[near_slot[k], HD:, :], w, preferred_element_type=jnp.float32
                    )

                att = lax.fori_loop(0, count, weigh, jnp.zeros((HD, QR), jnp.float32))
                att = att.astype(jnp.bfloat16).astype(jnp.float32)
                delta = jnp.sum(cols[HD:].astype(jnp.float32) * att, axis=0, keepdims=True)

                def spread_grad(k, out):
                    ds = (scores[k] * inverse * (dots[k] - delta)).astype(jnp.bfloat16)
                    lhs = jnp.concatenate([ds, low[k]], axis=1)
                    acc[near_slot[k]] += jnp.dot(lhs, rhs_d, preferred_element_type=jnp.float32)
                    return out + jnp.dot(
                        kvt[near_slot[k], :HD, :], ds, preferred_element_type=jnp.float32
                    )

                dq = lax.fori_loop(0, count, spread_grad, jnp.zeros((HD, QR), jnp.float32))
                both = jnp.concatenate([dq * scaling, att], axis=0).T
                res_q[slot] = both.astype(jnp.bfloat16).reshape(2, BP, 128)

            return carry

        lax.fori_loop(0, slots, one_block, 0)

        def finish(s, carry):
            total = acc[s]
            res_kv[s] = where_lane(total * scaling, total).astype(jnp.bfloat16).reshape(KF, BP, 128)
            return carry

        lax.fori_loop(0, slots, finish, 0)
        stores = [
            pltpu.make_async_copy(
                res_kv.at[:, pl.ds(2 - 2 * half, 4)], out_main.at[:, pl.ds(2 - 2 * half, 4)], sem.at[0]
            ),
            pltpu.make_async_copy(res_kv.at[:, pl.ds(4 * half, 2)], out_halo, sem.at[1]),
            pltpu.make_async_copy(res_q, out_main.at[:, pl.ds(4 * half, 2)], sem.at[2]),
        ]
        for store in stores:
            store.start()
        for store in stores:
            store.wait()


def attend(block_table, brain_mask, main, halo, tm_size):
    slots = main.shape[0]
    any_spec = pl.BlockSpec(memory_space=ANY)
    smem = pl.BlockSpec(memory_space=pltpu.SMEM)
    return pl.pallas_call(
        functools.partial(attend_kernel, tm_size),
        out_shape=(
            jax.ShapeDtypeStruct((slots, 6, BP, 128), jnp.bfloat16),
            jax.ShapeDtypeStruct((slots, 2, BP, 128), jnp.bfloat16),
        ),
        in_specs=[smem, smem, any_spec, any_spec, any_spec],
        out_specs=(any_spec, any_spec),
        scratch_shapes=[
            pltpu.VMEM((slots, KF, BP, 128), jnp.bfloat16),
            pltpu.VMEM((slots, 128, KR), jnp.bfloat16),
            pltpu.VMEM((slots, 2, BP, 128), jnp.bfloat16),
            pltpu.VMEM((9, KR, QR), jnp.float32),
            pltpu.VMEM((slots, KR, 128), jnp.float32),
            pltpu.VMEM((9, KR, QR), jnp.float32),
            pltpu.VMEM((9, KR, QR), jnp.float32),
            pltpu.VMEM((9, KR, QR), jnp.bfloat16),
            pltpu.VMEM((slots, 2, BP, 128), jnp.bfloat16),
            pltpu.VMEM((slots, KF, BP, 128), jnp.bfloat16),
            pltpu.SMEM((16,), jnp.int32),
            pltpu.SMEM((16,), jnp.int32),
            pltpu.SMEM((16,), jnp.int32),
            pltpu.SemaphoreType.DMA((4,)),
        ],
        compiler_params=pltpu.CompilerParams(vmem_limit_bytes=56 << 20),
        name="attend",
    )(block_table, brain_mask, main, halo, jnp.asarray(window_bias()))


def last_kernel(got_ref, halo_ref, tok_ref, gout_ref, wqkv_ref, tg_ref, terms_ref, grads, att):
    def pair(a, b):
        low = where_lane(a, pltpu.roll(b, HD, 1))
        high = where_lane(pltpu.roll(a, HD, 1), b)
        return low.astype(jnp.bfloat16), high.astype(jnp.bfloat16)

    for i in range(HEADS // 2):
        at = 128 * i
        kvs, qas = [], []
        for h in (2 * i, 2 * i + 1):
            first = got_ref[0, h].astype(jnp.float32)
            second = got_ref[1, h].astype(jnp.float32)
            edge = jnp.concatenate([halo_ref[1, h], halo_ref[0, h]], axis=0).astype(jnp.float32)
            kvs.append((first[2:6] + second[0:4] + edge).reshape(LF * BP, 128))
            qas.append(jnp.concatenate([first[0:2], second[4:6]], axis=0).reshape(LF * BP, 128))
        dk, dv = pair(*kvs)
        dq, da = pair(*qas)
        grads[:, at : at + 128] = dq
        grads[:, HW + at : HW + at + 128] = dk
        grads[:, 2 * HW + at : 2 * HW + at + 128] = dv
        att[:, at : at + 128] = da
    tg_ref[...] = lax.dot_general(
        grads[...], wqkv_ref[...], (((1,), (1,)), ((), ())), preferred_element_type=jnp.float32
    ).astype(jnp.bfloat16)
    tok_t = tok_ref[...].T
    att_t = att[...].T
    for i in range(9):
        terms_ref[768 * i : 768 * (i + 1), :] = jnp.dot(
            tok_t, grads[:, 128 * i : 128 * (i + 1)], preferred_element_type=jnp.float32
        ).astype(terms_ref.dtype)
    for i in range(6):
        terms_ref[6912 + 384 * i : 6912 + 384 * (i + 1), :] = jnp.dot(
            att_t, gout_ref[:, 128 * i : 128 * (i + 1)], preferred_element_type=jnp.float32
        ).astype(terms_ref.dtype)


def last(got, got_halo, tokens, grad_out, w_qkv):
    vmem = pl.BlockSpec(memory_space=pltpu.VMEM)
    return pl.pallas_call(
        last_kernel,
        out_shape=(
            jax.ShapeDtypeStruct((LF * BP, D), jnp.bfloat16),
            jax.ShapeDtypeStruct((9216, 128), jnp.bfloat16),
        ),
        in_specs=[vmem] * 5,
        out_specs=(vmem, vmem),
        scratch_shapes=[
            pltpu.VMEM((LF * BP, 3 * HW), jnp.bfloat16),
            pltpu.VMEM((LF * BP, HW), jnp.bfloat16),
        ],
        compiler_params=pltpu.CompilerParams(vmem_limit_bytes=40 << 20),
        name="last",
    )(got, got_halo, tokens, grad_out, w_qkv)


ROWS = 9216
HALF = ROWS // 2
GROUP = 8
CHUNK = HALF // GROUP
PIECE = CHUNK // GROUP


def sum_kernel(src, out, b0, hs, b1, s1, b2, b3, ss0, r0, ss1, r1, ss2, r2, ss3, r3, ss4, r4, ss5, r5):
    s = lax.axis_index("space")
    t = lax.axis_index("tm")
    core = s % 2
    chip = s // 2
    rank1 = (1 - core) * chip + core * t
    rank2 = (1 - core) * t + core * chip
    base = core * HALF
    far = HALF - base
    sibling = {"space": s + 1 - 2 * core, "tm": t}

    def peer1(i):
        return {"space": (1 - core) * (2 * i + core) + core * s, "tm": (1 - core) * t + core * i}

    def peer2(j):
        return {"space": core * (2 * j + core) + (1 - core) * s, "tm": core * t + (1 - core) * j}

    def remote(a, b, send, recv, device):
        return pltpu.make_async_remote_copy(
            src_ref=a, dst_ref=b, send_sem=send, recv_sem=recv,
            device_id=device, device_id_type=pl.DeviceIdType.MESH,
        )

    def rows(start, index):
        return pl.ds(pl.multiple_of(start + index * CHUNK, CHUNK), CHUNK)

    barrier = pltpu.get_barrier_semaphore()
    pl.semaphore_signal(barrier, inc=1, device_id=sibling, device_id_type=pl.DeviceIdType.MESH)

    def greet(n, carry):
        i = (rank1 + n) % GROUP
        j = (rank2 + n) % GROUP
        pl.semaphore_signal(barrier, inc=1, device_id=peer1(i), device_id_type=pl.DeviceIdType.MESH)
        pl.semaphore_signal(barrier, inc=1, device_id=peer2(j), device_id_type=pl.DeviceIdType.MESH)
        return carry

    lax.fori_loop(1, GROUP, greet, 0)
    pl.semaphore_wait(barrier, 2 * GROUP - 1)

    def copy0(k):
        return remote(src.at[rows(far, k)], b0.at[k], ss0.at[k], r0.at[k], sibling)

    def copy1(i, slot):
        return remote(hs.at[i], b1.at[slot], ss1.at[i], r1.at[slot], peer1(i))

    def copy2(j, slot):
        return remote(s1.at[j], b2.at[slot], ss2.at[j], r2.at[slot], peer2(j))

    def copy3(j, slot):
        return remote(b3.at[slot], b3.at[slot], ss3.at[j], r3.at[slot], peer2(j))

    def copy4(i, chunk):
        return remote(
            out.at[rows(base, chunk)], out.at[rows(base, chunk)], ss4.at[i], r4.at[chunk], peer1(i)
        )

    def copy5(chunk, start):
        return remote(
            out.at[rows(start, chunk)], out.at[rows(start, chunk)], ss5.at[chunk], r5.at[chunk], sibling
        )

    def start0(n, carry):
        copy0((rank2 + 1 + n) % GROUP).start()
        return carry

    lax.fori_loop(0, GROUP, start0, 0)

    def stage0(n, carry):
        i = (rank1 + n) % GROUP
        copy0(i).wait_recv()
        hs[i] = (
            src[rows(base, i), :].astype(jnp.float32) + b0[i].astype(jnp.float32)
        ).astype(jnp.bfloat16)
        copy1(i, rank1).start()
        return carry

    lax.fori_loop(1, GROUP, stage0, 0)
    copy0(rank1).wait_recv()
    own = src[rows(base, rank1), :].astype(jnp.float32) + b0[rank1].astype(jnp.float32)
    s1[...] = own.reshape(GROUP, PIECE, 128)

    def stage1(n, carry):
        i = (rank1 + GROUP - n) % GROUP
        copy1(i, i).wait_recv()
        s1[...] += b1[i].astype(jnp.float32).reshape(GROUP, PIECE, 128)
        return carry

    lax.fori_loop(1, GROUP, stage1, 0)

    def start2(n, carry):
        copy2((rank2 + n) % GROUP, rank2).start()
        return carry

    lax.fori_loop(1, GROUP, start2, 0)
    b3[rank2] = s1[rank2]

    def stage2(n, carry):
        j = (rank2 + GROUP - n) % GROUP
        copy2(j, j).wait_recv()
        b3[rank2] += b2[j]
        return carry

    lax.fori_loop(1, GROUP, stage2, 0)

    def start3(n, carry):
        copy3((rank2 + n) % GROUP, rank2).start()
        return carry

    lax.fori_loop(1, GROUP, start3, 0)

    def stage3(n, carry):
        j = (rank2 + GROUP - n) % GROUP
        copy3(j, j).wait_recv()
        return carry

    lax.fori_loop(1, GROUP, stage3, 0)
    out[rows(base, rank1), :] = b3[...].reshape(CHUNK, 128).astype(jnp.bfloat16)

    def start4(n, carry):
        copy4((rank1 + n) % GROUP, rank1).start()
        return carry

    lax.fori_loop(1, GROUP, start4, 0)
    copy5(rank1, base).start()

    def stage4(n, carry):
        i = (rank1 + GROUP - n) % GROUP
        copy4(i, i).wait_recv()
        copy5(i, base).start()
        return carry

    lax.fori_loop(1, GROUP, stage4, 0)

    def stage5(n, carry):
        copy5(n, far).wait_recv()
        copy5(n, base).wait_send()
        copy0(n).wait_send()
        return carry

    lax.fori_loop(0, GROUP, stage5, 0)

    def done(n, carry):
        i = (rank1 + n) % GROUP
        j = (rank2 + n) % GROUP
        copy1(i, rank1).wait_send()
        copy2(j, rank2).wait_send()
        copy3(j, rank2).wait_send()
        copy4(i, rank1).wait_send()
        return carry

    lax.fori_loop(1, GROUP, done, 0)


def sum_all(terms):
    vmem = pl.BlockSpec(memory_space=pltpu.VMEM)
    return pl.pallas_call(
        sum_kernel,
        out_shape=jax.ShapeDtypeStruct((ROWS, 128), jnp.bfloat16),
        in_specs=[vmem],
        out_specs=vmem,
        scratch_shapes=[
            pltpu.VMEM((GROUP, CHUNK, 128), jnp.bfloat16),
            pltpu.VMEM((GROUP, CHUNK, 128), jnp.bfloat16),
            pltpu.VMEM((GROUP, CHUNK, 128), jnp.bfloat16),
            pltpu.VMEM((GROUP, PIECE, 128), jnp.float32),
            pltpu.VMEM((GROUP, PIECE, 128), jnp.float32),
            pltpu.VMEM((GROUP, PIECE, 128), jnp.float32),
        ]
        + [pltpu.SemaphoreType.DMA((GROUP,))] * 12,
        compiler_params=pltpu.CompilerParams(
            has_side_effects=True, collective_id=3, vmem_limit_bytes=32 << 20
        ),
        name="sum_all",
    )(terms)


def widen_kernel(src, qkv, out):
    for i in range(9):
        qkv[:, 128 * i : 128 * (i + 1)] = src[D * i : D * (i + 1), :].astype(jnp.float32)
    for i in range(6):
        start = 9 * D + HW * i
        out[:, 128 * i : 128 * (i + 1)] = src[start : start + HW, :].astype(jnp.float32)


def widen(terms):
    vmem = pl.BlockSpec(memory_space=pltpu.VMEM)
    return pl.pallas_call(
        widen_kernel,
        out_shape=(
            jax.ShapeDtypeStruct((D, 3 * HW), jnp.float32),
            jax.ShapeDtypeStruct((HW, D), jnp.float32),
        ),
        in_specs=[vmem],
        out_specs=(vmem, vmem),
        compiler_params=pltpu.CompilerParams(vmem_limit_bytes=32 << 20),
        name="widen",
    )(terms)


def shards(tokens, grad_out, w_qkv, w_out, brain_mask, block_table):
    slots = lax.axis_size("space")
    tm_size = lax.axis_size("tm")
    flat_tokens = tokens.reshape(-1, D)
    flat_grad = grad_out.reshape(-1, D)
    packed = project(flat_tokens, flat_grad, w_qkv, w_out)
    main, halo = spread(packed, slots, tm_size)
    main, halo = attend(block_table, brain_mask, main, halo, tm_size)
    got, got_halo = collect(main, halo, slots, tm_size)
    token_grads, terms = last(got, got_halo, flat_tokens, flat_grad, w_qkv)
    qkv_grads, out_grads = widen(sum_all(terms))
    return (token_grads.reshape(tokens.shape), qkv_grads, out_grads)


def solution(mesh):
    in_specs = (P("space", "tm", None, None), P("space", "tm", None, None), P(), P(), P(), P())
    out_specs = (P("space", "tm", None, None), P(), P())
    return jax.shard_map(shards, mesh=mesh, in_specs=in_specs, out_specs=out_specs, check_vma=False)
```

```python
import functools

import numpy as np
import jax
import jax.numpy as jnp
from jax import lax
from jax.experimental import pallas as pl
from jax.experimental.pallas import tpu as pltpu
from jax.sharding import PartitionSpec as P

D = 768
HEADS = 6
HD = 64
SIDE = 4
BP = 64
RAD_S = 3
RAD_T = 2
HW = HEADS * HD
LF = 4
KF = 6
KR = KF * BP
QR = 2 * BP
WORKERS = 2 * HEADS
ANY = pl.ANY


def where_lane(low, high):
    lane = lax.broadcasted_iota(jnp.int32, low.shape, low.ndim - 1)
    return jnp.where(lane < HD, low, high)


MESH = pl.DeviceIdType.MESH


def worker_space(w):
    return w + (w // 8) * (w - 8)


def worker_of(space):
    return 1 - (space // 8) * (space % 2), space - (space // 8) * ((space - 8) // 2)


def signal(semaphore, space, tm):
    pl.semaphore_signal(semaphore, inc=1, device_id={"space": space, "tm": tm}, device_id_type=MESH)


def remote(src, dst, send, recv, device):
    return pltpu.make_async_remote_copy(
        src_ref=src, dst_ref=dst, send_sem=send, recv_sem=recv, device_id=device, device_id_type=MESH
    )


def spread_kernel(
    slots, tm_size, tok_hbm, gout_hbm, wqkv_hbm, wout_hbm, main, halo,
    tok, gout, wqkv, wout, packed, lsem, ssem, hsem, rsem, rhsem,
):
    me = lax.axis_index("space")
    t = lax.axis_index("tm")
    after = lax.rem(t + 1, tm_size)
    before = lax.rem(t + tm_size - 1, tm_size)
    is_worker, worker = worker_of(me)
    loads = [
        pltpu.make_async_copy(wqkv_hbm, wqkv, lsem.at[0]),
        pltpu.make_async_copy(tok_hbm, tok, lsem.at[1]),
        pltpu.make_async_copy(wout_hbm, wout, lsem.at[2]),
        pltpu.make_async_copy(gout_hbm, gout, lsem.at[3]),
    ]
    for load in loads:
        load.start()

    barrier = pltpu.get_barrier_semaphore()

    @pl.when(is_worker == 1)
    def _():
        half = worker % 2
        source = lax.rem(t + tm_size - 1 + 2 * half, tm_size)

        def greet(i, carry):
            signal(barrier, lax.rem(me + i, slots), t)
            return carry

        def greet_halo(i, carry):
            signal(barrier, i, source)
            return carry

        lax.fori_loop(1, slots, greet, 0)
        lax.fori_loop(0, slots, greet_halo, 0)

    for load in loads:
        load.wait()
    proj = jnp.dot(tok[...], wqkv[...], preferred_element_type=jnp.float32)
    gatt = lax.dot_general(
        gout[...], wout[...], (((1,), (1,)), ((), ())), preferred_element_type=jnp.float32
    )

    def pair(low, high):
        first = where_lane(low, pltpu.roll(high, HD, 1)).astype(jnp.bfloat16)
        second = where_lane(pltpu.roll(low, HD, 1), high).astype(jnp.bfloat16)
        return first.reshape(LF, BP, 128), second.reshape(LF, BP, 128)

    for i in range(HEADS // 2):
        at = 128 * i
        keys = pair(proj[:, HW + at : HW + at + 128], proj[:, 2 * HW + at : 2 * HW + at + 128])
        queries = pair(proj[:, at : at + 128], gatt[:, at : at + 128])
        for j in range(2):
            packed[2 * i + j, 0:2] = queries[j][0:2]
            packed[2 * i + j, 2:6] = keys[j]
            packed[2 * i + j, 6:8] = queries[j][2:4]

    pl.semaphore_wait(barrier, 2 * WORKERS - is_worker)

    def main_copy(w):
        return remote(
            packed.at[w // 2, pl.ds(2 * (w % 2), 6)], main.at[me], ssem.at[w], rsem,
            {"space": worker_space(w), "tm": t},
        )

    def halo_copy(h, half):
        return remote(
            packed.at[h, pl.ds(4 - 2 * half, 2)], halo.at[me], hsem.at[2 * h + half], rhsem,
            {"space": worker_space(2 * h + half), "tm": before if half else after},
        )

    def send(i, carry):
        w = lax.rem(i + me, WORKERS)

        @pl.when(worker_space(w) != me)
        def _():
            main_copy(w).start()

        @pl.when(worker_space(w) == me)
        def _():
            pltpu.make_async_copy(
                packed.at[w // 2, pl.ds(2 * (w % 2), 6)], main.at[me], rsem
            ).start()

        return carry

    def send_halo(i, carry):
        h = lax.rem(i + me // 2, HEADS)
        halo_copy(h, 0).start()
        halo_copy(h, 1).start()
        return carry

    lax.fori_loop(0, HEADS, send_halo, 0)
    lax.fori_loop(0, WORKERS, send, 0)

    def finish(w, carry):
        @pl.when(worker_space(w) != me)
        def _():
            main_copy(w).wait_send()

        return carry

    def finish_halo(h, carry):
        halo_copy(h, 0).wait_send()
        halo_copy(h, 1).wait_send()
        return carry

    @pl.when(is_worker == 1)
    def _():
        pltpu.make_async_copy(halo, halo, rhsem).wait()
        pltpu.make_async_copy(main, main, rsem).wait()

    lax.fori_loop(0, HEADS, finish_halo, 0)
    lax.fori_loop(0, WORKERS, finish, 0)


def spread(tokens, grad_out, w_qkv, w_out, slots, tm_size):
    any_spec = pl.BlockSpec(memory_space=ANY)
    return pl.pallas_call(
        functools.partial(spread_kernel, slots, tm_size),
        out_shape=(
            jax.ShapeDtypeStruct((slots, 6, BP, 128), jnp.bfloat16),
            jax.ShapeDtypeStruct((slots, 2, BP, 128), jnp.bfloat16),
        ),
        in_specs=[any_spec] * 4,
        out_specs=(any_spec, any_spec),
        scratch_shapes=[
            pltpu.VMEM(tokens.shape, jnp.bfloat16),
            pltpu.VMEM(grad_out.shape, jnp.bfloat16),
            pltpu.VMEM(w_qkv.shape, jnp.bfloat16),
            pltpu.VMEM(w_out.shape, jnp.bfloat16),
            pltpu.VMEM((HEADS, 8, BP, 128), jnp.bfloat16),
            pltpu.SemaphoreType.DMA((4,)),
            pltpu.SemaphoreType.DMA((WORKERS,)),
            pltpu.SemaphoreType.DMA((WORKERS,)),
            pltpu.SemaphoreType.DMA,
            pltpu.SemaphoreType.DMA,
        ],
        compiler_params=pltpu.CompilerParams(
            has_side_effects=True, collective_id=1, vmem_limit_bytes=60 << 20
        ),
        name="spread",
    )(tokens, grad_out, w_qkv, w_out)


def window_bias():
    patch = np.arange(BP)
    px, py = patch // 16, patch // 4 % 4
    out = np.zeros((9, KF, BP, 2, BP), np.float32)
    for n in range(9):
        dr, dc = n // 3 - 1, n % 3 - 1
        near_x = np.abs(px[:, None] + 4 * dr - px[None, :]) <= RAD_S
        near_y = np.abs(py[:, None] + 4 * dc - py[None, :]) <= RAD_S
        for j in range(KF):
            for i in range(2):
                near = near_x & near_y & (abs(j - RAD_T - i) <= RAD_T)
                out[n, j, :, i, :] = np.where(near, 0.0, -np.inf)
    return out.reshape(9, KR, QR)


def attend_kernel(
    tm_size, table, mask, main, halo, bias_hbm, out_main, out_halo,
    kv, kvt, q, bias, acc, scores, dots, low, res_q, res_kv, slot_of, near_slot, near_off, sem,
):
    me = lax.axis_index("space")
    t = lax.axis_index("tm")
    is_worker, worker = worker_of(me)
    half = worker % 2
    slots = kv.shape[0]
    scaling = HD ** (-0.5)

    @pl.when(is_worker == 1)
    def _():
        loads = [
            pltpu.make_async_copy(
                main.at[:, pl.ds(2 - 2 * half, 4)], kv.at[:, pl.ds(2 - 2 * half, 4)], sem.at[0]
            ),
            pltpu.make_async_copy(halo, kv.at[:, pl.ds(4 * half, 2)], sem.at[1]),
            pltpu.make_async_copy(main.at[:, pl.ds(4 * half, 2)], q, sem.at[2]),
            pltpu.make_async_copy(bias_hbm, bias, sem.at[3]),
        ]
        for load in loads:
            load.start()
        acc[...] = jnp.zeros_like(acc)
        res_q[...] = jnp.zeros_like(res_q)

        def place(s, carry):
            slot_of[table[s]] = s
            return carry

        lax.fori_loop(0, slots, place, 0)
        for load in loads:
            load.wait()

        @pl.when((t == 0) & (half == 0))
        def _():
            bias[:, 0 : 2 * BP, :] = jnp.full((9, 2 * BP, QR), -jnp.inf, jnp.float32)

        @pl.when((t == tm_size - 1) & (half == 1))
        def _():
            bias[:, 4 * BP : 6 * BP, :] = jnp.full((9, 2 * BP, QR), -jnp.inf, jnp.float32)

        def flip(s, carry):
            kvt[s] = kv[s].reshape(KR, 128).T
            return carry

        lax.fori_loop(0, slots, flip, 0)

        def one_block(g, carry):
            @pl.when(mask[g] == 1)
            def _():
                slot = slot_of[g]
                row = g // SIDE
                col = g % SIDE
                count = jnp.int32(0)
                for n in range(9):
                    nr = row + (n // 3 - 1)
                    nc = col + (n % 3 - 1)
                    inside = (nr >= 0) & (nr < SIDE) & (nc >= 0) & (nc < SIDE)
                    nb = jnp.clip(nr, 0, SIDE - 1) * SIDE + jnp.clip(nc, 0, SIDE - 1)
                    valid = inside & (mask[nb] == 1)
                    near_slot[count] = slot_of[nb]
                    near_off[count] = n
                    count = count + valid.astype(jnp.int32)

                rows = q[slot].reshape(QR, 128)
                cols = rows.T
                zero = jnp.zeros_like(cols)
                first = lax.broadcasted_iota(jnp.int32, cols.shape, 0) < HD
                left = lax.broadcasted_iota(jnp.int32, cols.shape, 1) < HD
                rhs_a = jnp.concatenate(
                    [jnp.where(first, cols, zero), jnp.where(first, zero, cols)], axis=1
                )
                rhs_d = jnp.concatenate(
                    [jnp.where(left, rows, zero), jnp.where(left, zero, rows)], axis=0
                )

                def score(k, total):
                    keys = kv[near_slot[k]].reshape(KR, 128)
                    both = jnp.dot(keys, rhs_a, preferred_element_type=jnp.float32)
                    e = jnp.exp(both[:, :QR] * scaling + bias[near_off[k]])
                    scores[k] = e
                    dots[k] = both[:, QR:]
                    return total + jnp.sum(e.reshape(KR // 8, 8, QR), axis=0)

                total = lax.fori_loop(0, count, score, jnp.zeros((8, QR), jnp.float32))
                inverse = 1.0 / jnp.sum(total, axis=0, keepdims=True)

                def weigh(k, out):
                    w = (scores[k] * inverse).astype(jnp.bfloat16)
                    low[k] = w
                    return out + jnp.dot(
                        kvt[near_slot[k], HD:, :], w, preferred_element_type=jnp.float32
                    )

                att = lax.fori_loop(0, count, weigh, jnp.zeros((HD, QR), jnp.float32))
                att = att.astype(jnp.bfloat16).astype(jnp.float32)
                delta = jnp.sum(cols[HD:].astype(jnp.float32) * att, axis=0, keepdims=True)

                def spread_grad(k, out):
                    ds = (scores[k] * inverse * (dots[k] - delta)).astype(jnp.bfloat16)
                    lhs = jnp.concatenate([ds, low[k]], axis=1)
                    acc[near_slot[k]] += jnp.dot(lhs, rhs_d, preferred_element_type=jnp.float32)
                    return out + jnp.dot(
                        kvt[near_slot[k], :HD, :], ds, preferred_element_type=jnp.float32
                    )

                dq = lax.fori_loop(0, count, spread_grad, jnp.zeros((HD, QR), jnp.float32))
                both = jnp.concatenate([dq * scaling, att], axis=0).T
                res_q[slot] = both.astype(jnp.bfloat16).reshape(2, BP, 128)

            return carry

        lax.fori_loop(0, slots, one_block, 0)

        def finish(s, carry):
            total = acc[s]
            res_kv[s] = where_lane(total * scaling, total).astype(jnp.bfloat16).reshape(KF, BP, 128)
            return carry

        lax.fori_loop(0, slots, finish, 0)
        stores = [
            pltpu.make_async_copy(
                res_kv.at[:, pl.ds(2 - 2 * half, 4)], out_main.at[:, pl.ds(2 - 2 * half, 4)], sem.at[0]
            ),
            pltpu.make_async_copy(res_kv.at[:, pl.ds(4 * half, 2)], out_halo, sem.at[1]),
            pltpu.make_async_copy(res_q, out_main.at[:, pl.ds(4 * half, 2)], sem.at[2]),
        ]
        for store in stores:
            store.start()
        for store in stores:
            store.wait()


def attend(block_table, brain_mask, main, halo, tm_size):
    slots = main.shape[0]
    any_spec = pl.BlockSpec(memory_space=ANY)
    smem = pl.BlockSpec(memory_space=pltpu.SMEM)
    return pl.pallas_call(
        functools.partial(attend_kernel, tm_size),
        out_shape=(
            jax.ShapeDtypeStruct((slots, 6, BP, 128), jnp.bfloat16),
            jax.ShapeDtypeStruct((slots, 2, BP, 128), jnp.bfloat16),
        ),
        in_specs=[smem, smem, any_spec, any_spec, any_spec],
        out_specs=(any_spec, any_spec),
        scratch_shapes=[
            pltpu.VMEM((slots, KF, BP, 128), jnp.bfloat16),
            pltpu.VMEM((slots, 128, KR), jnp.bfloat16),
            pltpu.VMEM((slots, 2, BP, 128), jnp.bfloat16),
            pltpu.VMEM((9, KR, QR), jnp.float32),
            pltpu.VMEM((slots, KR, 128), jnp.float32),
            pltpu.VMEM((9, KR, QR), jnp.float32),
            pltpu.VMEM((9, KR, QR), jnp.float32),
            pltpu.VMEM((9, KR, QR), jnp.bfloat16),
            pltpu.VMEM((slots, 2, BP, 128), jnp.bfloat16),
            pltpu.VMEM((slots, KF, BP, 128), jnp.bfloat16),
            pltpu.SMEM((16,), jnp.int32),
            pltpu.SMEM((16,), jnp.int32),
            pltpu.SMEM((16,), jnp.int32),
            pltpu.SemaphoreType.DMA((4,)),
        ],
        compiler_params=pltpu.CompilerParams(vmem_limit_bytes=56 << 20),
        name="attend",
    )(block_table, brain_mask, main, halo, jnp.asarray(window_bias()))


ROWS = 9216
HALF = ROWS // 2
PART = 576
PARTS = HALF // PART
PIECE = 72
FIRST = (8, 4)
SECOND = (8, 16)


def finish_kernel(
    slots, tm_size, main, halo, tok_hbm, gout_hbm, wqkv_hbm, tg_ref, out,
    got, got_halo, tok, gout, wqkv, grads, att, src, b0, hs, b1, s1, b2, b3,
    lsem, cs, ch, cr, crh, ss0, r0, ss1, r1, ss2, r2, ss3, r3, ss4, r4, ss5, r5,
):
    s = lax.axis_index("space")
    t = lax.axis_index("tm")
    core = s % 2
    chip = s // 2
    is_worker, worker = worker_of(s)
    head = worker // 2
    half = worker % 2
    other = lax.rem(t + tm_size + 2 * half - 1, tm_size)
    after = lax.rem(t + 1, tm_size)
    before = lax.rem(t + tm_size - 1, tm_size)
    sibling = {"space": s + 1 - 2 * core, "tm": t}

    def rank1(c):
        return t // 2 if c else chip

    def rank2(c):
        return 2 * chip + t % 2 if c else t

    def peer1(c, i):
        return {"space": s, "tm": 2 * i + t % 2} if c else {"space": 2 * i, "tm": t}

    def peer2(c, j):
        return {"space": 2 * (j // 2) + 1, "tm": 2 * (t // 2) + j % 2} if c else {"space": s, "tm": j}

    loads = [
        pltpu.make_async_copy(tok_hbm, tok, lsem.at[0]),
        pltpu.make_async_copy(gout_hbm, gout, lsem.at[1]),
        pltpu.make_async_copy(wqkv_hbm, wqkv, lsem.at[2]),
    ]
    for load in loads:
        load.start()

    barrier = pltpu.get_barrier_semaphore()

    def greet(i, carry):
        w = lax.rem(i + s, WORKERS)

        @pl.when(worker_space(w) != s)
        def _():
            signal(barrier, worker_space(w), t)

        signal(barrier, worker_space(w), (1 - w % 2) * after + (w % 2) * before)
        return carry

    lax.fori_loop(0, WORKERS, greet, 0)
    signal(barrier, sibling["space"], t)
    for c in range(2):

        @pl.when(core == c)
        def _(c=c):
            def greet1(n, carry):
                peer = peer1(c, (rank1(c) + n) % FIRST[c])
                signal(barrier, peer["space"], peer["tm"])
                return carry

            def greet2(n, carry):
                peer = peer2(c, (rank2(c) + n) % SECOND[c])
                signal(barrier, peer["space"], peer["tm"])
                return carry

            lax.fori_loop(1, FIRST[c], greet1, 0)
            lax.fori_loop(1, SECOND[c], greet2, 0)

    pl.semaphore_wait(barrier, is_worker * (2 * slots - 1) + 15 + 4 * core)

    def main_copy(i):
        return remote(
            main.at[i], got.at[half, head], cs.at[i], cr, {"space": i, "tm": t}
        )

    def halo_copy(i):
        return remote(
            halo.at[i], got_halo.at[half, head], ch.at[i], crh, {"space": i, "tm": other}
        )

    @pl.when(is_worker == 1)
    def _():
        def send_halo(i, carry):
            halo_copy(lax.rem(i + s, slots)).start()
            return carry

        def send(i, carry):
            to = lax.rem(i + s, slots)

            @pl.when(to != s)
            def _():
                main_copy(to).start()

            @pl.when(to == s)
            def _():
                pltpu.make_async_copy(main.at[to], got.at[half, head], cr).start()

            return carry

        lax.fori_loop(0, slots, send_halo, 0)
        lax.fori_loop(0, slots, send, 0)

    for load in loads:
        load.wait()
    tok_t = tok[...].T
    pltpu.make_async_copy(got_halo, got_halo, crh).wait()
    pltpu.make_async_copy(got, got, cr).wait()

    def pair(a, b):
        low = where_lane(a, pltpu.roll(b, HD, 1))
        high = where_lane(pltpu.roll(a, HD, 1), b)
        return low.astype(jnp.bfloat16), high.astype(jnp.bfloat16)

    for i in range(HEADS // 2):
        at = 128 * i
        kvs, qas = [], []
        for h in (2 * i, 2 * i + 1):
            low = got[0, h].astype(jnp.float32)
            high = got[1, h].astype(jnp.float32)
            edge = jnp.concatenate([got_halo[1, h], got_halo[0, h]], axis=0).astype(jnp.float32)
            kvs.append((low[2:6] + high[0:4] + edge).reshape(LF * BP, 128))
            qas.append(jnp.concatenate([low[0:2], high[4:6]], axis=0).reshape(LF * BP, 128))
        dk, dv = pair(*kvs)
        dq, da = pair(*qas)
        grads[:, at : at + 128] = dq
        grads[:, HW + at : HW + at + 128] = dk
        grads[:, 2 * HW + at : 2 * HW + at + 128] = dv
        att[:, at : at + 128] = da
    for i in range(9):
        src[D * i : D * (i + 1), :] = jnp.dot(
            tok_t, grads[:, 128 * i : 128 * (i + 1)], preferred_element_type=jnp.float32
        ).astype(jnp.bfloat16)
    att_t = att[...].T
    for i in range(6):
        start = 9 * D + HW * i
        src[start : start + HW, :] = jnp.dot(
            att_t, gout[:, 128 * i : 128 * (i + 1)], preferred_element_type=jnp.float32
        ).astype(jnp.bfloat16)

    def token_grads():
        tg_ref[...] = lax.dot_general(
            grads[...], wqkv[...], (((1,), (1,)), ((), ())), preferred_element_type=jnp.float32
        ).astype(jnp.bfloat16)

    def sum_all(c):
        first, second = FIRST[c], SECOND[c]
        length = HALF // first
        parts = PARTS // first
        base = c * HALF
        far = HALF - base
        here1, here2 = rank1(c), rank2(c)

        def part(k):
            return pl.ds(pl.multiple_of(k * PART, PART), PART)

        def rows(start, index, size):
            return pl.ds(pl.multiple_of(start + index * size, PART), size)

        def copy0(k):
            return remote(src.at[rows(far, k, PART)], b0.at[part(k)], ss0.at[k], r0.at[k], sibling)

        def copy1(i, slot):
            return remote(
                hs.at[rows(0, i, length)], b1.at[rows(0, slot, length)], ss1.at[i], r1.at[slot],
                peer1(c, i),
            )

        def copy2(j, slot):
            return remote(s1.at[j], b2.at[slot], ss2.at[j], r2.at[slot], peer2(c, j))

        def copy3(j, slot):
            return remote(b3.at[slot], b3.at[slot], ss3.at[j], r3.at[slot], peer2(c, j))

        def copy4(i, chunk):
            where = rows(base, chunk, length)
            return remote(out.at[where], out.at[where], ss4.at[i], r4.at[chunk], peer1(c, i))

        def copy5(chunk):
            where = rows(base, chunk, length)
            return remote(out.at[where], out.at[where], ss5.at[chunk], r5.at[chunk], sibling)

        def from_sibling(chunk):
            where = rows(far, chunk, HALF // FIRST[1 - c])
            return remote(out.at[where], out.at[where], ss5.at[chunk], r5.at[chunk], sibling)

        begin = ((rank1(1 - c) + 1) % FIRST[1 - c]) * (PARTS // FIRST[1 - c])

        def start0(n, carry):
            copy0((begin + n) % PARTS).start()
            return carry

        lax.fori_loop(0, PARTS, start0, 0)
        token_grads()

        def both(k):
            copy0(k).wait_recv()
            return src[rows(base, k, PART), :].astype(jnp.float32) + b0[part(k), :].astype(jnp.float32)

        def stage0(n, carry):
            i = (here1 + n) % first
            for p in range(parts):
                hs[part(i * parts + p), :] = both(i * parts + p).astype(jnp.bfloat16)
            copy1(i, here1).start()
            return carry

        lax.fori_loop(1, first, stage0, 0)
        pieces = PART // PIECE
        for p in range(parts):
            s1[p * pieces : (p + 1) * pieces] = both(here1 * parts + p).reshape(pieces, PIECE, 128)

        def stage1(n, carry):
            i = (here1 + first - n) % first
            copy1(i, i).wait_recv()
            s1[0:second] += b1[rows(0, i, length), :].astype(jnp.float32).reshape(second, PIECE, 128)
            return carry

        lax.fori_loop(1, first, stage1, 0)

        def start2(n, carry):
            copy2((here2 + n) % second, here2).start()
            return carry

        lax.fori_loop(1, second, start2, 0)
        b3[here2] = s1[here2]

        def stage2(n, carry):
            j = (here2 + second - n) % second
            copy2(j, j).wait_recv()
            b3[here2] += b2[j]
            return carry

        lax.fori_loop(1, second, stage2, 0)

        def start3(n, carry):
            copy3((here2 + n) % second, here2).start()
            return carry

        lax.fori_loop(1, second, start3, 0)

        def stage3(n, carry):
            j = (here2 + second - n) % second
            copy3(j, j).wait_recv()
            return carry

        lax.fori_loop(1, second, stage3, 0)
        out[rows(base, here1, length), :] = b3[0:second].reshape(length, 128).astype(jnp.bfloat16)

        def start4(n, carry):
            copy4((here1 + n) % first, here1).start()
            return carry

        lax.fori_loop(1, first, start4, 0)
        copy5(here1).start()

        def stage4(n, carry):
            i = (here1 + first - n) % first
            copy4(i, i).wait_recv()
            copy5(i).start()
            return carry

        lax.fori_loop(1, first, stage4, 0)

        def stage5(n, carry):
            from_sibling(n).wait_recv()
            return carry

        lax.fori_loop(0, FIRST[1 - c], stage5, 0)

        def sent0(n, carry):
            copy0(n).wait_send()
            return carry

        lax.fori_loop(0, PARTS, sent0, 0)

        def sent1(n, carry):
            i = (here1 + n) % first
            copy1(i, here1).wait_send()
            copy4(i, here1).wait_send()
            copy5(i).wait_send()
            return carry

        lax.fori_loop(1, first, sent1, 0)
        copy5(here1).wait_send()

        def sent2(n, carry):
            j = (here2 + n) % second
            copy2(j, here2).wait_send()
            copy3(j, here2).wait_send()
            return carry

        lax.fori_loop(1, second, sent2, 0)

    for c in range(2):
        pl.when(core == c)(functools.partial(sum_all, c))

    @pl.when(is_worker == 1)
    def _():
        def finish(i, carry):
            halo_copy(i).wait_send()

            @pl.when(i != s)
            def _():
                main_copy(i).wait_send()

            return carry

        lax.fori_loop(0, slots, finish, 0)


def finish(main, halo, tokens, grad_out, w_qkv, slots, tm_size):
    any_spec = pl.BlockSpec(memory_space=ANY)
    vmem = pl.BlockSpec(memory_space=pltpu.VMEM)
    dma = pltpu.SemaphoreType.DMA
    return pl.pallas_call(
        functools.partial(finish_kernel, slots, tm_size),
        out_shape=(
            jax.ShapeDtypeStruct((LF * BP, D), jnp.bfloat16),
            jax.ShapeDtypeStruct((ROWS, 128), jnp.bfloat16),
        ),
        in_specs=[any_spec] * 5,
        out_specs=(vmem, vmem),
        scratch_shapes=[
            pltpu.VMEM((2, HEADS, 6, BP, 128), jnp.bfloat16),
            pltpu.VMEM((2, HEADS, 2, BP, 128), jnp.bfloat16),
            pltpu.VMEM(tokens.shape, jnp.bfloat16),
            pltpu.VMEM(grad_out.shape, jnp.bfloat16),
            pltpu.VMEM(w_qkv.shape, jnp.bfloat16),
            pltpu.VMEM((LF * BP, 3 * HW), jnp.bfloat16),
            pltpu.VMEM((LF * BP, HW), jnp.bfloat16),
            pltpu.VMEM((ROWS, 128), jnp.bfloat16),
            pltpu.VMEM((HALF, 128), jnp.bfloat16),
            pltpu.VMEM((HALF, 128), jnp.bfloat16),
            pltpu.VMEM((HALF, 128), jnp.bfloat16),
            pltpu.VMEM((16, PIECE, 128), jnp.float32),
            pltpu.VMEM((16, PIECE, 128), jnp.float32),
            pltpu.VMEM((16, PIECE, 128), jnp.float32),
            dma((3,)), dma((slots,)), dma((slots,)), dma, dma,
            dma((8,)), dma((8,)), dma((8,)), dma((8,)), dma((16,)), dma((16,)),
            dma((16,)), dma((16,)), dma((8,)), dma((8,)), dma((8,)), dma((8,)),
        ],
        compiler_params=pltpu.CompilerParams(
            has_side_effects=True, collective_id=2, vmem_limit_bytes=60 << 20
        ),
        name="finish",
    )(main, halo, tokens, grad_out, w_qkv)


def widen_kernel(src, qkv, out):
    for i in range(9):
        qkv[:, 128 * i : 128 * (i + 1)] = src[D * i : D * (i + 1), :].astype(jnp.float32)
    for i in range(6):
        start = 9 * D + HW * i
        out[:, 128 * i : 128 * (i + 1)] = src[start : start + HW, :].astype(jnp.float32)


def widen(terms):
    vmem = pl.BlockSpec(memory_space=pltpu.VMEM)
    return pl.pallas_call(
        widen_kernel,
        out_shape=(
            jax.ShapeDtypeStruct((D, 3 * HW), jnp.float32),
            jax.ShapeDtypeStruct((HW, D), jnp.float32),
        ),
        in_specs=[vmem],
        out_specs=(vmem, vmem),
        compiler_params=pltpu.CompilerParams(vmem_limit_bytes=32 << 20),
        name="widen",
    )(terms)


def shards(tokens, grad_out, w_qkv, w_out, brain_mask, block_table):
    slots = lax.axis_size("space")
    tm_size = lax.axis_size("tm")
    flat_tokens = tokens.reshape(-1, D)
    flat_grad = grad_out.reshape(-1, D)
    main, halo = spread(flat_tokens, flat_grad, w_qkv, w_out, slots, tm_size)
    main, halo = attend(block_table, brain_mask, main, halo, tm_size)
    token_grads, terms = finish(main, halo, flat_tokens, flat_grad, w_qkv, slots, tm_size)
    qkv_grads, out_grads = widen(terms)
    return (token_grads.reshape(tokens.shape), qkv_grads, out_grads)


def solution(mesh):
    in_specs = (P("space", "tm", None, None), P("space", "tm", None, None), P(), P(), P(), P())
    out_specs = (P("space", "tm", None, None), P(), P())
    return jax.shard_map(shards, mesh=mesh, in_specs=in_specs, out_specs=out_specs, check_vma=False)
```

```python
import functools

import numpy as np
import jax
import jax.numpy as jnp
from jax import lax
from jax.experimental import pallas as pl
from jax.experimental.pallas import tpu as pltpu
from jax.sharding import PartitionSpec as P

D = 768
HEADS = 6
HD = 64
SIDE = 4
BP = 64
RAD_S = 3
RAD_T = 2
HW = HEADS * HD
LF = 4
KF = 6
KR = KF * BP
QR = 2 * BP
WORKERS = 2 * HEADS
ANY = pl.ANY


def where_lane(low, high):
    lane = lax.broadcasted_iota(jnp.int32, low.shape, low.ndim - 1)
    return jnp.where(lane < HD, low, high)


MESH = pl.DeviceIdType.MESH


def worker_space(w):
    return w + (w // 8) * (w - 8)


def worker_of(space):
    return 1 - (space // 8) * (space % 2), space - (space // 8) * ((space - 8) // 2)


def signal(semaphore, space, tm):
    pl.semaphore_signal(semaphore, inc=1, device_id={"space": space, "tm": tm}, device_id_type=MESH)


def remote(src, dst, send, recv, device):
    return pltpu.make_async_remote_copy(
        src_ref=src, dst_ref=dst, send_sem=send, recv_sem=recv, device_id=device, device_id_type=MESH
    )


def spread_kernel(
    slots, tm_size, tok_hbm, gout_hbm, wqkv_hbm, wout_hbm, q, kv,
    tok, gout, wqkv, wout, qpack, kpack, lsem, qsem, ssem, hsem, rqsem, rsem,
):
    me = lax.axis_index("space")
    t = lax.axis_index("tm")
    after = lax.rem(t + 1, tm_size)
    before = lax.rem(t + tm_size - 1, tm_size)
    is_worker, worker = worker_of(me)
    loads = [
        pltpu.make_async_copy(wqkv_hbm, wqkv, lsem.at[0]),
        pltpu.make_async_copy(tok_hbm, tok, lsem.at[1]),
        pltpu.make_async_copy(wout_hbm, wout, lsem.at[2]),
        pltpu.make_async_copy(gout_hbm, gout, lsem.at[3]),
    ]
    for load in loads:
        load.start()

    barrier = pltpu.get_barrier_semaphore()

    @pl.when(is_worker == 1)
    def _():
        half = worker % 2
        source = lax.rem(t + tm_size - 1 + 2 * half, tm_size)

        def greet(i, carry):
            signal(barrier, lax.rem(me + i, slots), t)
            return carry

        def greet_halo(i, carry):
            signal(barrier, i, source)
            return carry

        lax.fori_loop(1, slots, greet, 0)
        lax.fori_loop(0, slots, greet_halo, 0)

    for load in loads:
        load.wait()
    proj = jnp.dot(tok[...], wqkv[...], preferred_element_type=jnp.float32)
    gatt = lax.dot_general(
        gout[...], wout[...], (((1,), (1,)), ((), ())), preferred_element_type=jnp.float32
    )

    def pair(low, high):
        first = where_lane(low, pltpu.roll(high, HD, 1)).astype(jnp.bfloat16)
        second = where_lane(pltpu.roll(low, HD, 1), high).astype(jnp.bfloat16)
        return first.reshape(LF, BP, 128), second.reshape(LF, BP, 128)

    for i in range(HEADS // 2):
        at = 128 * i
        keys = pair(proj[:, HW + at : HW + at + 128], proj[:, 2 * HW + at : 2 * HW + at + 128])
        queries = pair(proj[:, at : at + 128], gatt[:, at : at + 128])
        for j in range(2):
            qpack[2 * i + j] = queries[j]
            kpack[2 * i + j] = keys[j]

    pl.semaphore_wait(barrier, 2 * WORKERS - is_worker)

    def query_refs(w):
        return qpack.at[w // 2, pl.ds(2 * (w % 2), 2)], q.at[me]

    def key_refs(w):
        return kpack.at[w // 2], kv.at[me, pl.ds(2 - 2 * (w % 2), 4)]

    def query_copy(w):
        src, dst = query_refs(w)
        return remote(src, dst, qsem.at[w], rqsem, {"space": worker_space(w), "tm": t})

    def key_copy(w):
        src, dst = key_refs(w)
        return remote(src, dst, ssem.at[w], rsem, {"space": worker_space(w), "tm": t})

    def halo_copy(h, half):
        return remote(
            kpack.at[h, pl.ds(2 - 2 * half, 2)], kv.at[me, pl.ds(4 * half, 2)],
            hsem.at[2 * h + half], rsem,
            {"space": worker_space(2 * h + half), "tm": before if half else after},
        )

    def send(i, carry):
        w = lax.rem(i + me, WORKERS)

        @pl.when(worker_space(w) != me)
        def _():
            key_copy(w).start()
            query_copy(w).start()

        @pl.when(worker_space(w) == me)
        def _():
            src, dst = key_refs(w)
            pltpu.make_async_copy(src, dst, rsem).start()
            src, dst = query_refs(w)
            pltpu.make_async_copy(src, dst, rqsem).start()

        return carry

    def send_halo(i, carry):
        h = lax.rem(i + me // 2, HEADS)
        halo_copy(h, 0).start()
        halo_copy(h, 1).start()
        return carry

    lax.fori_loop(0, HEADS, send_halo, 0)
    lax.fori_loop(0, WORKERS, send, 0)

    def finish(w, carry):
        @pl.when(worker_space(w) != me)
        def _():
            key_copy(w).wait_send()
            query_copy(w).wait_send()

        return carry

    def finish_halo(h, carry):
        halo_copy(h, 0).wait_send()
        halo_copy(h, 1).wait_send()
        return carry

    @pl.when(is_worker == 1)
    def _():
        pltpu.make_async_copy(kv, kv, rsem).wait()
        pltpu.make_async_copy(q, q, rqsem).wait()

    lax.fori_loop(0, HEADS, finish_halo, 0)
    lax.fori_loop(0, WORKERS, finish, 0)


def spread(tokens, grad_out, w_qkv, w_out, slots, tm_size):
    any_spec = pl.BlockSpec(memory_space=ANY)
    vmem = pl.BlockSpec(memory_space=pltpu.VMEM)
    return pl.pallas_call(
        functools.partial(spread_kernel, slots, tm_size),
        out_shape=(
            jax.ShapeDtypeStruct((slots, 2, BP, 128), jnp.bfloat16),
            jax.ShapeDtypeStruct((slots, KF, BP, 128), jnp.bfloat16),
        ),
        in_specs=[any_spec] * 4,
        out_specs=(vmem, vmem),
        scratch_shapes=[
            pltpu.VMEM(tokens.shape, jnp.bfloat16),
            pltpu.VMEM(grad_out.shape, jnp.bfloat16),
            pltpu.VMEM(w_qkv.shape, jnp.bfloat16),
            pltpu.VMEM(w_out.shape, jnp.bfloat16),
            pltpu.VMEM((HEADS, LF, BP, 128), jnp.bfloat16),
            pltpu.VMEM((HEADS, LF, BP, 128), jnp.bfloat16),
            pltpu.SemaphoreType.DMA((4,)),
            pltpu.SemaphoreType.DMA((WORKERS,)),
            pltpu.SemaphoreType.DMA((WORKERS,)),
            pltpu.SemaphoreType.DMA((WORKERS,)),
            pltpu.SemaphoreType.DMA,
            pltpu.SemaphoreType.DMA,
        ],
        compiler_params=pltpu.CompilerParams(
            has_side_effects=True, collective_id=1, vmem_limit_bytes=28 << 20
        ),
        name="spread",
    )(tokens, grad_out, w_qkv, w_out)


UNROLL = 8
MOST = 12
PAIRS = 72


def window_bias():
    patch = np.arange(BP)
    px, py = patch // 16, patch // 4 % 4
    out = np.full((10, KF, BP, 2, BP), -np.inf, np.float32)
    for n in range(9):
        dr, dc = n // 3 - 1, n % 3 - 1
        near_x = np.abs(px[:, None] + 4 * dr - px[None, :]) <= RAD_S
        near_y = np.abs(py[:, None] + 4 * dc - py[None, :]) <= RAD_S
        for j in range(KF):
            for i in range(2):
                near = near_x & near_y & (abs(j - RAD_T - i) <= RAD_T)
                out[n, j, :, i, :] = np.where(near, 0.0, -np.inf)
    return out.reshape(10, KR, QR)


def attend_kernel(
    tm_size, table, mask, q, kv, bias_hbm, res_q, res_kv,
    kvt, bias, acc, scores, dots, low, rhs_a, rhs_d, total, inverse, delta, att, dq,
    slot_of, brain, pair_q, pair_k, pair_off, sem,
):
    me = lax.axis_index("space")
    t = lax.axis_index("tm")
    is_worker, worker = worker_of(me)
    half = worker % 2
    slots = kv.shape[0]
    scaling = HD ** (-0.5)

    @pl.when(is_worker == 1)
    def _():
        load = pltpu.make_async_copy(bias_hbm, bias, sem)
        load.start()

        def place(s, carry):
            slot_of[table[s]] = s
            return carry

        lax.fori_loop(0, slots, place, 0)

        def list_block(g, carry):
            blocks, pairs = carry
            inside_brain = mask[g] == 1
            slot = slot_of[g]
            brain[blocks] = slot
            row = g // SIDE
            col = g % SIDE
            for n in range(9):
                nr = row + (n // 3 - 1)
                nc = col + (n % 3 - 1)
                inside = (nr >= 0) & (nr < SIDE) & (nc >= 0) & (nc < SIDE)
                nb = jnp.clip(nr, 0, SIDE - 1) * SIDE + jnp.clip(nc, 0, SIDE - 1)
                valid = inside_brain & inside & (mask[nb] == 1)
                pair_q[pairs] = slot
                pair_k[pairs] = slot_of[nb]
                pair_off[pairs] = n
                pairs = jnp.minimum(pairs + valid.astype(jnp.int32), PAIRS)
            return (blocks + inside_brain.astype(jnp.int32), pairs)

        blocks, pairs = lax.fori_loop(0, slots, list_block, (jnp.int32(0), jnp.int32(0)))
        for n in range(UNROLL):
            pair_q[pairs + n] = brain[0]
            pair_k[pairs + n] = brain[0]
            pair_off[pairs + n] = 9
        steps = (pairs + (UNROLL - 1)) // UNROLL

        acc[...] = jnp.zeros_like(acc)
        res_q[...] = jnp.zeros_like(res_q)
        total[...] = jnp.zeros_like(total)
        att[...] = jnp.zeros_like(att)
        dq[...] = jnp.zeros_like(dq)

        def prepare(b, carry):
            slot = brain[b]
            kvt[slot] = kv[slot].reshape(KR, 128).T
            rows = q[slot].reshape(QR, 128)
            cols = rows.T
            zero = jnp.zeros_like(cols)
            first = lax.broadcasted_iota(jnp.int32, cols.shape, 0) < HD
            left = lax.broadcasted_iota(jnp.int32, cols.shape, 1) < HD
            rhs_a[slot, :, :QR] = jnp.where(first, cols * scaling, zero)
            rhs_a[slot, :, QR:] = jnp.where(first, zero, cols)
            rhs_d[slot, :QR, :] = jnp.where(left, rows, zero)
            rhs_d[slot, QR:, :] = jnp.where(left, zero, rows)
            return carry

        lax.fori_loop(0, blocks, prepare, 0)
        load.wait()

        @pl.when((t == 0) & (half == 0))
        def _():
            bias[:, 0 : 2 * BP, :] = jnp.full((10, 2 * BP, QR), -jnp.inf, jnp.float32)

        @pl.when((t == tm_size - 1) & (half == 1))
        def _():
            bias[:, 4 * BP : 6 * BP, :] = jnp.full((10, 2 * BP, QR), -jnp.inf, jnp.float32)

        def by_rows(x):
            return x.reshape(KR // 8, 8, QR)

        def score(step, carry):
            for u in range(UNROLL):
                p = step * UNROLL + u
                keys = kv[pair_k[p]].reshape(KR, 128)
                both = jnp.dot(keys, rhs_a[pair_q[p]], preferred_element_type=jnp.float32)
                e = jnp.exp(both[:, :QR] + bias[pair_off[p]])
                scores[p] = e
                dots[p] = both[:, QR:]
                total[pair_q[p]] += jnp.sum(by_rows(e), axis=0)
            return carry

        lax.fori_loop(0, steps, score, 0)

        def invert(b, carry):
            slot = brain[b]
            whole = jnp.sum(total[slot], axis=0, keepdims=True)
            inverse[slot] = jnp.broadcast_to(1.0 / whole, (8, QR))
            return carry

        lax.fori_loop(0, blocks, invert, 0)

        def weigh(step, carry):
            for u in range(UNROLL):
                p = step * UNROLL + u
                w = by_rows(scores[p]) * inverse[pair_q[p]][None]
                w = w.reshape(KR, QR).astype(jnp.bfloat16)
                low[p] = w
                att[pair_q[p]] += jnp.dot(
                    kvt[pair_k[p], HD:, :], w, preferred_element_type=jnp.float32
                )
            return carry

        lax.fori_loop(0, steps, weigh, 0)

        def rest(b, carry):
            slot = brain[b]
            rounded = att[slot].astype(jnp.bfloat16).astype(jnp.float32)
            att[slot] = rounded
            grad = rhs_a[slot, HD:, QR:].astype(jnp.float32)
            one = jnp.sum(grad * rounded, axis=0, keepdims=True)
            delta[slot] = jnp.broadcast_to(one, (8, QR))
            return carry

        lax.fori_loop(0, blocks, rest, 0)

        def spread_grad(step, carry):
            for u in range(UNROLL):
                p = step * UNROLL + u
                qs = pair_q[p]
                ds = by_rows(scores[p]) * inverse[qs][None] * (by_rows(dots[p]) - delta[qs][None])
                ds = ds.reshape(KR, QR).astype(jnp.bfloat16)
                lhs = jnp.concatenate([ds, low[p]], axis=1)
                acc[pair_k[p]] += jnp.dot(lhs, rhs_d[qs], preferred_element_type=jnp.float32)
                dq[qs] += jnp.dot(kvt[pair_k[p], :HD, :], ds, preferred_element_type=jnp.float32)
            return carry

        lax.fori_loop(0, steps, spread_grad, 0)

        def give(b, carry):
            slot = brain[b]
            both = jnp.concatenate([dq[slot] * scaling, att[slot]], axis=0).T
            res_q[slot] = both.astype(jnp.bfloat16).reshape(2, BP, 128)
            return carry

        lax.fori_loop(0, blocks, give, 0)

        def finish_keys(s, carry):
            whole = acc[s]
            res_kv[s] = where_lane(whole * scaling, whole).astype(jnp.bfloat16).reshape(KF, BP, 128)
            return carry

        lax.fori_loop(0, slots, finish_keys, 0)


def attend(block_table, brain_mask, q, kv, tm_size):
    slots = q.shape[0]
    smem = pl.BlockSpec(memory_space=pltpu.SMEM)
    vmem = pl.BlockSpec(memory_space=pltpu.VMEM)
    store = (PAIRS + UNROLL, KR, QR)
    return pl.pallas_call(
        functools.partial(attend_kernel, tm_size),
        out_shape=(
            jax.ShapeDtypeStruct((slots, 2, BP, 128), jnp.bfloat16),
            jax.ShapeDtypeStruct((slots, KF, BP, 128), jnp.bfloat16),
        ),
        in_specs=[smem, smem, vmem, vmem, pl.BlockSpec(memory_space=ANY)],
        out_specs=(vmem, vmem),
        scratch_shapes=[
            pltpu.VMEM((slots, 128, KR), jnp.bfloat16),
            pltpu.VMEM((10, KR, QR), jnp.float32),
            pltpu.VMEM((slots, KR, 128), jnp.float32),
            pltpu.VMEM(store, jnp.float32),
            pltpu.VMEM(store, jnp.float32),
            pltpu.VMEM(store, jnp.bfloat16),
            pltpu.VMEM((slots, 128, 2 * QR), jnp.bfloat16),
            pltpu.VMEM((slots, 2 * QR, 128), jnp.bfloat16),
            pltpu.VMEM((slots, 8, QR), jnp.float32),
            pltpu.VMEM((slots, 8, QR), jnp.float32),
            pltpu.VMEM((slots, 8, QR), jnp.float32),
            pltpu.VMEM((slots, HD, QR), jnp.float32),
            pltpu.VMEM((slots, HD, QR), jnp.float32),
            pltpu.SMEM((16,), jnp.int32),
            pltpu.SMEM((17,), jnp.int32),
            pltpu.SMEM((PAIRS + UNROLL,), jnp.int32),
            pltpu.SMEM((PAIRS + UNROLL,), jnp.int32),
            pltpu.SMEM((PAIRS + UNROLL,), jnp.int32),
            pltpu.SemaphoreType.DMA,
        ],
        compiler_params=pltpu.CompilerParams(vmem_limit_bytes=56 << 20),
        name="attend",
    )(block_table, brain_mask, q, kv, jnp.asarray(window_bias()))


ROWS = 9216
HALF = ROWS // 2
PART = 576
PARTS = HALF // PART
PIECE = 72
FIRST = (8, 4)
SECOND = (8, 16)


def finish_kernel(
    slots, tm_size, res_q, res_kv, tok_hbm, gout_hbm, wqkv_hbm, tg_ref, out,
    got_q, got_kv, got_halo, tok, gout, wqkv, grads, att, src, b0, hs, b1, s1, b2, b3,
    lsem, cq, cs, ch, cqr, cr, crh, ss0, r0, ss1, r1, ss2, r2, ss3, r3, ss4, r4, ss5, r5,
):
    s = lax.axis_index("space")
    t = lax.axis_index("tm")
    core = s % 2
    chip = s // 2
    is_worker, worker = worker_of(s)
    head = worker // 2
    half = worker % 2
    other = lax.rem(t + tm_size + 2 * half - 1, tm_size)
    after = lax.rem(t + 1, tm_size)
    before = lax.rem(t + tm_size - 1, tm_size)
    sibling = {"space": s + 1 - 2 * core, "tm": t}

    def rank1(c):
        return t // 2 if c else chip

    def rank2(c):
        return 2 * chip + t % 2 if c else t

    def peer1(c, i):
        return {"space": s, "tm": 2 * i + t % 2} if c else {"space": 2 * i, "tm": t}

    def peer2(c, j):
        return {"space": 2 * (j // 2) + 1, "tm": 2 * (t // 2) + j % 2} if c else {"space": s, "tm": j}

    loads = [
        pltpu.make_async_copy(tok_hbm, tok, lsem.at[0]),
        pltpu.make_async_copy(gout_hbm, gout, lsem.at[1]),
        pltpu.make_async_copy(wqkv_hbm, wqkv, lsem.at[2]),
    ]
    for load in loads:
        load.start()

    barrier = pltpu.get_barrier_semaphore()

    def greet(i, carry):
        w = lax.rem(i + s, WORKERS)

        @pl.when(worker_space(w) != s)
        def _():
            signal(barrier, worker_space(w), t)

        signal(barrier, worker_space(w), (1 - w % 2) * after + (w % 2) * before)
        return carry

    lax.fori_loop(0, WORKERS, greet, 0)
    signal(barrier, sibling["space"], t)
    for c in range(2):

        @pl.when(core == c)
        def _(c=c):
            def greet1(n, carry):
                peer = peer1(c, (rank1(c) + n) % FIRST[c])
                signal(barrier, peer["space"], peer["tm"])
                return carry

            def greet2(n, carry):
                peer = peer2(c, (rank2(c) + n) % SECOND[c])
                signal(barrier, peer["space"], peer["tm"])
                return carry

            lax.fori_loop(1, FIRST[c], greet1, 0)
            lax.fori_loop(1, SECOND[c], greet2, 0)

    pl.semaphore_wait(barrier, is_worker * (2 * slots - 1) + 15 + 4 * core)

    def query_refs(i):
        return res_q.at[i], got_q.at[half, head]

    def key_refs(i):
        return res_kv.at[i, pl.ds(2 - 2 * half, 4)], got_kv.at[half, head]

    def query_copy(i):
        a, b = query_refs(i)
        return remote(a, b, cq.at[i], cqr, {"space": i, "tm": t})

    def key_copy(i):
        a, b = key_refs(i)
        return remote(a, b, cs.at[i], cr, {"space": i, "tm": t})

    def halo_copy(i):
        return remote(
            res_kv.at[i, pl.ds(4 * half, 2)], got_halo.at[half, head], ch.at[i], crh,
            {"space": i, "tm": other},
        )

    @pl.when(is_worker == 1)
    def _():
        def send_queries(i, carry):
            to = lax.rem(i + s, slots)

            @pl.when(to != s)
            def _():
                query_copy(to).start()

            @pl.when(to == s)
            def _():
                a, b = query_refs(to)
                pltpu.make_async_copy(a, b, cqr).start()

            return carry

        def send_keys(i, carry):
            to = lax.rem(i + s, slots)
            halo_copy(to).start()

            @pl.when(to != s)
            def _():
                key_copy(to).start()

            @pl.when(to == s)
            def _():
                a, b = key_refs(to)
                pltpu.make_async_copy(a, b, cr).start()

            return carry

        lax.fori_loop(0, slots, send_queries, 0)
        lax.fori_loop(0, slots, send_keys, 0)

    for load in loads:
        load.wait()
    tok_t = tok[...].T
    pltpu.make_async_copy(got_q, got_q, cqr).wait()
    pltpu.make_async_copy(got_halo, got_halo, crh).wait()
    pltpu.make_async_copy(got_kv, got_kv, cr).wait()

    def pair(a, b):
        low = where_lane(a, pltpu.roll(b, HD, 1))
        high = where_lane(pltpu.roll(a, HD, 1), b)
        return low.astype(jnp.bfloat16), high.astype(jnp.bfloat16)

    for i in range(HEADS // 2):
        at = 128 * i
        kvs, qas = [], []
        for h in (2 * i, 2 * i + 1):
            low = got_kv[0, h].astype(jnp.float32)
            high = got_kv[1, h].astype(jnp.float32)
            edge = jnp.concatenate([got_halo[1, h], got_halo[0, h]], axis=0).astype(jnp.float32)
            kvs.append((low + high + edge).reshape(LF * BP, 128))
            rows = jnp.concatenate([got_q[0, h], got_q[1, h]], axis=0).astype(jnp.float32)
            qas.append(rows.reshape(LF * BP, 128))
        dk, dv = pair(*kvs)
        dq, da = pair(*qas)
        grads[:, at : at + 128] = dq
        grads[:, HW + at : HW + at + 128] = dk
        grads[:, 2 * HW + at : 2 * HW + at + 128] = dv
        att[:, at : at + 128] = da
    for i in range(9):
        src[D * i : D * (i + 1), :] = jnp.dot(
            tok_t, grads[:, 128 * i : 128 * (i + 1)], preferred_element_type=jnp.float32
        ).astype(jnp.bfloat16)
    att_t = att[...].T
    for i in range(6):
        start = 9 * D + HW * i
        src[start : start + HW, :] = jnp.dot(
            att_t, gout[:, 128 * i : 128 * (i + 1)], preferred_element_type=jnp.float32
        ).astype(jnp.bfloat16)

    def token_grads():
        tg_ref[...] = lax.dot_general(
            grads[...], wqkv[...], (((1,), (1,)), ((), ())), preferred_element_type=jnp.float32
        ).astype(jnp.bfloat16)

    def sum_all(c):
        first, second = FIRST[c], SECOND[c]
        length = HALF // first
        parts = PARTS // first
        base = c * HALF
        far = HALF - base
        here1, here2 = rank1(c), rank2(c)

        def part(k):
            return pl.ds(pl.multiple_of(k * PART, PART), PART)

        def rows(start, index, size):
            return pl.ds(pl.multiple_of(start + index * size, PART), size)

        def copy0(k):
            return remote(src.at[rows(far, k, PART)], b0.at[part(k)], ss0.at[k], r0.at[k], sibling)

        def copy1(i, slot):
            return remote(
                hs.at[rows(0, i, length)], b1.at[rows(0, slot, length)], ss1.at[i], r1.at[slot],
                peer1(c, i),
            )

        def copy2(j, slot):
            return remote(s1.at[j], b2.at[slot], ss2.at[j], r2.at[slot], peer2(c, j))

        def copy3(j, slot):
            return remote(b3.at[slot], b3.at[slot], ss3.at[j], r3.at[slot], peer2(c, j))

        def copy4(i, chunk):
            where = rows(base, chunk, length)
            return remote(out.at[where], out.at[where], ss4.at[i], r4.at[chunk], peer1(c, i))

        def copy5(chunk):
            where = rows(base, chunk, length)
            return remote(out.at[where], out.at[where], ss5.at[chunk], r5.at[chunk], sibling)

        def from_sibling(chunk):
            where = rows(far, chunk, HALF // FIRST[1 - c])
            return remote(out.at[where], out.at[where], ss5.at[chunk], r5.at[chunk], sibling)

        begin = ((rank1(1 - c) + 1) % FIRST[1 - c]) * (PARTS // FIRST[1 - c])

        def start0(n, carry):
            copy0((begin + n) % PARTS).start()
            return carry

        lax.fori_loop(0, PARTS, start0, 0)
        token_grads()

        def both(k):
            copy0(k).wait_recv()
            return src[rows(base, k, PART), :].astype(jnp.float32) + b0[part(k), :].astype(jnp.float32)

        def stage0(n, carry):
            i = (here1 + n) % first
            for p in range(parts):
                hs[part(i * parts + p), :] = both(i * parts + p).astype(jnp.bfloat16)
            copy1(i, here1).start()
            return carry

        lax.fori_loop(1, first, stage0, 0)
        pieces = PART // PIECE
        for p in range(parts):
            s1[p * pieces : (p + 1) * pieces] = both(here1 * parts + p).reshape(pieces, PIECE, 128)

        def stage1(n, carry):
            i = (here1 + first - n) % first
            copy1(i, i).wait_recv()
            s1[0:second] += b1[rows(0, i, length), :].astype(jnp.float32).reshape(second, PIECE, 128)
            return carry

        lax.fori_loop(1, first, stage1, 0)

        def start2(n, carry):
            copy2((here2 + n) % second, here2).start()
            return carry

        lax.fori_loop(1, second, start2, 0)
        b3[here2] = s1[here2]

        def stage2(n, carry):
            j = (here2 + second - n) % second
            copy2(j, j).wait_recv()
            b3[here2] += b2[j]
            return carry

        lax.fori_loop(1, second, stage2, 0)

        def start3(n, carry):
            copy3((here2 + n) % second, here2).start()
            return carry

        lax.fori_loop(1, second, start3, 0)

        def stage3(n, carry):
            j = (here2 + second - n) % second
            copy3(j, j).wait_recv()
            return carry

        lax.fori_loop(1, second, stage3, 0)
        out[rows(base, here1, length), :] = b3[0:second].reshape(length, 128).astype(jnp.bfloat16)

        def start4(n, carry):
            copy4((here1 + n) % first, here1).start()
            return carry

        lax.fori_loop(1, first, start4, 0)
        copy5(here1).start()

        def stage4(n, carry):
            i = (here1 + first - n) % first
            copy4(i, i).wait_recv()
            copy5(i).start()
            return carry

        lax.fori_loop(1, first, stage4, 0)

        def stage5(n, carry):
            from_sibling(n).wait_recv()
            return carry

        lax.fori_loop(0, FIRST[1 - c], stage5, 0)

        def sent0(n, carry):
            copy0(n).wait_send()
            return carry

        lax.fori_loop(0, PARTS, sent0, 0)

        def sent1(n, carry):
            i = (here1 + n) % first
            copy1(i, here1).wait_send()
            copy4(i, here1).wait_send()
            copy5(i).wait_send()
            return carry

        lax.fori_loop(1, first, sent1, 0)
        copy5(here1).wait_send()

        def sent2(n, carry):
            j = (here2 + n) % second
            copy2(j, here2).wait_send()
            copy3(j, here2).wait_send()
            return carry

        lax.fori_loop(1, second, sent2, 0)

    for c in range(2):
        pl.when(core == c)(functools.partial(sum_all, c))

    @pl.when(is_worker == 1)
    def _():
        def finish(i, carry):
            halo_copy(i).wait_send()

            @pl.when(i != s)
            def _():
                query_copy(i).wait_send()
                key_copy(i).wait_send()

            return carry

        lax.fori_loop(0, slots, finish, 0)


def finish(res_q, res_kv, tokens, grad_out, w_qkv, slots, tm_size):
    any_spec = pl.BlockSpec(memory_space=ANY)
    vmem = pl.BlockSpec(memory_space=pltpu.VMEM)
    dma = pltpu.SemaphoreType.DMA
    return pl.pallas_call(
        functools.partial(finish_kernel, slots, tm_size),
        out_shape=(
            jax.ShapeDtypeStruct((LF * BP, D), jnp.bfloat16),
            jax.ShapeDtypeStruct((ROWS, 128), jnp.bfloat16),
        ),
        in_specs=[vmem, vmem] + [any_spec] * 3,
        out_specs=(vmem, vmem),
        scratch_shapes=[
            pltpu.VMEM((2, HEADS, 2, BP, 128), jnp.bfloat16),
            pltpu.VMEM((2, HEADS, LF, BP, 128), jnp.bfloat16),
            pltpu.VMEM((2, HEADS, 2, BP, 128), jnp.bfloat16),
            pltpu.VMEM(tokens.shape, jnp.bfloat16),
            pltpu.VMEM(grad_out.shape, jnp.bfloat16),
            pltpu.VMEM(w_qkv.shape, jnp.bfloat16),
            pltpu.VMEM((LF * BP, 3 * HW), jnp.bfloat16),
            pltpu.VMEM((LF * BP, HW), jnp.bfloat16),
            pltpu.VMEM((ROWS, 128), jnp.bfloat16),
            pltpu.VMEM((HALF, 128), jnp.bfloat16),
            pltpu.VMEM((HALF, 128), jnp.bfloat16),
            pltpu.VMEM((HALF, 128), jnp.bfloat16),
            pltpu.VMEM((16, PIECE, 128), jnp.float32),
            pltpu.VMEM((16, PIECE, 128), jnp.float32),
            pltpu.VMEM((16, PIECE, 128), jnp.float32),
            dma((3,)), dma((slots,)), dma((slots,)), dma((slots,)), dma, dma, dma,
            dma((8,)), dma((8,)), dma((8,)), dma((8,)), dma((16,)), dma((16,)),
            dma((16,)), dma((16,)), dma((8,)), dma((8,)), dma((8,)), dma((8,)),
        ],
        compiler_params=pltpu.CompilerParams(
            has_side_effects=True, collective_id=2, vmem_limit_bytes=32 << 20
        ),
        name="finish",
    )(res_q, res_kv, tokens, grad_out, w_qkv)


def widen_kernel(src, qkv, out):
    for i in range(9):
        qkv[:, 128 * i : 128 * (i + 1)] = src[D * i : D * (i + 1), :].astype(jnp.float32)
    for i in range(6):
        start = 9 * D + HW * i
        out[:, 128 * i : 128 * (i + 1)] = src[start : start + HW, :].astype(jnp.float32)


def widen(terms):
    vmem = pl.BlockSpec(memory_space=pltpu.VMEM)
    return pl.pallas_call(
        widen_kernel,
        out_shape=(
            jax.ShapeDtypeStruct((D, 3 * HW), jnp.float32),
            jax.ShapeDtypeStruct((HW, D), jnp.float32),
        ),
        in_specs=[vmem],
        out_specs=(vmem, vmem),
        compiler_params=pltpu.CompilerParams(vmem_limit_bytes=32 << 20),
        name="widen",
    )(terms)


def shards(tokens, grad_out, w_qkv, w_out, brain_mask, block_table):
    slots = lax.axis_size("space")
    tm_size = lax.axis_size("tm")
    flat_tokens = tokens.reshape(-1, D)
    flat_grad = grad_out.reshape(-1, D)
    q, kv = spread(flat_tokens, flat_grad, w_qkv, w_out, slots, tm_size)
    res_q, res_kv = attend(block_table, brain_mask, q, kv, tm_size)
    token_grads, terms = finish(res_q, res_kv, flat_tokens, flat_grad, w_qkv, slots, tm_size)
    qkv_grads, out_grads = widen(terms)
    return (token_grads.reshape(tokens.shape), qkv_grads, out_grads)


def solution(mesh):
    in_specs = (P("space", "tm", None, None), P("space", "tm", None, None), P(), P(), P(), P())
    out_specs = (P("space", "tm", None, None), P(), P())
    return jax.shard_map(shards, mesh=mesh, in_specs=in_specs, out_specs=out_specs, check_vma=False)
```

```python
import functools

import numpy as np
import jax
import jax.numpy as jnp
from jax import lax
from jax.experimental import pallas as pl
from jax.experimental.pallas import tpu as pltpu
from jax.sharding import PartitionSpec as P

D = 768
HEADS = 6
HD = 64
SIDE = 4
BP = 64
RAD_S = 3
RAD_T = 2
HW = HEADS * HD
LF = 4
KF = 6
KR = KF * BP
QR = 2 * BP
WORKERS = 2 * HEADS


def where_lane(low, high):
    lane = lax.broadcasted_iota(jnp.int32, low.shape, low.ndim - 1)
    return jnp.where(lane < HD, low, high)


MESH = pl.DeviceIdType.MESH


def worker_space(w):
    row = w // 6
    at = w - 6 * row
    return 8 * row + at + (at + 2 * row) // 3


def worker_of(space):
    row = space // 8
    at = space - 8 * row
    return ((at + 1 + 2 * row) % 4 + 3) // 4, 6 * row + at - (at + 2 * row) // 4


def signal(semaphore, space, tm):
    pl.semaphore_signal(semaphore, inc=1, device_id={"space": space, "tm": tm}, device_id_type=MESH)


def remote(src, dst, send, recv, device):
    return pltpu.make_async_remote_copy(
        src_ref=src, dst_ref=dst, send_sem=send, recv_sem=recv, device_id=device, device_id_type=MESH
    )


def spread_kernel(
    slots, tm_size, tok_hbm, gout_hbm, wqkv_hbm, wout_hbm, held,
    tok, gout, wqkv, wout, packed, lsem, ssem, hsem, rsem,
):
    me = lax.axis_index("space")
    t = lax.axis_index("tm")
    after = lax.rem(t + 1, tm_size)
    before = lax.rem(t + tm_size - 1, tm_size)
    is_worker, worker = worker_of(me)
    loads = [
        pltpu.make_async_copy(wqkv_hbm, wqkv, lsem.at[0]),
        pltpu.make_async_copy(tok_hbm, tok, lsem.at[1]),
        pltpu.make_async_copy(wout_hbm, wout, lsem.at[2]),
        pltpu.make_async_copy(gout_hbm, gout, lsem.at[3]),
    ]
    for load in loads:
        load.start()

    barrier = pltpu.get_barrier_semaphore()

    @pl.when(is_worker == 1)
    def _():
        half = worker % 2
        source = lax.rem(t + tm_size - 1 + 2 * half, tm_size)

        def greet(i, carry):
            signal(barrier, lax.rem(me + i, slots), t)
            return carry

        def greet_halo(i, carry):
            signal(barrier, i, source)
            return carry

        lax.fori_loop(1, slots, greet, 0)
        lax.fori_loop(0, slots, greet_halo, 0)

    for load in loads:
        load.wait()
    proj = jnp.dot(tok[...], wqkv[...], preferred_element_type=jnp.float32)
    gatt = lax.dot_general(
        gout[...], wout[...], (((1,), (1,)), ((), ())), preferred_element_type=jnp.float32
    )

    def pair(low, high):
        first = where_lane(low, pltpu.roll(high, HD, 1)).astype(jnp.bfloat16)
        second = where_lane(pltpu.roll(low, HD, 1), high).astype(jnp.bfloat16)
        return first.reshape(LF, BP, 128), second.reshape(LF, BP, 128)

    for i in range(HEADS // 2):
        at = 128 * i
        keys = pair(proj[:, HW + at : HW + at + 128], proj[:, 2 * HW + at : 2 * HW + at + 128])
        queries = pair(proj[:, at : at + 128], gatt[:, at : at + 128])
        for j in range(2):
            packed[2 * i + j, 0:2] = queries[j][2:4]
            packed[2 * i + j, 2:6] = keys[j]
            packed[2 * i + j, 6:8] = queries[j][0:2]

    pl.semaphore_wait(barrier, 2 * WORKERS - is_worker)

    def main_refs(w):
        start = 2 - 2 * (w % 2)
        return packed.at[w // 2, pl.ds(start, 6)], held.at[me, pl.ds(start, 6)]

    def main_copy(w):
        src, dst = main_refs(w)
        return remote(src, dst, ssem.at[w], rsem, {"space": worker_space(w), "tm": t})

    def halo_copy(h, half):
        return remote(
            packed.at[h, pl.ds(4 - 2 * half, 2)], held.at[me, pl.ds(6 * half, 2)],
            hsem.at[2 * h + half], rsem,
            {"space": worker_space(2 * h + half), "tm": before if half else after},
        )

    def send(i, carry):
        w = lax.rem(i + me, WORKERS)

        @pl.when(worker_space(w) != me)
        def _():
            main_copy(w).start()

        @pl.when(worker_space(w) == me)
        def _():
            src, dst = main_refs(w)
            pltpu.make_async_copy(src, dst, rsem).start()

        return carry

    def send_halo(i, carry):
        h = lax.rem(i + me // 2, HEADS)
        halo_copy(h, 0).start()
        halo_copy(h, 1).start()
        return carry

    lax.fori_loop(0, HEADS, send_halo, 0)
    lax.fori_loop(0, WORKERS, send, 0)

    def finish(w, carry):
        @pl.when(worker_space(w) != me)
        def _():
            main_copy(w).wait_send()

        return carry

    def finish_halo(h, carry):
        halo_copy(h, 0).wait_send()
        halo_copy(h, 1).wait_send()
        return carry

    @pl.when(is_worker == 1)
    def _():
        pltpu.make_async_copy(held, held, rsem).wait()

    lax.fori_loop(0, HEADS, finish_halo, 0)
    lax.fori_loop(0, WORKERS, finish, 0)


def spread(tokens, grad_out, w_qkv, w_out, slots, tm_size):
    hbm = pl.BlockSpec(memory_space=pltpu.HBM)
    vmem = pl.BlockSpec(memory_space=pltpu.VMEM)
    return pl.pallas_call(
        functools.partial(spread_kernel, slots, tm_size),
        out_shape=jax.ShapeDtypeStruct((slots, 8, BP, 128), jnp.bfloat16),
        in_specs=[hbm] * 4,
        out_specs=vmem,
        scratch_shapes=[
            pltpu.VMEM(tokens.shape, jnp.bfloat16),
            pltpu.VMEM(grad_out.shape, jnp.bfloat16),
            pltpu.VMEM(w_qkv.shape, jnp.bfloat16),
            pltpu.VMEM(w_out.shape, jnp.bfloat16),
            pltpu.VMEM((HEADS, 8, BP, 128), jnp.bfloat16),
            pltpu.SemaphoreType.DMA((4,)),
            pltpu.SemaphoreType.DMA((WORKERS,)),
            pltpu.SemaphoreType.DMA((WORKERS,)),
            pltpu.SemaphoreType.DMA,
        ],
        compiler_params=pltpu.CompilerParams(
            has_side_effects=True, collective_id=1, vmem_limit_bytes=28 << 20
        ),
        name="spread",
    )(tokens, grad_out, w_qkv, w_out)


UNROLL = 8
MOST = 12
PAIRS = 72


def window_bias():
    patch = np.arange(BP)
    px, py = patch // 16, patch // 4 % 4
    out = np.full((10, KF, BP, 2, BP), -np.inf, np.float32)
    for n in range(9):
        dr, dc = n // 3 - 1, n % 3 - 1
        near_x = np.abs(px[:, None] + 4 * dr - px[None, :]) <= RAD_S
        near_y = np.abs(py[:, None] + 4 * dc - py[None, :]) <= RAD_S
        for j in range(KF):
            for i in range(2):
                near = near_x & near_y & (abs(j - RAD_T - i) <= RAD_T)
                out[n, j, :, i, :] = np.where(near, 0.0, -np.inf)
    return out.reshape(10, KR, QR)


def attend_kernel(
    tm_size, table, mask, held, bias_hbm, res_q, res_kv,
    kvt, bias, acc, scores, dots, rhs_a, rhs_d, total, inverse, delta, att, dq,
    slot_of, brain, pair_q, pair_k, pair_off, sem,
):
    me = lax.axis_index("space")
    t = lax.axis_index("tm")
    is_worker, worker = worker_of(me)
    half = worker % 2
    slots = held.shape[0]
    scaling = HD ** (-0.5)

    def keys_of(slot):
        return held[slot, pl.ds(2 * half, KF)].reshape(KR, 128)

    @pl.when(is_worker == 1)
    def _():
        load = pltpu.make_async_copy(bias_hbm, bias, sem)
        load.start()

        def place(s, carry):
            slot_of[table[s]] = s
            return carry

        lax.fori_loop(0, slots, place, 0)

        def list_block(g, carry):
            blocks, pairs = carry
            inside_brain = mask[g] == 1
            slot = slot_of[g]
            brain[blocks] = slot
            row = g // SIDE
            col = g % SIDE
            for n in range(9):
                nr = row + (n // 3 - 1)
                nc = col + (n % 3 - 1)
                inside = (nr >= 0) & (nr < SIDE) & (nc >= 0) & (nc < SIDE)
                nb = jnp.clip(nr, 0, SIDE - 1) * SIDE + jnp.clip(nc, 0, SIDE - 1)
                valid = inside_brain & inside & (mask[nb] == 1)
                pair_q[pairs] = slot
                pair_k[pairs] = slot_of[nb]
                pair_off[pairs] = n
                pairs = jnp.minimum(pairs + valid.astype(jnp.int32), PAIRS)
            return (blocks + inside_brain.astype(jnp.int32), pairs)

        blocks, pairs = lax.fori_loop(0, slots, list_block, (jnp.int32(0), jnp.int32(0)))
        for n in range(UNROLL):
            pair_q[pairs + n] = brain[0]
            pair_k[pairs + n] = brain[0]
            pair_off[pairs + n] = 9
        steps = (pairs + (UNROLL - 1)) // UNROLL

        acc[...] = jnp.zeros_like(acc)
        res_q[...] = jnp.zeros_like(res_q)
        total[...] = jnp.zeros_like(total)
        att[...] = jnp.zeros_like(att)
        dq[...] = jnp.zeros_like(dq)

        def prepare(b, carry):
            slot = brain[b]
            kvt[slot] = keys_of(slot).T
            rows = held[slot, pl.ds(6 - 6 * half, 2)].reshape(QR, 128)
            cols = rows.T
            zero = jnp.zeros_like(cols)
            first = lax.broadcasted_iota(jnp.int32, cols.shape, 0) < HD
            left = lax.broadcasted_iota(jnp.int32, cols.shape, 1) < HD
            rhs_a[slot, :, :QR] = jnp.where(first, cols * scaling, zero)
            rhs_a[slot, :, QR:] = jnp.where(first, zero, cols)
            rhs_d[slot, :QR, :] = jnp.where(left, rows, zero)
            rhs_d[slot, QR:, :] = jnp.where(left, zero, rows)
            return carry

        lax.fori_loop(0, blocks, prepare, 0)
        load.wait()

        @pl.when((t == 0) & (half == 0))
        def _():
            bias[:, 0 : 2 * BP, :] = jnp.full((10, 2 * BP, QR), -jnp.inf, jnp.float32)

        @pl.when((t == tm_size - 1) & (half == 1))
        def _():
            bias[:, 4 * BP : 6 * BP, :] = jnp.full((10, 2 * BP, QR), -jnp.inf, jnp.float32)

        def by_rows(x):
            return x.reshape(KR // 8, 8, QR)

        def score(step, carry):
            for u in range(UNROLL):
                p = step * UNROLL + u
                keys = keys_of(pair_k[p])
                both = jnp.dot(keys, rhs_a[pair_q[p]], preferred_element_type=jnp.float32)
                e = jnp.exp(both[:, :QR] + bias[pair_off[p]])
                scores[p] = e
                dots[p] = both[:, QR:]
                total[pair_q[p]] += jnp.sum(by_rows(e), axis=0)
            return carry

        lax.fori_loop(0, steps, score, 0)

        def invert(b, carry):
            slot = brain[b]
            whole = jnp.sum(total[slot], axis=0, keepdims=True)
            inverse[slot] = jnp.broadcast_to(1.0 / whole, (8, QR))
            return carry

        lax.fori_loop(0, blocks, invert, 0)

        def weigh(step, carry):
            for u in range(UNROLL):
                p = step * UNROLL + u
                w = by_rows(scores[p]) * inverse[pair_q[p]][None]
                w = w.reshape(KR, QR).astype(jnp.bfloat16)
                att[pair_q[p]] += jnp.dot(
                    kvt[pair_k[p], HD:, :], w, preferred_element_type=jnp.float32
                )
            return carry

        lax.fori_loop(0, steps, weigh, 0)

        def rest(b, carry):
            slot = brain[b]
            rounded = att[slot].astype(jnp.bfloat16).astype(jnp.float32)
            att[slot] = rounded
            grad = rhs_a[slot, HD:, QR:].astype(jnp.float32)
            one = jnp.sum(grad * rounded, axis=0, keepdims=True)
            delta[slot] = jnp.broadcast_to(one, (8, QR))
            return carry

        lax.fori_loop(0, blocks, rest, 0)

        def spread_grad(step, carry):
            for u in range(UNROLL):
                p = step * UNROLL + u
                qs = pair_q[p]
                w = by_rows(scores[p]) * inverse[qs][None]
                ds = w * (by_rows(dots[p]) - delta[qs][None])
                ds = ds.reshape(KR, QR).astype(jnp.bfloat16)
                lhs = jnp.concatenate([ds, w.reshape(KR, QR).astype(jnp.bfloat16)], axis=1)
                acc[pair_k[p]] += jnp.dot(lhs, rhs_d[qs], preferred_element_type=jnp.float32)
                dq[qs] += jnp.dot(kvt[pair_k[p], :HD, :], ds, preferred_element_type=jnp.float32)
            return carry

        lax.fori_loop(0, steps, spread_grad, 0)

        def give(b, carry):
            slot = brain[b]
            both = jnp.concatenate([dq[slot] * scaling, att[slot]], axis=0).T
            res_q[slot] = both.astype(jnp.bfloat16).reshape(2, BP, 128)
            return carry

        lax.fori_loop(0, blocks, give, 0)

        def finish_keys(s, carry):
            whole = acc[s]
            res_kv[s] = where_lane(whole * scaling, whole).astype(jnp.bfloat16).reshape(KF, BP, 128)
            return carry

        lax.fori_loop(0, slots, finish_keys, 0)


def attend(block_table, brain_mask, held, tm_size):
    slots = held.shape[0]
    smem = pl.BlockSpec(memory_space=pltpu.SMEM)
    vmem = pl.BlockSpec(memory_space=pltpu.VMEM)
    store = (PAIRS + UNROLL, KR, QR)
    return pl.pallas_call(
        functools.partial(attend_kernel, tm_size),
        out_shape=(
            jax.ShapeDtypeStruct((slots, 2, BP, 128), jnp.bfloat16),
            jax.ShapeDtypeStruct((slots, KF, BP, 128), jnp.bfloat16),
        ),
        in_specs=[smem, smem, vmem, pl.BlockSpec(memory_space=pltpu.HBM)],
        out_specs=(vmem, vmem),
        scratch_shapes=[
            pltpu.VMEM((slots, 128, KR), jnp.bfloat16),
            pltpu.VMEM((10, KR, QR), jnp.float32),
            pltpu.VMEM((slots, KR, 128), jnp.float32),
            pltpu.VMEM(store, jnp.float32),
            pltpu.VMEM(store, jnp.float32),
            pltpu.VMEM((slots, 128, 2 * QR), jnp.bfloat16),
            pltpu.VMEM((slots, 2 * QR, 128), jnp.bfloat16),
            pltpu.VMEM((slots, 8, QR), jnp.float32),
            pltpu.VMEM((slots, 8, QR), jnp.float32),
            pltpu.VMEM((slots, 8, QR), jnp.float32),
            pltpu.VMEM((slots, HD, QR), jnp.float32),
            pltpu.VMEM((slots, HD, QR), jnp.float32),
            pltpu.SMEM((16,), jnp.int32),
            pltpu.SMEM((17,), jnp.int32),
            pltpu.SMEM((PAIRS + UNROLL,), jnp.int32),
            pltpu.SMEM((PAIRS + UNROLL,), jnp.int32),
            pltpu.SMEM((PAIRS + UNROLL,), jnp.int32),
            pltpu.SemaphoreType.DMA,
        ],
        compiler_params=pltpu.CompilerParams(vmem_limit_bytes=47 << 20),
        name="attend",
    )(block_table, brain_mask, held, jnp.asarray(window_bias()))


ROWS = 9216
KEYS_AT = 6 * D
STARTS = (0, 4096)
HALVES = (2048, 2560)
PIECES = (32, 40)
PARTS = 8
FIRST = (8, 4)
SECOND = (8, 16)


def finish_kernel(
    slots, tm_size, res_q, res_kv, tok_hbm, gout_hbm, wqkv_hbm, tg_ref, out,
    got_q, got_kv, got_halo, tok, gout, wqkv, grads, att, src, early, late,
    lsem, cq, cs, ch, cqr, cr, crh, ss0, r0, ss1, r1, ss2, r2, ss3, r3, ss4, r4, ss5, r5,
):
    s = lax.axis_index("space")
    t = lax.axis_index("tm")
    core = s % 2
    chip = s // 2
    is_worker, worker = worker_of(s)
    head = worker // 2
    half = worker % 2
    other = lax.rem(t + tm_size + 2 * half - 1, tm_size)
    after = lax.rem(t + 1, tm_size)
    before = lax.rem(t + tm_size - 1, tm_size)
    sibling = {"space": s + 1 - 2 * core, "tm": t}

    def rank1(c):
        return t // 2 if c else chip

    def rank2(c):
        return 2 * chip + t % 2 if c else t

    def peer1(c, i):
        return {"space": s, "tm": 2 * i + t % 2} if c else {"space": 2 * i, "tm": t}

    def peer2(c, j):
        return {"space": 2 * (j // 2) + 1, "tm": 2 * (t // 2) + j % 2} if c else {"space": s, "tm": j}

    loads = [
        pltpu.make_async_copy(tok_hbm, tok, lsem.at[0]),
        pltpu.make_async_copy(gout_hbm, gout, lsem.at[1]),
        pltpu.make_async_copy(wqkv_hbm, wqkv, lsem.at[2]),
    ]
    for load in loads:
        load.start()

    barrier = pltpu.get_barrier_semaphore()

    def greet(i, carry):
        w = lax.rem(i + s, WORKERS)

        @pl.when(worker_space(w) != s)
        def _():
            signal(barrier, worker_space(w), t)

        signal(barrier, worker_space(w), (1 - w % 2) * after + (w % 2) * before)
        return carry

    lax.fori_loop(0, WORKERS, greet, 0)
    signal(barrier, sibling["space"], t)
    for c in range(2):

        @pl.when(core == c)
        def _(c=c):
            def greet1(n, carry):
                peer = peer1(c, (rank1(c) + n) % FIRST[c])
                signal(barrier, peer["space"], peer["tm"])
                return carry

            def greet2(n, carry):
                peer = peer2(c, (rank2(c) + n) % SECOND[c])
                signal(barrier, peer["space"], peer["tm"])
                return carry

            lax.fori_loop(1, FIRST[c], greet1, 0)
            lax.fori_loop(1, SECOND[c], greet2, 0)

    pl.semaphore_wait(barrier, is_worker * (2 * slots - 1) + 15 + 4 * core)

    def query_refs(i):
        return res_q.at[i], got_q.at[half, head]

    def key_refs(i):
        return res_kv.at[i, pl.ds(2 - 2 * half, 4)], got_kv.at[half, head]

    def query_copy(i):
        a, b = query_refs(i)
        return remote(a, b, cq.at[i], cqr, {"space": i, "tm": t})

    def key_copy(i):
        a, b = key_refs(i)
        return remote(a, b, cs.at[i], cr, {"space": i, "tm": t})

    def halo_copy(i):
        return remote(
            res_kv.at[i, pl.ds(4 * half, 2)], got_halo.at[half, head], ch.at[i], crh,
            {"space": i, "tm": other},
        )

    @pl.when(is_worker == 1)
    def _():
        def send_queries(i, carry):
            to = lax.rem(i + s, slots)

            @pl.when(to != s)
            def _():
                query_copy(to).start()

            @pl.when(to == s)
            def _():
                a, b = query_refs(to)
                pltpu.make_async_copy(a, b, cqr).start()

            return carry

        def send_keys(i, carry):
            to = lax.rem(i + s, slots)
            halo_copy(to).start()

            @pl.when(to != s)
            def _():
                key_copy(to).start()

            @pl.when(to == s)
            def _():
                a, b = key_refs(to)
                pltpu.make_async_copy(a, b, cr).start()

            return carry

        lax.fori_loop(0, slots, send_queries, 0)
        lax.fori_loop(0, slots, send_keys, 0)

    for load in loads:
        load.wait()
    tok_t = tok[...].T

    def pair(a, b):
        low = where_lane(a, pltpu.roll(b, HD, 1))
        high = where_lane(pltpu.roll(a, HD, 1), b)
        return low.astype(jnp.bfloat16), high.astype(jnp.bfloat16)

    def query_terms():
        pltpu.make_async_copy(got_q, got_q, cqr).wait()
        for i in range(HEADS // 2):
            at = 128 * i
            both = []
            for h in (2 * i, 2 * i + 1):
                rows = jnp.concatenate([got_q[0, h], got_q[1, h]], axis=0).astype(jnp.float32)
                both.append(rows.reshape(LF * BP, 128))
            dq, da = pair(*both)
            grads[:, at : at + 128] = dq
            att[:, at : at + 128] = da
            src[D * i : D * (i + 1), :] = jnp.dot(
                tok_t, dq, preferred_element_type=jnp.float32
            ).astype(jnp.bfloat16)
        att_t = att[...].T
        for i in range(6):
            start = 3 * D + HW * i
            src[start : start + HW, :] = jnp.dot(
                att_t, gout[:, 128 * i : 128 * (i + 1)], preferred_element_type=jnp.float32
            ).astype(jnp.bfloat16)

    def key_terms():
        pltpu.make_async_copy(got_halo, got_halo, crh).wait()
        pltpu.make_async_copy(got_kv, got_kv, cr).wait()
        for i in range(HEADS // 2):
            both = []
            for h in (2 * i, 2 * i + 1):
                low = got_kv[0, h].astype(jnp.float32)
                high = got_kv[1, h].astype(jnp.float32)
                edge = jnp.concatenate([got_halo[1, h], got_halo[0, h]], axis=0).astype(jnp.float32)
                both.append((low + high + edge).reshape(LF * BP, 128))
            for k, value in enumerate(pair(*both)):
                at = (1 + k) * HW + 128 * i
                grads[:, at : at + 128] = value
                start = KEYS_AT + D * (3 * k + i)
                src[start : start + D, :] = jnp.dot(
                    tok_t, value, preferred_element_type=jnp.float32
                ).astype(jnp.bfloat16)

    def token_grads():
        tg_ref[...] = lax.dot_general(
            grads[...], wqkv[...], (((1,), (1,)), ((), ())), preferred_element_type=jnp.float32
        ).astype(jnp.bfloat16)

    def stages(c, p):
        b0, hs, b1, s1, h2, b2, b3 = (early, late)[p]
        first, second = FIRST[c], SECOND[c]
        half_rows, piece = HALVES[p], PIECES[p]
        length = half_rows // first
        step = half_rows // PARTS
        parts = PARTS // first
        pieces = step // piece
        base = STARTS[p] + c * half_rows
        far = STARTS[p] + (1 - c) * half_rows
        here1, here2 = rank1(c), rank2(c)

        def rows(start, index, size):
            return pl.ds(pl.multiple_of(start + index * size, 64), size)

        def copy0(k):
            return remote(
                src.at[rows(far, k, step)], b0.at[rows(0, k, step)], ss0.at[p, k], r0.at[p, k], sibling
            )

        def copy1(i, slot):
            return remote(
                hs.at[rows(0, i, length)], b1.at[rows(0, slot, length)], ss1.at[p, i],
                r1.at[p, slot], peer1(c, i),
            )

        def copy2(j, slot):
            return remote(h2.at[j], b2.at[slot], ss2.at[p, j], r2.at[p, slot], peer2(c, j))

        def copy3(j, slot):
            return remote(b3.at[slot], b3.at[slot], ss3.at[p, j], r3.at[p, slot], peer2(c, j))

        def copy4(i, chunk):
            where = rows(base, chunk, length)
            return remote(out.at[where], out.at[where], ss4.at[p, i], r4.at[p, chunk], peer1(c, i))

        def copy5(chunk):
            where = rows(base, chunk, length)
            return remote(out.at[where], out.at[where], ss5.at[p, chunk], r5.at[p, chunk], sibling)

        def from_sibling(chunk):
            where = rows(far, chunk, half_rows // FIRST[1 - c])
            return remote(out.at[where], out.at[where], ss5.at[p, chunk], r5.at[p, chunk], sibling)

        def loop(low, high, body):
            def run(n, carry):
                body(n)
                return carry

            lax.fori_loop(low, high, run, 0)

        def send_pair():
            begin = ((rank1(1 - c) + 1) % FIRST[1 - c]) * (PARTS // FIRST[1 - c])
            loop(0, PARTS, lambda n: copy0((begin + n) % PARTS).start())

        def both(k):
            copy0(k).wait_recv()
            mine = src[rows(base, k, step), :].astype(jnp.float32)
            return mine + b0[rows(0, k, step), :].astype(jnp.float32)

        def send_first():
            def one(n):
                i = (here1 + n) % first
                for e in range(parts):
                    k = i * parts + e
                    hs[rows(0, k, step), :] = both(k).astype(jnp.bfloat16)
                copy1(i, here1).start()

            loop(1, first, one)
            for e in range(parts):
                own = both(here1 * parts + e)
                s1[e * pieces : (e + 1) * pieces] = own.reshape(pieces, piece, 128)

        def send_second():
            def one(n):
                i = (here1 + first - n) % first
                copy1(i, i).wait_recv()
                more = b1[rows(0, i, length), :].astype(jnp.float32)
                s1[0:second] += more.reshape(second, piece, 128)

            loop(1, first, one)
            h2[0:second] = s1[0:second].astype(jnp.bfloat16)
            loop(1, second, lambda n: copy2((here2 + n) % second, here2).start())

        def send_third():
            def one(n, sum_so_far):
                j = (here2 + second - n) % second
                copy2(j, j).wait_recv()
                return sum_so_far + b2[j].astype(jnp.float32)

            b3[here2] = lax.fori_loop(1, second, one, s1[here2]).astype(jnp.bfloat16)
            loop(1, second, lambda n: copy3((here2 + n) % second, here2).start())

        def send_fourth():
            def one(n):
                j = (here2 + second - n) % second
                copy3(j, j).wait_recv()

            loop(1, second, one)
            whole = b3[0:second].astype(jnp.float32).reshape(length, 128)
            out[rows(base, here1, length), :] = whole.astype(jnp.bfloat16)
            loop(1, first, lambda n: copy4((here1 + n) % first, here1).start())
            copy5(here1).start()

        def send_fifth():
            def one(n):
                i = (here1 + first - n) % first
                copy4(i, i).wait_recv()
                copy5(i).start()

            loop(1, first, one)

        def end():
            loop(0, FIRST[1 - c], lambda n: from_sibling(n).wait_recv())
            loop(0, PARTS, lambda n: copy0(n).wait_send())

            def one(n):
                i = (here1 + n) % first
                copy1(i, here1).wait_send()
                copy4(i, here1).wait_send()
                copy5(i).wait_send()

            loop(1, first, one)
            copy5(here1).wait_send()

            def two(n):
                j = (here2 + n) % second
                copy2(j, here2).wait_send()
                copy3(j, here2).wait_send()

            loop(1, second, two)

        return send_pair, send_first, send_second, send_third, send_fourth, send_fifth, end

    def sum_all(c):
        a, b = stages(c, 0), stages(c, 1)
        query_terms()
        a[0]()
        key_terms()
        b[0]()
        a[1]()
        b[1]()
        a[2]()
        b[2]()
        a[3]()
        token_grads()
        b[3]()
        a[4]()
        b[4]()
        a[5]()
        b[5]()
        a[6]()
        b[6]()

    for c in range(2):
        pl.when(core == c)(functools.partial(sum_all, c))

    @pl.when(is_worker == 1)
    def _():
        def finish(i, carry):
            halo_copy(i).wait_send()

            @pl.when(i != s)
            def _():
                query_copy(i).wait_send()
                key_copy(i).wait_send()

            return carry

        lax.fori_loop(0, slots, finish, 0)


def finish(res_q, res_kv, tokens, grad_out, w_qkv, slots, tm_size):
    hbm = pl.BlockSpec(memory_space=pltpu.HBM)
    vmem = pl.BlockSpec(memory_space=pltpu.VMEM)
    dma = pltpu.SemaphoreType.DMA
    sums = [
        [pltpu.VMEM((HALVES[p], 128), jnp.bfloat16)] * 3
        + [pltpu.VMEM((16, PIECES[p], 128), jnp.float32)]
        + [pltpu.VMEM((16, PIECES[p], 128), jnp.bfloat16)] * 3
        for p in range(2)
    ]
    return pl.pallas_call(
        functools.partial(finish_kernel, slots, tm_size),
        out_shape=(
            jax.ShapeDtypeStruct((LF * BP, D), jnp.bfloat16),
            jax.ShapeDtypeStruct((ROWS, 128), jnp.bfloat16),
        ),
        in_specs=[vmem, vmem] + [hbm] * 3,
        out_specs=(vmem, vmem),
        scratch_shapes=[
            pltpu.VMEM((2, HEADS, 2, BP, 128), jnp.bfloat16),
            pltpu.VMEM((2, HEADS, LF, BP, 128), jnp.bfloat16),
            pltpu.VMEM((2, HEADS, 2, BP, 128), jnp.bfloat16),
            pltpu.VMEM(tokens.shape, jnp.bfloat16),
            pltpu.VMEM(grad_out.shape, jnp.bfloat16),
            pltpu.VMEM(w_qkv.shape, jnp.bfloat16),
            pltpu.VMEM((LF * BP, 3 * HW), jnp.bfloat16),
            pltpu.VMEM((LF * BP, HW), jnp.bfloat16),
            pltpu.VMEM((ROWS, 128), jnp.bfloat16),
            *sums,
            dma((3,)), dma((slots,)), dma((slots,)), dma((slots,)), dma, dma, dma,
            *[dma((2, size)) for size in (8, 8, 8, 8, 16, 16, 16, 16, 8, 8, 8, 8)],
        ],
        compiler_params=pltpu.CompilerParams(
            has_side_effects=True, collective_id=2, vmem_limit_bytes=32 << 20
        ),
        name="finish",
    )(res_q, res_kv, tokens, grad_out, w_qkv)


def widen_kernel(src, qkv, out):
    for i in range(9):
        start = D * i if i < 3 else KEYS_AT + D * (i - 3)
        qkv[:, 128 * i : 128 * (i + 1)] = src[start : start + D, :].astype(jnp.float32)
    for i in range(6):
        start = 3 * D + HW * i
        out[:, 128 * i : 128 * (i + 1)] = src[start : start + HW, :].astype(jnp.float32)


def widen(terms):
    vmem = pl.BlockSpec(memory_space=pltpu.VMEM)
    return pl.pallas_call(
        widen_kernel,
        out_shape=(
            jax.ShapeDtypeStruct((D, 3 * HW), jnp.float32),
            jax.ShapeDtypeStruct((HW, D), jnp.float32),
        ),
        in_specs=[vmem],
        out_specs=(vmem, vmem),
        compiler_params=pltpu.CompilerParams(vmem_limit_bytes=32 << 20),
        name="widen",
    )(terms)


def shards(tokens, grad_out, w_qkv, w_out, brain_mask, block_table):
    slots = lax.axis_size("space")
    tm_size = lax.axis_size("tm")
    flat_tokens = tokens.reshape(-1, D)
    flat_grad = grad_out.reshape(-1, D)
    held = spread(flat_tokens, flat_grad, w_qkv, w_out, slots, tm_size)
    res_q, res_kv = attend(block_table, brain_mask, held, tm_size)
    token_grads, terms = finish(res_q, res_kv, flat_tokens, flat_grad, w_qkv, slots, tm_size)
    qkv_grads, out_grads = widen(terms)
    return (token_grads.reshape(tokens.shape), qkv_grads, out_grads)


def solution(mesh):
    in_specs = (P("space", "tm", None, None), P("space", "tm", None, None), P(), P(), P(), P())
    out_specs = (P("space", "tm", None, None), P(), P())
    return jax.shard_map(shards, mesh=mesh, in_specs=in_specs, out_specs=out_specs, check_vma=False)
```

```python
import functools

import numpy as np
import jax
import jax.numpy as jnp
from jax import lax
from jax.experimental import pallas as pl
from jax.experimental.pallas import tpu as pltpu
from jax.sharding import PartitionSpec as P

D = 768
HEADS = 6
HD = 64
SIDE = 4
BP = 64
RAD_S = 3
RAD_T = 2
HW = HEADS * HD
LF = 4
KF = 6
KR = KF * BP
QR = 2 * BP
WORKERS = 2 * HEADS


def where_lane(low, high):
    lane = lax.broadcasted_iota(jnp.int32, low.shape, low.ndim - 1)
    return jnp.where(lane < HD, low, high)


MESH = pl.DeviceIdType.MESH


def worker_space(w):
    return w


def worker_of(space):
    return 1 - space // WORKERS, space


def signal(semaphore, space, tm):
    pl.semaphore_signal(semaphore, inc=1, device_id={"space": space, "tm": tm}, device_id_type=MESH)


def remote(src, dst, send, recv, device):
    return pltpu.make_async_remote_copy(
        src_ref=src, dst_ref=dst, send_sem=send, recv_sem=recv, device_id=device, device_id_type=MESH
    )


def spread_kernel(
    slots, tm_size, tok_hbm, gout_hbm, wqkv_hbm, wout_hbm, held,
    tok, gout, wqkv, wout, packed, lsem, ssem, hsem, rsem,
):
    me = lax.axis_index("space")
    t = lax.axis_index("tm")
    after = lax.rem(t + 1, tm_size)
    before = lax.rem(t + tm_size - 1, tm_size)
    is_worker, worker = worker_of(me)
    loads = [
        pltpu.make_async_copy(wqkv_hbm, wqkv, lsem.at[0]),
        pltpu.make_async_copy(tok_hbm, tok, lsem.at[1]),
        pltpu.make_async_copy(wout_hbm, wout, lsem.at[2]),
        pltpu.make_async_copy(gout_hbm, gout, lsem.at[3]),
    ]
    for load in loads:
        load.start()

    barrier = pltpu.get_barrier_semaphore()

    @pl.when(is_worker == 1)
    def _():
        half = worker % 2
        source = lax.rem(t + tm_size - 1 + 2 * half, tm_size)

        def greet(i, carry):
            signal(barrier, lax.rem(me + i, slots), t)
            return carry

        def greet_halo(i, carry):
            signal(barrier, i, source)
            return carry

        lax.fori_loop(1, slots, greet, 0)
        lax.fori_loop(0, slots, greet_halo, 0)

    for load in loads:
        load.wait()
    proj = jnp.dot(tok[...], wqkv[...], preferred_element_type=jnp.float32)
    gatt = lax.dot_general(
        gout[...], wout[...], (((1,), (1,)), ((), ())), preferred_element_type=jnp.float32
    )

    def pair(low, high):
        first = where_lane(low, pltpu.roll(high, HD, 1)).astype(jnp.bfloat16)
        second = where_lane(pltpu.roll(low, HD, 1), high).astype(jnp.bfloat16)
        return first.reshape(LF, BP, 128), second.reshape(LF, BP, 128)

    for i in range(HEADS // 2):
        at = 128 * i
        keys = pair(proj[:, HW + at : HW + at + 128], proj[:, 2 * HW + at : 2 * HW + at + 128])
        queries = pair(proj[:, at : at + 128], gatt[:, at : at + 128])
        for j in range(2):
            packed[2 * i + j, 0:2] = queries[j][2:4]
            packed[2 * i + j, 2:6] = keys[j]
            packed[2 * i + j, 6:8] = queries[j][0:2]

    pl.semaphore_wait(barrier, 2 * WORKERS - is_worker)

    def main_refs(w):
        start = 2 - 2 * (w % 2)
        return packed.at[w // 2, pl.ds(start, 6)], held.at[me, pl.ds(start, 6)]

    def main_copy(w):
        src, dst = main_refs(w)
        return remote(src, dst, ssem.at[w], rsem, {"space": worker_space(w), "tm": t})

    def halo_copy(h, half):
        return remote(
            packed.at[h, pl.ds(4 - 2 * half, 2)], held.at[me, pl.ds(6 * half, 2)],
            hsem.at[2 * h + half], rsem,
            {"space": worker_space(2 * h + half), "tm": before if half else after},
        )

    def send(i, carry):
        w = lax.rem(i + me, WORKERS)

        @pl.when(worker_space(w) != me)
        def _():
            main_copy(w).start()

        @pl.when(worker_space(w) == me)
        def _():
            src, dst = main_refs(w)
            pltpu.make_async_copy(src, dst, rsem).start()

        return carry

    def send_halo(i, carry):
        h = lax.rem(i + me // 2, HEADS)
        halo_copy(h, 0).start()
        halo_copy(h, 1).start()
        return carry

    lax.fori_loop(0, HEADS, send_halo, 0)
    lax.fori_loop(0, WORKERS, send, 0)

    def finish(w, carry):
        @pl.when(worker_space(w) != me)
        def _():
            main_copy(w).wait_send()

        return carry

    def finish_halo(h, carry):
        halo_copy(h, 0).wait_send()
        halo_copy(h, 1).wait_send()
        return carry

    @pl.when(is_worker == 1)
    def _():
        pltpu.make_async_copy(held, held, rsem).wait()

    lax.fori_loop(0, HEADS, finish_halo, 0)
    lax.fori_loop(0, WORKERS, finish, 0)


def spread(tokens, grad_out, w_qkv, w_out, slots, tm_size):
    hbm = pl.BlockSpec(memory_space=pltpu.HBM)
    return pl.pallas_call(
        functools.partial(spread_kernel, slots, tm_size),
        out_shape=jax.ShapeDtypeStruct((slots, 8, BP, 128), jnp.bfloat16),
        in_specs=[hbm] * 4,
        out_specs=hbm,
        scratch_shapes=[
            pltpu.VMEM(tokens.shape, jnp.bfloat16),
            pltpu.VMEM(grad_out.shape, jnp.bfloat16),
            pltpu.VMEM(w_qkv.shape, jnp.bfloat16),
            pltpu.VMEM(w_out.shape, jnp.bfloat16),
            pltpu.VMEM((HEADS, 8, BP, 128), jnp.bfloat16),
            pltpu.SemaphoreType.DMA((4,)),
            pltpu.SemaphoreType.DMA((WORKERS,)),
            pltpu.SemaphoreType.DMA((WORKERS,)),
            pltpu.SemaphoreType.DMA,
        ],
        compiler_params=pltpu.CompilerParams(
            has_side_effects=True, collective_id=1, vmem_limit_bytes=60 << 20
        ),
        name="spread",
    )(tokens, grad_out, w_qkv, w_out)


UNROLL = 8
MOST = 12
PAIRS = 72


def window_bias():
    patch = np.arange(BP)
    px, py = patch // 16, patch // 4 % 4
    out = np.full((10, KF, BP, 2, BP), -np.inf, np.float32)
    for n in range(9):
        dr, dc = n // 3 - 1, n % 3 - 1
        near_x = np.abs(px[:, None] + 4 * dr - px[None, :]) <= RAD_S
        near_y = np.abs(py[:, None] + 4 * dc - py[None, :]) <= RAD_S
        for j in range(KF):
            for i in range(2):
                near = near_x & near_y & (abs(j - RAD_T - i) <= RAD_T)
                out[n, j, :, i, :] = np.where(near, 0.0, -np.inf)
    return out.reshape(10, KR, QR)


def attend_kernel(
    tm_size, table, mask, held_hbm, bias_hbm, res_q, res_kv,
    held, kvt, bias, acc, scores, dots, rhs_a, rhs_d, total, inverse, delta, att, dq,
    slot_of, brain, pair_q, pair_k, pair_off, sem,
):
    me = lax.axis_index("space")
    t = lax.axis_index("tm")
    is_worker, worker = worker_of(me)
    half = worker % 2
    slots = held.shape[0]
    scaling = HD ** (-0.5)

    def keys_of(slot):
        return held[slot, pl.ds(2 * half, KF)].reshape(KR, 128)

    @pl.when(is_worker == 1)
    def _():
        loads = [
            pltpu.make_async_copy(held_hbm, held, sem.at[0]),
            pltpu.make_async_copy(bias_hbm, bias, sem.at[1]),
        ]
        for load in loads:
            load.start()

        def place(s, carry):
            slot_of[table[s]] = s
            return carry

        lax.fori_loop(0, slots, place, 0)

        def list_block(g, carry):
            blocks, pairs = carry
            inside_brain = mask[g] == 1
            slot = slot_of[g]
            brain[blocks] = slot
            row = g // SIDE
            col = g % SIDE
            for n in range(9):
                nr = row + (n // 3 - 1)
                nc = col + (n % 3 - 1)
                inside = (nr >= 0) & (nr < SIDE) & (nc >= 0) & (nc < SIDE)
                nb = jnp.clip(nr, 0, SIDE - 1) * SIDE + jnp.clip(nc, 0, SIDE - 1)
                valid = inside_brain & inside & (mask[nb] == 1)
                pair_q[pairs] = slot
                pair_k[pairs] = slot_of[nb]
                pair_off[pairs] = n
                pairs = jnp.minimum(pairs + valid.astype(jnp.int32), PAIRS)
            return (blocks + inside_brain.astype(jnp.int32), pairs)

        blocks, pairs = lax.fori_loop(0, slots, list_block, (jnp.int32(0), jnp.int32(0)))
        for n in range(UNROLL):
            pair_q[pairs + n] = brain[0]
            pair_k[pairs + n] = brain[0]
            pair_off[pairs + n] = 9
        steps = (pairs + (UNROLL - 1)) // UNROLL

        acc[...] = jnp.zeros_like(acc)
        res_q[...] = jnp.zeros_like(res_q)
        total[...] = jnp.zeros_like(total)
        att[...] = jnp.zeros_like(att)
        dq[...] = jnp.zeros_like(dq)

        def prepare(b, carry):
            slot = brain[b]
            kvt[slot] = keys_of(slot).T
            rows = held[slot, pl.ds(6 - 6 * half, 2)].reshape(QR, 128)
            cols = rows.T
            zero = jnp.zeros_like(cols)
            first = lax.broadcasted_iota(jnp.int32, cols.shape, 0) < HD
            left = lax.broadcasted_iota(jnp.int32, cols.shape, 1) < HD
            rhs_a[slot, :, :QR] = jnp.where(first, cols * scaling, zero)
            rhs_a[slot, :, QR:] = jnp.where(first, zero, cols)
            rhs_d[slot, :QR, :] = jnp.where(left, rows, zero)
            rhs_d[slot, QR:, :] = jnp.where(left, zero, rows)
            return carry

        loads[0].wait()
        lax.fori_loop(0, blocks, prepare, 0)
        loads[1].wait()

        @pl.when((t == 0) & (half == 0))
        def _():
            bias[:, 0 : 2 * BP, :] = jnp.full((10, 2 * BP, QR), -jnp.inf, jnp.float32)

        @pl.when((t == tm_size - 1) & (half == 1))
        def _():
            bias[:, 4 * BP : 6 * BP, :] = jnp.full((10, 2 * BP, QR), -jnp.inf, jnp.float32)

        def by_rows(x):
            return x.reshape(KR // 8, 8, QR)

        def score(step, carry):
            for u in range(UNROLL):
                p = step * UNROLL + u
                keys = keys_of(pair_k[p])
                both = jnp.dot(keys, rhs_a[pair_q[p]], preferred_element_type=jnp.float32)
                e = jnp.exp(both[:, :QR] + bias[pair_off[p]])
                scores[p] = e
                dots[p] = both[:, QR:]
                total[pair_q[p]] += jnp.sum(by_rows(e), axis=0)
            return carry

        lax.fori_loop(0, steps, score, 0)

        def invert(b, carry):
            slot = brain[b]
            whole = jnp.sum(total[slot], axis=0, keepdims=True)
            inverse[slot] = jnp.broadcast_to(1.0 / whole, (8, QR))
            return carry

        lax.fori_loop(0, blocks, invert, 0)

        def weigh(step, carry):
            for u in range(UNROLL):
                p = step * UNROLL + u
                w = by_rows(scores[p]) * inverse[pair_q[p]][None]
                w = w.reshape(KR, QR).astype(jnp.bfloat16)
                att[pair_q[p]] += jnp.dot(
                    kvt[pair_k[p], HD:, :], w, preferred_element_type=jnp.float32
                )
            return carry

        lax.fori_loop(0, steps, weigh, 0)

        def rest(b, carry):
            slot = brain[b]
            rounded = att[slot].astype(jnp.bfloat16).astype(jnp.float32)
            att[slot] = rounded
            grad = rhs_a[slot, HD:, QR:].astype(jnp.float32)
            one = jnp.sum(grad * rounded, axis=0, keepdims=True)
            delta[slot] = jnp.broadcast_to(one, (8, QR))
            return carry

        lax.fori_loop(0, blocks, rest, 0)

        def spread_grad(step, carry):
            for u in range(UNROLL):
                p = step * UNROLL + u
                qs = pair_q[p]
                w = by_rows(scores[p]) * inverse[qs][None]
                ds = w * (by_rows(dots[p]) - delta[qs][None])
                ds = ds.reshape(KR, QR).astype(jnp.bfloat16)
                lhs = jnp.concatenate([ds, w.reshape(KR, QR).astype(jnp.bfloat16)], axis=1)
                acc[pair_k[p]] += jnp.dot(lhs, rhs_d[qs], preferred_element_type=jnp.float32)
                dq[qs] += jnp.dot(kvt[pair_k[p], :HD, :], ds, preferred_element_type=jnp.float32)
            return carry

        lax.fori_loop(0, steps, spread_grad, 0)

        def give(b, carry):
            slot = brain[b]
            both = jnp.concatenate([dq[slot] * scaling, att[slot]], axis=0).T
            res_q[slot] = both.astype(jnp.bfloat16).reshape(2, BP, 128)
            return carry

        lax.fori_loop(0, blocks, give, 0)

        def finish_keys(s, carry):
            whole = acc[s]
            res_kv[s] = where_lane(whole * scaling, whole).astype(jnp.bfloat16).reshape(KF, BP, 128)
            return carry

        lax.fori_loop(0, slots, finish_keys, 0)


def attend(block_table, brain_mask, held, tm_size):
    slots = held.shape[0]
    smem = pl.BlockSpec(memory_space=pltpu.SMEM)
    vmem = pl.BlockSpec(memory_space=pltpu.VMEM)
    hbm = pl.BlockSpec(memory_space=pltpu.HBM)
    store = (PAIRS + UNROLL, KR, QR)
    return pl.pallas_call(
        functools.partial(attend_kernel, tm_size),
        out_shape=(
            jax.ShapeDtypeStruct((slots, 2, BP, 128), jnp.bfloat16),
            jax.ShapeDtypeStruct((slots, KF, BP, 128), jnp.bfloat16),
        ),
        in_specs=[smem, smem, hbm, hbm],
        out_specs=(vmem, vmem),
        scratch_shapes=[
            pltpu.VMEM(held.shape, jnp.bfloat16),
            pltpu.VMEM((slots, 128, KR), jnp.bfloat16),
            pltpu.VMEM((10, KR, QR), jnp.float32),
            pltpu.VMEM((slots, KR, 128), jnp.float32),
            pltpu.VMEM(store, jnp.float32),
            pltpu.VMEM(store, jnp.float32),
            pltpu.VMEM((slots, 128, 2 * QR), jnp.bfloat16),
            pltpu.VMEM((slots, 2 * QR, 128), jnp.bfloat16),
            pltpu.VMEM((slots, 8, QR), jnp.float32),
            pltpu.VMEM((slots, 8, QR), jnp.float32),
            pltpu.VMEM((slots, 8, QR), jnp.float32),
            pltpu.VMEM((slots, HD, QR), jnp.float32),
            pltpu.VMEM((slots, HD, QR), jnp.float32),
            pltpu.SMEM((16,), jnp.int32),
            pltpu.SMEM((17,), jnp.int32),
            pltpu.SMEM((PAIRS + UNROLL,), jnp.int32),
            pltpu.SMEM((PAIRS + UNROLL,), jnp.int32),
            pltpu.SMEM((PAIRS + UNROLL,), jnp.int32),
            pltpu.SemaphoreType.DMA((2,)),
        ],
        compiler_params=pltpu.CompilerParams(vmem_limit_bytes=50 << 20),
        name="attend",
    )(block_table, brain_mask, held, jnp.asarray(window_bias()))


ROWS = 9216
KEYS_AT = 6 * D
STARTS = (0, 4096)
HALVES = (2048, 2560)
PIECES = (32, 40)
PARTS = 8
FIRST = (8, 4)
SECOND = (8, 16)


def finish_kernel(
    slots, tm_size, res_q, res_kv, tok_hbm, gout_hbm, wqkv_hbm, tg_ref, out,
    got_q, got_kv, got_halo, pair_in, summed, tok, gout, wqkv, grads, att, src, early, late,
    lsem, psem, cq, cs, ch, cqr, cr, crh, ss0, r0, ss1, r1, ss2, r2, ss3, r3, ss4, r4, ss5, r5,
):
    s = lax.axis_index("space")
    t = lax.axis_index("tm")
    core = s % 2
    chip = s // 2
    is_worker, worker = worker_of(s)
    head = worker // 2
    half = worker % 2
    other = lax.rem(t + tm_size + 2 * half - 1, tm_size)
    after = lax.rem(t + 1, tm_size)
    before = lax.rem(t + tm_size - 1, tm_size)
    sibling = {"space": s + 1 - 2 * core, "tm": t}

    def rank1(c):
        return t // 2 if c else chip

    def rank2(c):
        return 2 * chip + t % 2 if c else t

    def peer1(c, i):
        return {"space": s, "tm": 2 * i + t % 2} if c else {"space": 2 * i, "tm": t}

    def peer2(c, j):
        return {"space": 2 * (j // 2) + 1, "tm": 2 * (t // 2) + j % 2} if c else {"space": s, "tm": j}

    loads = [
        pltpu.make_async_copy(tok_hbm, tok, lsem.at[0]),
        pltpu.make_async_copy(gout_hbm, gout, lsem.at[1]),
        pltpu.make_async_copy(wqkv_hbm, wqkv, lsem.at[2]),
    ]
    for load in loads:
        load.start()

    barrier = pltpu.get_barrier_semaphore()

    def greet(i, carry):
        w = lax.rem(i + s, WORKERS)

        @pl.when(worker_space(w) != s)
        def _():
            signal(barrier, worker_space(w), t)

        signal(barrier, worker_space(w), (1 - w % 2) * after + (w % 2) * before)
        return carry

    lax.fori_loop(0, WORKERS, greet, 0)
    signal(barrier, sibling["space"], t)
    for c in range(2):

        @pl.when(core == c)
        def _(c=c):
            def greet1(n, carry):
                peer = peer1(c, (rank1(c) + n) % FIRST[c])
                signal(barrier, peer["space"], peer["tm"])
                return carry

            def greet2(n, carry):
                peer = peer2(c, (rank2(c) + n) % SECOND[c])
                signal(barrier, peer["space"], peer["tm"])
                return carry

            lax.fori_loop(1, FIRST[c], greet1, 0)
            lax.fori_loop(1, SECOND[c], greet2, 0)

    pl.semaphore_wait(barrier, is_worker * (2 * slots - 1) + 15 + 4 * core)

    each = slots // 2
    pair_copy = remote(
        res_kv.at[pl.ds(each * (1 - half), each), pl.ds(2 - 2 * half, 4)], pair_in,
        psem.at[0], psem.at[1], sibling,
    )

    def query_refs(i):
        return res_q.at[i], got_q.at[half, head]

    def key_refs(i):
        return summed.at[i % each], got_kv.at[head]

    def query_copy(i):
        a, b = query_refs(i)
        return remote(a, b, cq.at[i], cqr, {"space": i, "tm": t})

    def key_copy(i):
        a, b = key_refs(i)
        return remote(a, b, cs.at[i], cr, {"space": i, "tm": t})

    def halo_copy(i):
        return remote(
            res_kv.at[i, pl.ds(4 * half, 2)], got_halo.at[half, head], ch.at[i], crh,
            {"space": i, "tm": other},
        )

    @pl.when(is_worker == 1)
    def _():
        def send_queries(i, carry):
            to = lax.rem(i + s, slots)

            @pl.when(to != s)
            def _():
                query_copy(to).start()

            @pl.when(to == s)
            def _():
                a, b = query_refs(to)
                pltpu.make_async_copy(a, b, cqr).start()

            return carry

        def send_halo(i, carry):
            halo_copy(lax.rem(i + s, slots)).start()
            return carry

        def send_keys(i, carry):
            at = lax.rem(i + s, each)
            to = each * half + at
            mine = res_kv[to, pl.ds(2 - 2 * half, 4)].astype(jnp.float32)
            summed[at] = (mine + pair_in[at].astype(jnp.float32)).astype(jnp.bfloat16)

            @pl.when(to != s)
            def _():
                key_copy(to).start()

            @pl.when(to == s)
            def _():
                a, b = key_refs(to)
                pltpu.make_async_copy(a, b, cr).start()

            return carry

        pair_copy.start()
        lax.fori_loop(0, slots, send_queries, 0)
        lax.fori_loop(0, slots, send_halo, 0)
        pair_copy.wait_recv()
        lax.fori_loop(0, each, send_keys, 0)

    for load in loads:
        load.wait()
    tok_t = tok[...].T

    def pair(a, b):
        low = where_lane(a, pltpu.roll(b, HD, 1))
        high = where_lane(pltpu.roll(a, HD, 1), b)
        return low.astype(jnp.bfloat16), high.astype(jnp.bfloat16)

    def query_terms():
        pltpu.make_async_copy(got_q, got_q, cqr).wait()
        for i in range(HEADS // 2):
            at = 128 * i
            both = []
            for h in (2 * i, 2 * i + 1):
                rows = jnp.concatenate([got_q[0, h], got_q[1, h]], axis=0).astype(jnp.float32)
                both.append(rows.reshape(LF * BP, 128))
            dq, da = pair(*both)
            grads[:, at : at + 128] = dq
            att[:, at : at + 128] = da
            src[D * i : D * (i + 1), :] = jnp.dot(
                tok_t, dq, preferred_element_type=jnp.float32
            ).astype(jnp.bfloat16)
        att_t = att[...].T
        for i in range(6):
            start = 3 * D + HW * i
            src[start : start + HW, :] = jnp.dot(
                att_t, gout[:, 128 * i : 128 * (i + 1)], preferred_element_type=jnp.float32
            ).astype(jnp.bfloat16)

    def key_terms():
        pltpu.make_async_copy(got_halo, got_halo, crh).wait()
        pltpu.make_async_copy(got_kv, got_kv, cr).wait()
        for i in range(HEADS // 2):
            both = []
            for h in (2 * i, 2 * i + 1):
                edge = jnp.concatenate([got_halo[1, h], got_halo[0, h]], axis=0).astype(jnp.float32)
                both.append((got_kv[h].astype(jnp.float32) + edge).reshape(LF * BP, 128))
            for k, value in enumerate(pair(*both)):
                at = (1 + k) * HW + 128 * i
                grads[:, at : at + 128] = value
                start = KEYS_AT + D * (3 * k + i)
                src[start : start + D, :] = jnp.dot(
                    tok_t, value, preferred_element_type=jnp.float32
                ).astype(jnp.bfloat16)

    def token_grads():
        tg_ref[...] = lax.dot_general(
            grads[...], wqkv[...], (((1,), (1,)), ((), ())), preferred_element_type=jnp.float32
        ).astype(jnp.bfloat16)

    def stages(c, p):
        b0, hs, b1, s1, h2, b2, b3 = (early, late)[p]
        first, second = FIRST[c], SECOND[c]
        half_rows, piece = HALVES[p], PIECES[p]
        length = half_rows // first
        step = half_rows // PARTS
        parts = PARTS // first
        pieces = step // piece
        base = STARTS[p] + c * half_rows
        far = STARTS[p] + (1 - c) * half_rows
        here1, here2 = rank1(c), rank2(c)

        def rows(start, index, size):
            return pl.ds(pl.multiple_of(start + index * size, 64), size)

        def copy0(k):
            return remote(
                src.at[rows(far, k, step)], b0.at[rows(0, k, step)], ss0.at[p, k], r0.at[p, k], sibling
            )

        def copy1(i, slot):
            return remote(
                hs.at[rows(0, i, length)], b1.at[rows(0, slot, length)], ss1.at[p, i],
                r1.at[p, slot], peer1(c, i),
            )

        def copy2(j, slot):
            return remote(h2.at[j], b2.at[slot], ss2.at[p, j], r2.at[p, slot], peer2(c, j))

        def copy3(j, slot):
            return remote(b3.at[slot], b3.at[slot], ss3.at[p, j], r3.at[p, slot], peer2(c, j))

        def copy4(i, chunk):
            where = rows(base, chunk, length)
            return remote(out.at[where], out.at[where], ss4.at[p, i], r4.at[p, chunk], peer1(c, i))

        def copy5(chunk):
            where = rows(base, chunk, length)
            return remote(out.at[where], out.at[where], ss5.at[p, chunk], r5.at[p, chunk], sibling)

        def from_sibling(chunk):
            where = rows(far, chunk, half_rows // FIRST[1 - c])
            return remote(out.at[where], out.at[where], ss5.at[p, chunk], r5.at[p, chunk], sibling)

        def loop(low, high, body):
            def run(n, carry):
                body(n)
                return carry

            lax.fori_loop(low, high, run, 0)

        def send_pair():
            begin = ((rank1(1 - c) + 1) % FIRST[1 - c]) * (PARTS // FIRST[1 - c])
            loop(0, PARTS, lambda n: copy0((begin + n) % PARTS).start())

        def both(k):
            copy0(k).wait_recv()
            mine = src[rows(base, k, step), :].astype(jnp.float32)
            return mine + b0[rows(0, k, step), :].astype(jnp.float32)

        def send_first():
            def one(n):
                i = (here1 + n) % first
                for e in range(parts):
                    k = i * parts + e
                    hs[rows(0, k, step), :] = both(k).astype(jnp.bfloat16)
                copy1(i, here1).start()

            loop(1, first, one)
            for e in range(parts):
                own = both(here1 * parts + e)
                s1[e * pieces : (e + 1) * pieces] = own.reshape(pieces, piece, 128)

        def send_second():
            def one(n):
                i = (here1 + first - n) % first
                copy1(i, i).wait_recv()
                more = b1[rows(0, i, length), :].astype(jnp.float32)
                s1[0:second] += more.reshape(second, piece, 128)

            loop(1, first, one)
            h2[0:second] = s1[0:second].astype(jnp.bfloat16)
            loop(1, second, lambda n: copy2((here2 + n) % second, here2).start())

        def send_third():
            def one(n, sum_so_far):
                j = (here2 + second - n) % second
                copy2(j, j).wait_recv()
                return sum_so_far + b2[j].astype(jnp.float32)

            b3[here2] = lax.fori_loop(1, second, one, s1[here2]).astype(jnp.bfloat16)
            loop(1, second, lambda n: copy3((here2 + n) % second, here2).start())

        def send_fourth():
            def one(n):
                j = (here2 + second - n) % second
                copy3(j, j).wait_recv()

            loop(1, second, one)
            whole = b3[0:second].astype(jnp.float32).reshape(length, 128)
            out[rows(base, here1, length), :] = whole.astype(jnp.bfloat16)
            loop(1, first, lambda n: copy4((here1 + n) % first, here1).start())
            copy5(here1).start()

        def send_fifth():
            def one(n):
                i = (here1 + first - n) % first
                copy4(i, i).wait_recv()
                copy5(i).start()

            loop(1, first, one)

        def end():
            loop(0, FIRST[1 - c], lambda n: from_sibling(n).wait_recv())
            loop(0, PARTS, lambda n: copy0(n).wait_send())

            def one(n):
                i = (here1 + n) % first
                copy1(i, here1).wait_send()
                copy4(i, here1).wait_send()
                copy5(i).wait_send()

            loop(1, first, one)
            copy5(here1).wait_send()

            def two(n):
                j = (here2 + n) % second
                copy2(j, here2).wait_send()
                copy3(j, here2).wait_send()

            loop(1, second, two)

        return send_pair, send_first, send_second, send_third, send_fourth, send_fifth, end

    def sum_all(c):
        a, b = stages(c, 0), stages(c, 1)
        query_terms()
        a[0]()
        key_terms()
        b[0]()
        a[1]()
        b[1]()
        a[2]()
        b[2]()
        a[3]()
        token_grads()
        b[3]()
        a[4]()
        b[4]()
        a[5]()
        b[5]()
        a[6]()
        b[6]()

    for c in range(2):
        pl.when(core == c)(functools.partial(sum_all, c))

    @pl.when(is_worker == 1)
    def _():
        def finish(i, carry):
            halo_copy(i).wait_send()

            @pl.when(i != s)
            def _():
                query_copy(i).wait_send()

            return carry

        def finish_keys(i, carry):
            to = each * half + i

            @pl.when(to != s)
            def _():
                key_copy(to).wait_send()

            return carry

        lax.fori_loop(0, slots, finish, 0)
        lax.fori_loop(0, each, finish_keys, 0)
        pair_copy.wait_send()


def finish(res_q, res_kv, tokens, grad_out, w_qkv, slots, tm_size):
    hbm = pl.BlockSpec(memory_space=pltpu.HBM)
    vmem = pl.BlockSpec(memory_space=pltpu.VMEM)
    dma = pltpu.SemaphoreType.DMA
    sums = [
        [pltpu.VMEM((HALVES[p], 128), jnp.bfloat16)] * 3
        + [pltpu.VMEM((16, PIECES[p], 128), jnp.float32)]
        + [pltpu.VMEM((16, PIECES[p], 128), jnp.bfloat16)] * 3
        for p in range(2)
    ]
    return pl.pallas_call(
        functools.partial(finish_kernel, slots, tm_size),
        out_shape=(
            jax.ShapeDtypeStruct((LF * BP, D), jnp.bfloat16),
            jax.ShapeDtypeStruct((ROWS, 128), jnp.bfloat16),
        ),
        in_specs=[vmem, vmem] + [hbm] * 3,
        out_specs=(vmem, vmem),
        scratch_shapes=[
            pltpu.VMEM((2, HEADS, 2, BP, 128), jnp.bfloat16),
            pltpu.VMEM((HEADS, LF, BP, 128), jnp.bfloat16),
            pltpu.VMEM((2, HEADS, 2, BP, 128), jnp.bfloat16),
            pltpu.VMEM((slots // 2, LF, BP, 128), jnp.bfloat16),
            pltpu.VMEM((slots // 2, LF, BP, 128), jnp.bfloat16),
            pltpu.VMEM(tokens.shape, jnp.bfloat16),
            pltpu.VMEM(grad_out.shape, jnp.bfloat16),
            pltpu.VMEM(w_qkv.shape, jnp.bfloat16),
            pltpu.VMEM((LF * BP, 3 * HW), jnp.bfloat16),
            pltpu.VMEM((LF * BP, HW), jnp.bfloat16),
            pltpu.VMEM((ROWS, 128), jnp.bfloat16),
            *sums,
            dma((3,)), dma((2,)), dma((slots,)), dma((slots,)), dma((slots,)), dma, dma, dma,
            *[dma((2, size)) for size in (8, 8, 8, 8, 16, 16, 16, 16, 8, 8, 8, 8)],
        ],
        compiler_params=pltpu.CompilerParams(
            has_side_effects=True, collective_id=2, vmem_limit_bytes=32 << 20
        ),
        name="finish",
    )(res_q, res_kv, tokens, grad_out, w_qkv)


def widen_kernel(src, qkv, out):
    for i in range(9):
        start = D * i if i < 3 else KEYS_AT + D * (i - 3)
        qkv[:, 128 * i : 128 * (i + 1)] = src[start : start + D, :].astype(jnp.float32)
    for i in range(6):
        start = 3 * D + HW * i
        out[:, 128 * i : 128 * (i + 1)] = src[start : start + HW, :].astype(jnp.float32)


def widen(terms):
    vmem = pl.BlockSpec(memory_space=pltpu.VMEM)
    return pl.pallas_call(
        widen_kernel,
        out_shape=(
            jax.ShapeDtypeStruct((D, 3 * HW), jnp.float32),
            jax.ShapeDtypeStruct((HW, D), jnp.float32),
        ),
        in_specs=[vmem],
        out_specs=(vmem, vmem),
        compiler_params=pltpu.CompilerParams(vmem_limit_bytes=32 << 20),
        name="widen",
    )(terms)


def shards(tokens, grad_out, w_qkv, w_out, brain_mask, block_table):
    slots = lax.axis_size("space")
    tm_size = lax.axis_size("tm")
    flat_tokens = tokens.reshape(-1, D)
    flat_grad = grad_out.reshape(-1, D)
    held = spread(flat_tokens, flat_grad, w_qkv, w_out, slots, tm_size)
    res_q, res_kv = attend(block_table, brain_mask, held, tm_size)
    token_grads, terms = finish(res_q, res_kv, flat_tokens, flat_grad, w_qkv, slots, tm_size)
    qkv_grads, out_grads = widen(terms)
    return (token_grads.reshape(tokens.shape), qkv_grads, out_grads)


def solution(mesh):
    in_specs = (P("space", "tm", None, None), P("space", "tm", None, None), P(), P(), P(), P())
    out_specs = (P("space", "tm", None, None), P(), P())
    return jax.shard_map(shards, mesh=mesh, in_specs=in_specs, out_specs=out_specs, check_vma=False)
```

```python
import functools

import numpy as np
import jax
import jax.numpy as jnp
from jax import lax
from jax.experimental import pallas as pl
from jax.experimental.pallas import tpu as pltpu
from jax.sharding import PartitionSpec as P

D = 768
HEADS = 6
HD = 64
SIDE = 4
BP = 64
RAD_S = 3
RAD_T = 2
HW = HEADS * HD
LF = 4
KF = 6
KR = KF * BP
QR = 2 * BP
WORKERS = 2 * HEADS


def where_lane(low, high):
    lane = lax.broadcasted_iota(jnp.int32, low.shape, low.ndim - 1)
    return jnp.where(lane < HD, low, high)


MESH = pl.DeviceIdType.MESH


def worker_space(w):
    return w


def worker_of(space):
    return 1 - space // WORKERS, space


def signal(semaphore, space, tm):
    pl.semaphore_signal(semaphore, inc=1, device_id={"space": space, "tm": tm}, device_id_type=MESH)


def remote(src, dst, send, recv, device):
    return pltpu.make_async_remote_copy(
        src_ref=src, dst_ref=dst, send_sem=send, recv_sem=recv, device_id=device, device_id_type=MESH
    )


def spread_kernel(
    slots, tm_size, tok_hbm, gout_hbm, wqkv_hbm, wout_hbm, held,
    tok, gout, wqkv, wout, packed, lsem, ssem, hsem, rsem,
):
    me = lax.axis_index("space")
    t = lax.axis_index("tm")
    after = lax.rem(t + 1, tm_size)
    before = lax.rem(t + tm_size - 1, tm_size)
    is_worker, worker = worker_of(me)
    loads = [
        pltpu.make_async_copy(wqkv_hbm, wqkv, lsem.at[0]),
        pltpu.make_async_copy(tok_hbm, tok, lsem.at[1]),
        pltpu.make_async_copy(wout_hbm, wout, lsem.at[2]),
        pltpu.make_async_copy(gout_hbm, gout, lsem.at[3]),
    ]
    for load in loads:
        load.start()

    barrier = pltpu.get_barrier_semaphore()

    @pl.when(is_worker == 1)
    def _():
        half = worker % 2
        source = lax.rem(t + tm_size - 1 + 2 * half, tm_size)

        def greet(i, carry):
            signal(barrier, lax.rem(me + i, slots), t)
            return carry

        def greet_halo(i, carry):
            signal(barrier, i, source)
            return carry

        lax.fori_loop(1, slots, greet, 0)
        lax.fori_loop(0, slots, greet_halo, 0)

    for load in loads:
        load.wait()

    def pair(low, high):
        first = where_lane(low, pltpu.roll(high, HD, 1)).astype(jnp.bfloat16)
        second = where_lane(pltpu.roll(low, HD, 1), high).astype(jnp.bfloat16)
        return first.reshape(LF, BP, 128), second.reshape(LF, BP, 128)

    def main_refs(w):
        start = 2 - 2 * (w % 2)
        return packed.at[w // 2, pl.ds(start, 6)], held.at[me, pl.ds(start, 6)]

    def main_copy(w):
        src, dst = main_refs(w)
        return remote(src, dst, ssem.at[w], rsem, {"space": worker_space(w), "tm": t})

    def halo_copy(h, half):
        return remote(
            packed.at[h, pl.ds(4 - 2 * half, 2)], held.at[me, pl.ds(6 * half, 2)],
            hsem.at[2 * h + half], rsem,
            {"space": worker_space(2 * h + half), "tm": before if half else after},
        )

    for turn in range(HEADS // 2):
        i = (me // 2 + turn) % (HEADS // 2)

        def columns(start):
            return pl.ds(pl.multiple_of(start + 128 * i, 128), 128)

        def product(start):
            return jnp.dot(tok[...], wqkv[:, columns(start)], preferred_element_type=jnp.float32)

        gatt = lax.dot_general(
            gout[...], wout[columns(0), :], (((1,), (1,)), ((), ())),
            preferred_element_type=jnp.float32,
        )
        keys = pair(product(HW), product(2 * HW))
        queries = pair(product(0), gatt)
        for j in range(2):
            packed[2 * i + j, 0:2] = queries[j][2:4]
            packed[2 * i + j, 2:6] = keys[j]
            packed[2 * i + j, 6:8] = queries[j][0:2]
        if turn == 0:
            pl.semaphore_wait(barrier, 2 * WORKERS - is_worker)

        def send(k, carry):
            w = 4 * i + (k + me) % 4

            @pl.when(worker_space(w) != me)
            def _():
                main_copy(w).start()

            @pl.when(worker_space(w) == me)
            def _():
                src, dst = main_refs(w)
                pltpu.make_async_copy(src, dst, rsem).start()

            return carry

        for j in range(2):
            halo_copy(2 * i + j, 0).start()
            halo_copy(2 * i + j, 1).start()
        lax.fori_loop(0, 4, send, 0)

    def finish(w, carry):
        @pl.when(worker_space(w) != me)
        def _():
            main_copy(w).wait_send()

        return carry

    def finish_halo(h, carry):
        halo_copy(h, 0).wait_send()
        halo_copy(h, 1).wait_send()
        return carry

    @pl.when(is_worker == 1)
    def _():
        pltpu.make_async_copy(held, held, rsem).wait()

    lax.fori_loop(0, HEADS, finish_halo, 0)
    lax.fori_loop(0, WORKERS, finish, 0)


def spread(tokens, grad_out, w_qkv, w_out, slots, tm_size):
    hbm = pl.BlockSpec(memory_space=pltpu.HBM)
    return pl.pallas_call(
        functools.partial(spread_kernel, slots, tm_size),
        out_shape=jax.ShapeDtypeStruct((slots, 8, BP, 128), jnp.bfloat16),
        in_specs=[hbm] * 4,
        out_specs=hbm,
        scratch_shapes=[
            pltpu.VMEM(tokens.shape, jnp.bfloat16),
            pltpu.VMEM(grad_out.shape, jnp.bfloat16),
            pltpu.VMEM(w_qkv.shape, jnp.bfloat16),
            pltpu.VMEM(w_out.shape, jnp.bfloat16),
            pltpu.VMEM((HEADS, 8, BP, 128), jnp.bfloat16),
            pltpu.SemaphoreType.DMA((4,)),
            pltpu.SemaphoreType.DMA((WORKERS,)),
            pltpu.SemaphoreType.DMA((WORKERS,)),
            pltpu.SemaphoreType.DMA,
        ],
        compiler_params=pltpu.CompilerParams(
            has_side_effects=True, collective_id=1, vmem_limit_bytes=60 << 20
        ),
        name="spread",
    )(tokens, grad_out, w_qkv, w_out)


UNROLL = 12
MOST = 12
PAIRS = 72


def window_bias():
    patch = np.arange(BP)
    px, py = patch // 16, patch // 4 % 4
    out = np.full((10, KF, BP, 2, BP), -np.inf, np.float32)
    for n in range(9):
        dr, dc = n // 3 - 1, n % 3 - 1
        near_x = np.abs(px[:, None] + 4 * dr - px[None, :]) <= RAD_S
        near_y = np.abs(py[:, None] + 4 * dc - py[None, :]) <= RAD_S
        for j in range(KF):
            for i in range(2):
                near = near_x & near_y & (abs(j - RAD_T - i) <= RAD_T)
                out[n, j, :, i, :] = np.where(near, 0.0, -np.inf)
    return out.reshape(10, KR, QR)


def attend_kernel(
    tm_size, table, mask, held_hbm, bias_hbm, res_q, res_kv,
    held, kvt, bias, acc, scores, dots, rhs_a, rhs_d, total, inverse, delta, att, dq,
    slot_of, brain, pair_q, pair_k, pair_off, sem,
):
    me = lax.axis_index("space")
    t = lax.axis_index("tm")
    is_worker, worker = worker_of(me)
    half = worker % 2
    slots = held.shape[0]
    scaling = HD ** (-0.5)

    def keys_of(slot):
        return held[slot, pl.ds(2 * half, KF)].reshape(KR, 128)

    @pl.when(is_worker == 1)
    def _():
        loads = [
            pltpu.make_async_copy(held_hbm, held, sem.at[0]),
            pltpu.make_async_copy(bias_hbm, bias, sem.at[1]),
        ]
        for load in loads:
            load.start()

        def place(s, carry):
            slot_of[table[s]] = s
            return carry

        lax.fori_loop(0, slots, place, 0)

        def list_block(g, carry):
            blocks, pairs = carry

            def add(g, blocks, pairs):
                slot = slot_of[g]
                brain[blocks] = slot
                row = g // SIDE
                col = g % SIDE
                for n in range(9):
                    nr = row + (n // 3 - 1)
                    nc = col + (n % 3 - 1)
                    inside = (nr >= 0) & (nr < SIDE) & (nc >= 0) & (nc < SIDE)
                    nb = jnp.clip(nr, 0, SIDE - 1) * SIDE + jnp.clip(nc, 0, SIDE - 1)
                    valid = inside & (mask[nb] == 1)
                    pair_q[pairs] = slot
                    pair_k[pairs] = slot_of[nb]
                    pair_off[pairs] = n
                    pairs = jnp.minimum(pairs + valid.astype(jnp.int32), PAIRS)
                return (blocks + 1, pairs)

            return lax.cond(
                mask[g] == 1, functools.partial(add, g, blocks, pairs), lambda: (blocks, pairs)
            )

        blocks, pairs = lax.fori_loop(0, slots, list_block, (jnp.int32(0), jnp.int32(0)))
        for n in range(UNROLL):
            pair_q[pairs + n] = brain[0]
            pair_k[pairs + n] = brain[0]
            pair_off[pairs + n] = 9
        steps = (pairs + (UNROLL - 1)) // UNROLL

        acc[...] = jnp.zeros_like(acc)
        res_q[...] = jnp.zeros_like(res_q)
        total[...] = jnp.zeros_like(total)
        att[...] = jnp.zeros_like(att)
        dq[...] = jnp.zeros_like(dq)

        def prepare(b, carry):
            slot = brain[b]
            kvt[slot] = keys_of(slot).T
            rows = held[slot, pl.ds(6 - 6 * half, 2)].reshape(QR, 128)
            cols = rows.T
            zero = jnp.zeros_like(cols)
            first = lax.broadcasted_iota(jnp.int32, cols.shape, 0) < HD
            left = lax.broadcasted_iota(jnp.int32, cols.shape, 1) < HD
            rhs_a[slot, :, :QR] = jnp.where(first, cols * scaling, zero)
            rhs_a[slot, :, QR:] = jnp.where(first, zero, cols)
            rhs_d[slot, :QR, :] = jnp.where(left, rows, zero)
            rhs_d[slot, QR:, :] = jnp.where(left, zero, rows)
            return carry

        loads[0].wait()
        lax.fori_loop(0, blocks, prepare, 0)
        loads[1].wait()

        @pl.when((t == 0) & (half == 0))
        def _():
            bias[:, 0 : 2 * BP, :] = jnp.full((10, 2 * BP, QR), -jnp.inf, jnp.float32)

        @pl.when((t == tm_size - 1) & (half == 1))
        def _():
            bias[:, 4 * BP : 6 * BP, :] = jnp.full((10, 2 * BP, QR), -jnp.inf, jnp.float32)

        def by_rows(x):
            return x.reshape(KR // 8, 8, QR)

        def score(step, carry):
            for u in range(UNROLL):
                p = step * UNROLL + u
                keys = keys_of(pair_k[p])
                both = jnp.dot(keys, rhs_a[pair_q[p]], preferred_element_type=jnp.float32)
                e = jnp.exp(both[:, :QR] + bias[pair_off[p]])
                scores[p] = e
                dots[p] = both[:, QR:]
                total[pair_q[p]] += jnp.sum(by_rows(e), axis=0)
            return carry

        lax.fori_loop(0, steps, score, 0)

        def invert(b, carry):
            slot = brain[b]
            whole = jnp.sum(total[slot], axis=0, keepdims=True)
            inverse[slot] = jnp.broadcast_to(1.0 / whole, (8, QR))
            return carry

        lax.fori_loop(0, blocks, invert, 0)

        def weigh(step, carry):
            for u in range(UNROLL):
                p = step * UNROLL + u
                w = by_rows(scores[p]) * inverse[pair_q[p]][None]
                w = w.reshape(KR, QR).astype(jnp.bfloat16)
                att[pair_q[p]] += jnp.dot(
                    kvt[pair_k[p], HD:, :], w, preferred_element_type=jnp.float32
                )
            return carry

        lax.fori_loop(0, steps, weigh, 0)

        def rest(b, carry):
            slot = brain[b]
            rounded = att[slot].astype(jnp.bfloat16).astype(jnp.float32)
            att[slot] = rounded
            grad = rhs_a[slot, HD:, QR:].astype(jnp.float32)
            one = jnp.sum(grad * rounded, axis=0, keepdims=True)
            delta[slot] = jnp.broadcast_to(one, (8, QR))
            return carry

        lax.fori_loop(0, blocks, rest, 0)

        def spread_grad(step, carry):
            for u in range(UNROLL):
                p = step * UNROLL + u
                qs = pair_q[p]
                w = by_rows(scores[p]) * inverse[qs][None]
                ds = w * (by_rows(dots[p]) - delta[qs][None])
                ds = ds.reshape(KR, QR).astype(jnp.bfloat16)
                lhs = jnp.concatenate([ds, w.reshape(KR, QR).astype(jnp.bfloat16)], axis=1)
                acc[pair_k[p]] += jnp.dot(lhs, rhs_d[qs], preferred_element_type=jnp.float32)
                dq[qs] += jnp.dot(kvt[pair_k[p], :HD, :], ds, preferred_element_type=jnp.float32)
            return carry

        lax.fori_loop(0, steps, spread_grad, 0)

        def give(b, carry):
            slot = brain[b]
            both = jnp.concatenate([dq[slot] * scaling, att[slot]], axis=0).T
            res_q[slot] = both.astype(jnp.bfloat16).reshape(2, BP, 128)
            return carry

        lax.fori_loop(0, blocks, give, 0)

        def finish_keys(s, carry):
            whole = acc[s]
            res_kv[s] = where_lane(whole * scaling, whole).astype(jnp.bfloat16).reshape(KF, BP, 128)
            return carry

        lax.fori_loop(0, slots, finish_keys, 0)


def attend(block_table, brain_mask, held, tm_size):
    slots = held.shape[0]
    smem = pl.BlockSpec(memory_space=pltpu.SMEM)
    vmem = pl.BlockSpec(memory_space=pltpu.VMEM)
    hbm = pl.BlockSpec(memory_space=pltpu.HBM)
    store = (PAIRS + UNROLL, KR, QR)
    return pl.pallas_call(
        functools.partial(attend_kernel, tm_size),
        out_shape=(
            jax.ShapeDtypeStruct((slots, 2, BP, 128), jnp.bfloat16),
            jax.ShapeDtypeStruct((slots, KF, BP, 128), jnp.bfloat16),
        ),
        in_specs=[smem, smem, hbm, hbm],
        out_specs=(vmem, vmem),
        scratch_shapes=[
            pltpu.VMEM(held.shape, jnp.bfloat16),
            pltpu.VMEM((slots, 128, KR), jnp.bfloat16),
            pltpu.VMEM((10, KR, QR), jnp.float32),
            pltpu.VMEM((slots, KR, 128), jnp.float32),
            pltpu.VMEM(store, jnp.float32),
            pltpu.VMEM(store, jnp.float32),
            pltpu.VMEM((slots, 128, 2 * QR), jnp.bfloat16),
            pltpu.VMEM((slots, 2 * QR, 128), jnp.bfloat16),
            pltpu.VMEM((slots, 8, QR), jnp.float32),
            pltpu.VMEM((slots, 8, QR), jnp.float32),
            pltpu.VMEM((slots, 8, QR), jnp.float32),
            pltpu.VMEM((slots, HD, QR), jnp.float32),
            pltpu.VMEM((slots, HD, QR), jnp.float32),
            pltpu.SMEM((16,), jnp.int32),
            pltpu.SMEM((17,), jnp.int32),
            pltpu.SMEM((PAIRS + UNROLL,), jnp.int32),
            pltpu.SMEM((PAIRS + UNROLL,), jnp.int32),
            pltpu.SMEM((PAIRS + UNROLL,), jnp.int32),
            pltpu.SemaphoreType.DMA((2,)),
        ],
        compiler_params=pltpu.CompilerParams(vmem_limit_bytes=48 << 20),
        name="attend",
    )(block_table, brain_mask, held, jnp.asarray(window_bias()))


ROWS = 9216
KEYS_AT = 6 * D
STARTS = (0, 4096)
HALVES = (2048, 2560)
PIECES = (32, 40)
PARTS = 8
FIRST = (8, 4)
SECOND = (8, 16)


def finish_kernel(
    slots, tm_size, res_q, res_kv, tok_hbm, gout_hbm, wqkv_hbm, tg_ref, out,
    got_q, got_kv, got_halo, pair_in, summed, tok, gout, wqkv, grads, att, src, early, late,
    lsem, psem, cq, cs, ch, cqr, cr, crh, ss0, r0, ss1, r1, ss2, r2, ss3, r3, ss4, r4, ss5, r5,
):
    s = lax.axis_index("space")
    t = lax.axis_index("tm")
    core = s % 2
    chip = s // 2
    is_worker, worker = worker_of(s)
    head = worker // 2
    half = worker % 2
    other = lax.rem(t + tm_size + 2 * half - 1, tm_size)
    after = lax.rem(t + 1, tm_size)
    before = lax.rem(t + tm_size - 1, tm_size)
    sibling = {"space": s + 1 - 2 * core, "tm": t}

    def rank1(c):
        return t // 2 if c else chip

    def rank2(c):
        return 2 * chip + t % 2 if c else t

    def peer1(c, i):
        return {"space": s, "tm": 2 * i + t % 2} if c else {"space": 2 * i, "tm": t}

    def peer2(c, j):
        return {"space": 2 * (j // 2) + 1, "tm": 2 * (t // 2) + j % 2} if c else {"space": s, "tm": j}

    loads = [
        pltpu.make_async_copy(tok_hbm, tok, lsem.at[0]),
        pltpu.make_async_copy(gout_hbm, gout, lsem.at[1]),
        pltpu.make_async_copy(wqkv_hbm, wqkv, lsem.at[2]),
    ]
    for load in loads:
        load.start()

    barrier = pltpu.get_barrier_semaphore()

    def greet(i, carry):
        w = lax.rem(i + s, WORKERS)

        @pl.when(worker_space(w) != s)
        def _():
            signal(barrier, worker_space(w), t)

        signal(barrier, worker_space(w), (1 - w % 2) * after + (w % 2) * before)
        return carry

    lax.fori_loop(0, WORKERS, greet, 0)
    signal(barrier, sibling["space"], t)
    for c in range(2):

        @pl.when(core == c)
        def _(c=c):
            def greet1(n, carry):
                peer = peer1(c, (rank1(c) + n) % FIRST[c])
                signal(barrier, peer["space"], peer["tm"])
                return carry

            def greet2(n, carry):
                peer = peer2(c, (rank2(c) + n) % SECOND[c])
                signal(barrier, peer["space"], peer["tm"])
                return carry

            lax.fori_loop(1, FIRST[c], greet1, 0)
            lax.fori_loop(1, SECOND[c], greet2, 0)

    pl.semaphore_wait(barrier, is_worker * (2 * slots - 1) + 15 + 4 * core)

    each = slots // 2
    pair_copy = remote(
        res_kv.at[pl.ds(each * (1 - half), each), pl.ds(2 - 2 * half, 4)], pair_in,
        psem.at[0], psem.at[1], sibling,
    )

    def query_refs(i):
        return res_q.at[i], got_q.at[half, head]

    def key_refs(i):
        return summed.at[i % each], got_kv.at[head]

    def query_copy(i):
        a, b = query_refs(i)
        return remote(a, b, cq.at[i], cqr, {"space": i, "tm": t})

    def key_copy(i):
        a, b = key_refs(i)
        return remote(a, b, cs.at[i], cr, {"space": i, "tm": t})

    def halo_copy(i):
        return remote(
            res_kv.at[i, pl.ds(4 * half, 2)], got_halo.at[half, head], ch.at[i], crh,
            {"space": i, "tm": other},
        )

    @pl.when(is_worker == 1)
    def _():
        def send_queries(i, carry):
            to = lax.rem(i + s, slots)

            @pl.when(to != s)
            def _():
                query_copy(to).start()

            @pl.when(to == s)
            def _():
                a, b = query_refs(to)
                pltpu.make_async_copy(a, b, cqr).start()

            return carry

        def send_halo(i, carry):
            halo_copy(lax.rem(i + s, slots)).start()
            return carry

        def send_keys(i, carry):
            at = lax.rem(i + s, each)
            to = each * half + at
            mine = res_kv[to, pl.ds(2 - 2 * half, 4)].astype(jnp.float32)
            summed[at] = (mine + pair_in[at].astype(jnp.float32)).astype(jnp.bfloat16)

            @pl.when(to != s)
            def _():
                key_copy(to).start()

            @pl.when(to == s)
            def _():
                a, b = key_refs(to)
                pltpu.make_async_copy(a, b, cr).start()

            return carry

        pair_copy.start()
        lax.fori_loop(0, slots, send_queries, 0)
        lax.fori_loop(0, slots, send_halo, 0)
        pair_copy.wait_recv()
        lax.fori_loop(0, each, send_keys, 0)

    for load in loads:
        load.wait()
    tok_t = tok[...].T

    def pair(a, b):
        low = where_lane(a, pltpu.roll(b, HD, 1))
        high = where_lane(pltpu.roll(a, HD, 1), b)
        return low.astype(jnp.bfloat16), high.astype(jnp.bfloat16)

    def query_terms():
        pltpu.make_async_copy(got_q, got_q, cqr).wait()
        for i in range(HEADS // 2):
            at = 128 * i
            both = []
            for h in (2 * i, 2 * i + 1):
                rows = jnp.concatenate([got_q[0, h], got_q[1, h]], axis=0).astype(jnp.float32)
                both.append(rows.reshape(LF * BP, 128))
            dq, da = pair(*both)
            grads[:, at : at + 128] = dq
            att[:, at : at + 128] = da
            src[D * i : D * (i + 1), :] = jnp.dot(
                tok_t, dq, preferred_element_type=jnp.float32
            ).astype(jnp.bfloat16)
        att_t = att[...].T
        for i in range(6):
            start = 3 * D + HW * i
            src[start : start + HW, :] = jnp.dot(
                att_t, gout[:, 128 * i : 128 * (i + 1)], preferred_element_type=jnp.float32
            ).astype(jnp.bfloat16)

    def key_terms():
        pltpu.make_async_copy(got_halo, got_halo, crh).wait()
        pltpu.make_async_copy(got_kv, got_kv, cr).wait()
        for i in range(HEADS // 2):
            both = []
            for h in (2 * i, 2 * i + 1):
                edge = jnp.concatenate([got_halo[1, h], got_halo[0, h]], axis=0).astype(jnp.float32)
                both.append((got_kv[h].astype(jnp.float32) + edge).reshape(LF * BP, 128))
            for k, value in enumerate(pair(*both)):
                at = (1 + k) * HW + 128 * i
                grads[:, at : at + 128] = value
                start = KEYS_AT + D * (3 * k + i)
                src[start : start + D, :] = jnp.dot(
                    tok_t, value, preferred_element_type=jnp.float32
                ).astype(jnp.bfloat16)

    def token_grads():
        tg_ref[...] = lax.dot_general(
            grads[...], wqkv[...], (((1,), (1,)), ((), ())), preferred_element_type=jnp.float32
        ).astype(jnp.bfloat16)

    def stages(c, p):
        b0, hs, b1, s1, h2, b2, b3 = (early, late)[p]
        first, second = FIRST[c], SECOND[c]
        half_rows, piece = HALVES[p], PIECES[p]
        length = half_rows // first
        step = half_rows // PARTS
        parts = PARTS // first
        pieces = step // piece
        base = STARTS[p] + c * half_rows
        far = STARTS[p] + (1 - c) * half_rows
        here1, here2 = rank1(c), rank2(c)

        def rows(start, index, size):
            return pl.ds(pl.multiple_of(start + index * size, 64), size)

        def copy0(k):
            return remote(
                src.at[rows(far, k, step)], b0.at[rows(0, k, step)], ss0.at[p, k], r0.at[p, k], sibling
            )

        def copy1(i, slot):
            return remote(
                hs.at[rows(0, i, length)], b1.at[rows(0, slot, length)], ss1.at[p, i],
                r1.at[p, slot], peer1(c, i),
            )

        def copy2(j, slot):
            return remote(h2.at[j], b2.at[slot], ss2.at[p, j], r2.at[p, slot], peer2(c, j))

        def copy3(j, slot):
            return remote(b3.at[slot], b3.at[slot], ss3.at[p, j], r3.at[p, slot], peer2(c, j))

        def copy4(i, chunk):
            where = rows(base, chunk, length)
            return remote(out.at[where], out.at[where], ss4.at[p, i], r4.at[p, chunk], peer1(c, i))

        def copy5(chunk):
            where = rows(base, chunk, length)
            return remote(out.at[where], out.at[where], ss5.at[p, chunk], r5.at[p, chunk], sibling)

        def from_sibling(chunk):
            where = rows(far, chunk, half_rows // FIRST[1 - c])
            return remote(out.at[where], out.at[where], ss5.at[p, chunk], r5.at[p, chunk], sibling)

        def loop(low, high, body):
            def run(n, carry):
                body(n)
                return carry

            lax.fori_loop(low, high, run, 0)

        def send_pair():
            begin = ((rank1(1 - c) + 1) % FIRST[1 - c]) * (PARTS // FIRST[1 - c])
            loop(0, PARTS, lambda n: copy0((begin + n) % PARTS).start())

        def both(k):
            copy0(k).wait_recv()
            mine = src[rows(base, k, step), :].astype(jnp.float32)
            return mine + b0[rows(0, k, step), :].astype(jnp.float32)

        def send_first():
            def one(n):
                i = (here1 + n) % first
                for e in range(parts):
                    k = i * parts + e
                    hs[rows(0, k, step), :] = both(k).astype(jnp.bfloat16)
                copy1(i, here1).start()

            loop(1, first, one)
            for e in range(parts):
                own = both(here1 * parts + e)
                s1[e * pieces : (e + 1) * pieces] = own.reshape(pieces, piece, 128)

        def send_second():
            def one(n):
                i = (here1 + first - n) % first
                copy1(i, i).wait_recv()
                more = b1[rows(0, i, length), :].astype(jnp.float32)
                s1[0:second] += more.reshape(second, piece, 128)

            loop(1, first, one)
            h2[0:second] = s1[0:second].astype(jnp.bfloat16)
            loop(1, second, lambda n: copy2((here2 + n) % second, here2).start())

        def send_third():
            def one(n, sum_so_far):
                j = (here2 + second - n) % second
                copy2(j, j).wait_recv()
                return sum_so_far + b2[j].astype(jnp.float32)

            b3[here2] = lax.fori_loop(1, second, one, s1[here2]).astype(jnp.bfloat16)
            loop(1, second, lambda n: copy3((here2 + n) % second, here2).start())

        def send_fourth():
            def one(n):
                j = (here2 + second - n) % second
                copy3(j, j).wait_recv()

            loop(1, second, one)
            whole = b3[0:second].astype(jnp.float32).reshape(length, 128)
            out[rows(base, here1, length), :] = whole.astype(jnp.bfloat16)
            loop(1, first, lambda n: copy4((here1 + n) % first, here1).start())
            copy5(here1).start()

        def send_fifth():
            def one(n):
                i = (here1 + first - n) % first
                copy4(i, i).wait_recv()
                copy5(i).start()

            loop(1, first, one)

        def end():
            loop(0, FIRST[1 - c], lambda n: from_sibling(n).wait_recv())
            loop(0, PARTS, lambda n: copy0(n).wait_send())

            def one(n):
                i = (here1 + n) % first
                copy1(i, here1).wait_send()
                copy4(i, here1).wait_send()
                copy5(i).wait_send()

            loop(1, first, one)
            copy5(here1).wait_send()

            def two(n):
                j = (here2 + n) % second
                copy2(j, here2).wait_send()
                copy3(j, here2).wait_send()

            loop(1, second, two)

        return send_pair, send_first, send_second, send_third, send_fourth, send_fifth, end

    def sum_all(c):
        a, b = stages(c, 0), stages(c, 1)
        query_terms()
        a[0]()
        key_terms()
        b[0]()
        a[1]()
        b[1]()
        a[2]()
        b[2]()
        a[3]()
        token_grads()
        b[3]()
        a[4]()
        b[4]()
        a[5]()
        b[5]()
        a[6]()
        b[6]()

    for c in range(2):
        pl.when(core == c)(functools.partial(sum_all, c))

    @pl.when(is_worker == 1)
    def _():
        def finish(i, carry):
            halo_copy(i).wait_send()

            @pl.when(i != s)
            def _():
                query_copy(i).wait_send()

            return carry

        def finish_keys(i, carry):
            to = each * half + i

            @pl.when(to != s)
            def _():
                key_copy(to).wait_send()

            return carry

        lax.fori_loop(0, slots, finish, 0)
        lax.fori_loop(0, each, finish_keys, 0)
        pair_copy.wait_send()


def finish(res_q, res_kv, tokens, grad_out, w_qkv, slots, tm_size):
    hbm = pl.BlockSpec(memory_space=pltpu.HBM)
    vmem = pl.BlockSpec(memory_space=pltpu.VMEM)
    dma = pltpu.SemaphoreType.DMA
    sums = [
        [pltpu.VMEM((HALVES[p], 128), jnp.bfloat16)] * 3
        + [pltpu.VMEM((16, PIECES[p], 128), jnp.float32)]
        + [pltpu.VMEM((16, PIECES[p], 128), jnp.bfloat16)] * 3
        for p in range(2)
    ]
    return pl.pallas_call(
        functools.partial(finish_kernel, slots, tm_size),
        out_shape=(
            jax.ShapeDtypeStruct((LF * BP, D), jnp.bfloat16),
            jax.ShapeDtypeStruct((ROWS, 128), jnp.bfloat16),
        ),
        in_specs=[vmem, vmem] + [hbm] * 3,
        out_specs=(vmem, vmem),
        scratch_shapes=[
            pltpu.VMEM((2, HEADS, 2, BP, 128), jnp.bfloat16),
            pltpu.VMEM((HEADS, LF, BP, 128), jnp.bfloat16),
            pltpu.VMEM((2, HEADS, 2, BP, 128), jnp.bfloat16),
            pltpu.VMEM((slots // 2, LF, BP, 128), jnp.bfloat16),
            pltpu.VMEM((slots // 2, LF, BP, 128), jnp.bfloat16),
            pltpu.VMEM(tokens.shape, jnp.bfloat16),
            pltpu.VMEM(grad_out.shape, jnp.bfloat16),
            pltpu.VMEM(w_qkv.shape, jnp.bfloat16),
            pltpu.VMEM((LF * BP, 3 * HW), jnp.bfloat16),
            pltpu.VMEM((LF * BP, HW), jnp.bfloat16),
            pltpu.VMEM((ROWS, 128), jnp.bfloat16),
            *sums,
            dma((3,)), dma((2,)), dma((slots,)), dma((slots,)), dma((slots,)), dma, dma, dma,
            *[dma((2, size)) for size in (8, 8, 8, 8, 16, 16, 16, 16, 8, 8, 8, 8)],
        ],
        compiler_params=pltpu.CompilerParams(
            has_side_effects=True, collective_id=2, vmem_limit_bytes=32 << 20
        ),
        name="finish",
    )(res_q, res_kv, tokens, grad_out, w_qkv)


def widen_kernel(src, tg, qkv, out, tg_out, wide, wide_out, sem):
    step = 96
    copies = [pltpu.make_async_copy(tg, tg_out, sem.at[0])]
    copies[0].start()
    for k in range(D // step):
        rows = pl.ds(step * k, step)
        for i in range(9):
            start = D * i if i < 3 else KEYS_AT + D * (i - 3)
            part = src[start + step * k : start + step * (k + 1), :]
            wide[rows, 128 * i : 128 * (i + 1)] = part.astype(jnp.float32)
        copies.append(pltpu.make_async_copy(wide.at[rows], qkv.at[rows], sem.at[len(copies)]))
        copies[-1].start()
    for k in range(HW // step):
        rows = pl.ds(step * k, step)
        for i in range(6):
            start = 3 * D + HW * i
            part = src[start + step * k : start + step * (k + 1), :]
            wide_out[rows, 128 * i : 128 * (i + 1)] = part.astype(jnp.float32)
        copies.append(pltpu.make_async_copy(wide_out.at[rows], out.at[rows], sem.at[len(copies)]))
        copies[-1].start()
    for copy in copies:
        copy.wait()


def widen(terms, token_grads):
    vmem = pl.BlockSpec(memory_space=pltpu.VMEM)
    hbm = pl.BlockSpec(memory_space=pltpu.HBM)
    return pl.pallas_call(
        widen_kernel,
        out_shape=(
            jax.ShapeDtypeStruct((D, 3 * HW), jnp.float32),
            jax.ShapeDtypeStruct((HW, D), jnp.float32),
            jax.ShapeDtypeStruct(token_grads.shape, jnp.bfloat16),
        ),
        in_specs=[vmem, vmem],
        out_specs=(hbm, hbm, hbm),
        scratch_shapes=[
            pltpu.VMEM((D, 3 * HW), jnp.float32),
            pltpu.VMEM((HW, D), jnp.float32),
            pltpu.SemaphoreType.DMA((1 + (D + HW) // 96,)),
        ],
        compiler_params=pltpu.CompilerParams(vmem_limit_bytes=32 << 20),
        name="widen",
    )(terms, token_grads)


def shards(tokens, grad_out, w_qkv, w_out, brain_mask, block_table):
    slots = lax.axis_size("space")
    tm_size = lax.axis_size("tm")
    flat_tokens = tokens.reshape(-1, D)
    flat_grad = grad_out.reshape(-1, D)
    held = spread(flat_tokens, flat_grad, w_qkv, w_out, slots, tm_size)
    res_q, res_kv = attend(block_table, brain_mask, held, tm_size)
    token_grads, terms = finish(res_q, res_kv, flat_tokens, flat_grad, w_qkv, slots, tm_size)
    qkv_grads, out_grads, token_grads = widen(terms, token_grads)
    return (token_grads.reshape(tokens.shape), qkv_grads, out_grads)


def solution(mesh):
    in_specs = (P("space", "tm", None, None), P("space", "tm", None, None), P(), P(), P(), P())
    out_specs = (P("space", "tm", None, None), P(), P())
    return jax.shard_map(shards, mesh=mesh, in_specs=in_specs, out_specs=out_specs, check_vma=False)
```

```python
import functools

import numpy as np
import jax
import jax.numpy as jnp
from jax import lax
from jax.experimental import pallas as pl
from jax.experimental.pallas import tpu as pltpu
from jax.sharding import PartitionSpec as P

D = 768
HEADS = 6
HD = 64
SIDE = 4
BP = 64
RAD_S = 3
RAD_T = 2
HW = HEADS * HD
LF = 4
KF = 6
KR = KF * BP
QR = 2 * BP
WORKERS = 2 * HEADS


def where_lane(low, high):
    lane = lax.broadcasted_iota(jnp.int32, low.shape, low.ndim - 1)
    return jnp.where(lane < HD, low, high)


MESH = pl.DeviceIdType.MESH


def worker_space(w):
    return w


def worker_of(space):
    return 1 - space // WORKERS, space


def signal(semaphore, space, tm):
    pl.semaphore_signal(semaphore, inc=1, device_id={"space": space, "tm": tm}, device_id_type=MESH)


def remote(src, dst, send, recv, device):
    return pltpu.make_async_remote_copy(
        src_ref=src, dst_ref=dst, send_sem=send, recv_sem=recv, device_id=device, device_id_type=MESH
    )


def spread_kernel(
    slots, tm_size, tok_hbm, gout_hbm, wqkv_hbm, wout_hbm, held,
    tok, gout, wqkv, wout, packed, lsem, ssem, hsem, rsem,
):
    me = lax.axis_index("space")
    t = lax.axis_index("tm")
    after = lax.rem(t + 1, tm_size)
    before = lax.rem(t + tm_size - 1, tm_size)
    is_worker, worker = worker_of(me)
    loads = [
        pltpu.make_async_copy(wqkv_hbm, wqkv, lsem.at[0]),
        pltpu.make_async_copy(tok_hbm, tok, lsem.at[1]),
        pltpu.make_async_copy(wout_hbm, wout, lsem.at[2]),
        pltpu.make_async_copy(gout_hbm, gout, lsem.at[3]),
    ]
    for load in loads:
        load.start()

    barrier = pltpu.get_barrier_semaphore()

    @pl.when(is_worker == 1)
    def _():
        half = worker % 2
        source = lax.rem(t + tm_size - 1 + 2 * half, tm_size)

        def greet(i, carry):
            signal(barrier, lax.rem(me + i, slots), t)
            return carry

        def greet_halo(i, carry):
            signal(barrier, i, source)
            return carry

        lax.fori_loop(1, slots, greet, 0)
        lax.fori_loop(0, slots, greet_halo, 0)

    for load in loads:
        load.wait()

    def pair(low, high):
        first = where_lane(low, pltpu.roll(high, HD, 1)).astype(jnp.bfloat16)
        second = where_lane(pltpu.roll(low, HD, 1), high).astype(jnp.bfloat16)
        return first.reshape(LF, BP, 128), second.reshape(LF, BP, 128)

    def main_refs(w):
        start = 2 - 2 * (w % 2)
        return packed.at[w // 2, pl.ds(start, 6)], held.at[me, pl.ds(start, 6)]

    def main_copy(w):
        src, dst = main_refs(w)
        return remote(src, dst, ssem.at[w], rsem, {"space": worker_space(w), "tm": t})

    def halo_copy(h, half):
        return remote(
            packed.at[h, pl.ds(4 - 2 * half, 2)], held.at[me, pl.ds(6 * half, 2)],
            hsem.at[2 * h + half], rsem,
            {"space": worker_space(2 * h + half), "tm": before if half else after},
        )

    for turn in range(HEADS // 2):
        i = (me + t + turn) % (HEADS // 2)

        def columns(start):
            return pl.ds(pl.multiple_of(start + 128 * i, 128), 128)

        def product(start):
            return jnp.dot(tok[...], wqkv[:, columns(start)], preferred_element_type=jnp.float32)

        gatt = lax.dot_general(
            gout[...], wout[columns(0), :], (((1,), (1,)), ((), ())),
            preferred_element_type=jnp.float32,
        )
        keys = pair(product(HW), product(2 * HW))
        queries = pair(product(0), gatt)
        for j in range(2):
            packed[2 * i + j, 0:2] = queries[j][2:4]
            packed[2 * i + j, 2:6] = keys[j]
            packed[2 * i + j, 6:8] = queries[j][0:2]
        if turn == 0:
            pl.semaphore_wait(barrier, 2 * WORKERS - is_worker)

        def send(k, carry):
            w = 4 * i + (k + me) % 4

            @pl.when(worker_space(w) != me)
            def _():
                main_copy(w).start()

            @pl.when(worker_space(w) == me)
            def _():
                src, dst = main_refs(w)
                pltpu.make_async_copy(src, dst, rsem).start()

            return carry

        for j in range(2):
            halo_copy(2 * i + j, 0).start()
            halo_copy(2 * i + j, 1).start()
        lax.fori_loop(0, 4, send, 0)

    def finish(w, carry):
        @pl.when(worker_space(w) != me)
        def _():
            main_copy(w).wait_send()

        return carry

    def finish_halo(h, carry):
        halo_copy(h, 0).wait_send()
        halo_copy(h, 1).wait_send()
        return carry

    @pl.when(is_worker == 1)
    def _():
        pltpu.make_async_copy(held, held, rsem).wait()

    lax.fori_loop(0, HEADS, finish_halo, 0)
    lax.fori_loop(0, WORKERS, finish, 0)


def spread(tokens, grad_out, w_qkv, w_out, slots, tm_size):
    hbm = pl.BlockSpec(memory_space=pltpu.HBM)
    return pl.pallas_call(
        functools.partial(spread_kernel, slots, tm_size),
        out_shape=jax.ShapeDtypeStruct((slots, 8, BP, 128), jnp.bfloat16),
        in_specs=[hbm] * 4,
        out_specs=hbm,
        scratch_shapes=[
            pltpu.VMEM(tokens.shape, jnp.bfloat16),
            pltpu.VMEM(grad_out.shape, jnp.bfloat16),
            pltpu.VMEM(w_qkv.shape, jnp.bfloat16),
            pltpu.VMEM(w_out.shape, jnp.bfloat16),
            pltpu.VMEM((HEADS, 8, BP, 128), jnp.bfloat16),
            pltpu.SemaphoreType.DMA((4,)),
            pltpu.SemaphoreType.DMA((WORKERS,)),
            pltpu.SemaphoreType.DMA((WORKERS,)),
            pltpu.SemaphoreType.DMA,
        ],
        compiler_params=pltpu.CompilerParams(
            has_side_effects=True, collective_id=1, vmem_limit_bytes=60 << 20
        ),
        name="spread",
    )(tokens, grad_out, w_qkv, w_out)


UNROLL = 12
MOST = 12
PAIRS = 72


def window_bias():
    patch = np.arange(BP)
    px, py = patch // 16, patch // 4 % 4
    out = np.full((10, KF, BP, 2, BP), -np.inf, np.float32)
    for n in range(9):
        dr, dc = n // 3 - 1, n % 3 - 1
        near_x = np.abs(px[:, None] + 4 * dr - px[None, :]) <= RAD_S
        near_y = np.abs(py[:, None] + 4 * dc - py[None, :]) <= RAD_S
        for j in range(KF):
            for i in range(2):
                near = near_x & near_y & (abs(j - RAD_T - i) <= RAD_T)
                out[n, j, :, i, :] = np.where(near, 0.0, -np.inf)
    return out.reshape(10, KR, QR)


def attend_kernel(
    tm_size, table, mask, held_hbm, bias_hbm, res_q, res_kv,
    held, kvt, bias, acc, scores, dots, rhs_a, rhs_d, total, inverse, delta, att, dq,
    slot_of, brain, pair_q, pair_k, pair_off, sem,
):
    me = lax.axis_index("space")
    t = lax.axis_index("tm")
    is_worker, worker = worker_of(me)
    half = worker % 2
    slots = held.shape[0]
    scaling = HD ** (-0.5)

    def keys_of(slot):
        return held[slot, pl.ds(2 * half, KF)].reshape(KR, 128)

    @pl.when(is_worker == 1)
    def _():
        loads = [
            pltpu.make_async_copy(held_hbm, held, sem.at[0]),
            pltpu.make_async_copy(bias_hbm, bias, sem.at[1]),
        ]
        for load in loads:
            load.start()

        def place(s, carry):
            slot_of[table[s]] = s
            return carry

        lax.fori_loop(0, slots, place, 0)

        def list_block(g, carry):
            blocks, pairs = carry

            def add(g, blocks, pairs):
                slot = slot_of[g]
                brain[blocks] = slot
                row = g // SIDE
                col = g % SIDE
                for n in range(9):
                    nr = row + (n // 3 - 1)
                    nc = col + (n % 3 - 1)
                    inside = (nr >= 0) & (nr < SIDE) & (nc >= 0) & (nc < SIDE)
                    nb = jnp.clip(nr, 0, SIDE - 1) * SIDE + jnp.clip(nc, 0, SIDE - 1)
                    valid = inside & (mask[nb] == 1)
                    pair_q[pairs] = slot
                    pair_k[pairs] = slot_of[nb]
                    pair_off[pairs] = n
                    pairs = jnp.minimum(pairs + valid.astype(jnp.int32), PAIRS)
                return (blocks + 1, pairs)

            return lax.cond(
                mask[g] == 1, functools.partial(add, g, blocks, pairs), lambda: (blocks, pairs)
            )

        blocks, pairs = lax.fori_loop(0, slots, list_block, (jnp.int32(0), jnp.int32(0)))
        for n in range(UNROLL):
            pair_q[pairs + n] = brain[0]
            pair_k[pairs + n] = brain[0]
            pair_off[pairs + n] = 9
        steps = (pairs + (UNROLL - 1)) // UNROLL

        acc[...] = jnp.zeros_like(acc)
        res_q[...] = jnp.zeros_like(res_q)
        total[...] = jnp.zeros_like(total)
        att[...] = jnp.zeros_like(att)
        dq[...] = jnp.zeros_like(dq)

        def prepare(b, carry):
            slot = brain[b]
            kvt[slot] = keys_of(slot).T
            rows = held[slot, pl.ds(6 - 6 * half, 2)].reshape(QR, 128)
            cols = rows.T
            zero = jnp.zeros_like(cols)
            first = lax.broadcasted_iota(jnp.int32, cols.shape, 0) < HD
            left = lax.broadcasted_iota(jnp.int32, cols.shape, 1) < HD
            rhs_a[slot, :, :QR] = jnp.where(first, cols * scaling, zero)
            rhs_a[slot, :, QR:] = jnp.where(first, zero, cols)
            rhs_d[slot, :QR, :] = jnp.where(left, rows, zero)
            rhs_d[slot, QR:, :] = jnp.where(left, zero, rows)
            return carry

        loads[0].wait()
        lax.fori_loop(0, blocks, prepare, 0)
        loads[1].wait()

        @pl.when((t == 0) & (half == 0))
        def _():
            bias[:, 0 : 2 * BP, :] = jnp.full((10, 2 * BP, QR), -jnp.inf, jnp.float32)

        @pl.when((t == tm_size - 1) & (half == 1))
        def _():
            bias[:, 4 * BP : 6 * BP, :] = jnp.full((10, 2 * BP, QR), -jnp.inf, jnp.float32)

        def by_rows(x):
            return x.reshape(KR // 8, 8, QR)

        def score(step, carry):
            for u in range(UNROLL):
                p = step * UNROLL + u
                keys = keys_of(pair_k[p])
                both = jnp.dot(keys, rhs_a[pair_q[p]], preferred_element_type=jnp.float32)
                e = jnp.exp(both[:, :QR] + bias[pair_off[p]])
                scores[p] = e
                dots[p] = both[:, QR:]
                total[pair_q[p]] += jnp.sum(by_rows(e), axis=0)
            return carry

        lax.fori_loop(0, steps, score, 0)

        def invert(b, carry):
            slot = brain[b]
            whole = jnp.sum(total[slot], axis=0, keepdims=True)
            inverse[slot] = jnp.broadcast_to(1.0 / whole, (8, QR))
            return carry

        lax.fori_loop(0, blocks, invert, 0)

        def weigh(step, carry):
            for u in range(UNROLL):
                p = step * UNROLL + u
                w = by_rows(scores[p]) * inverse[pair_q[p]][None]
                w = w.reshape(KR, QR).astype(jnp.bfloat16)
                att[pair_q[p]] += jnp.dot(
                    kvt[pair_k[p], HD:, :], w, preferred_element_type=jnp.float32
                )
            return carry

        lax.fori_loop(0, steps, weigh, 0)

        def rest(b, carry):
            slot = brain[b]
            rounded = att[slot].astype(jnp.bfloat16).astype(jnp.float32)
            att[slot] = rounded
            grad = rhs_a[slot, HD:, QR:].astype(jnp.float32)
            one = jnp.sum(grad * rounded, axis=0, keepdims=True)
            delta[slot] = jnp.broadcast_to(one, (8, QR))
            return carry

        lax.fori_loop(0, blocks, rest, 0)

        def spread_grad(step, carry):
            for u in range(UNROLL):
                p = step * UNROLL + u
                qs = pair_q[p]
                w = by_rows(scores[p]) * inverse[qs][None]
                ds = w * (by_rows(dots[p]) - delta[qs][None])
                ds = ds.reshape(KR, QR).astype(jnp.bfloat16)
                lhs = jnp.concatenate([ds, w.reshape(KR, QR).astype(jnp.bfloat16)], axis=1)
                acc[pair_k[p]] += jnp.dot(lhs, rhs_d[qs], preferred_element_type=jnp.float32)
                dq[qs] += jnp.dot(kvt[pair_k[p], :HD, :], ds, preferred_element_type=jnp.float32)
            return carry

        lax.fori_loop(0, steps, spread_grad, 0)

        def give(b, carry):
            slot = brain[b]
            both = jnp.concatenate([dq[slot] * scaling, att[slot]], axis=0).T
            res_q[slot] = both.astype(jnp.bfloat16).reshape(2, BP, 128)
            return carry

        lax.fori_loop(0, blocks, give, 0)

        def finish_keys(s, carry):
            whole = acc[s]
            res_kv[s] = where_lane(whole * scaling, whole).astype(jnp.bfloat16).reshape(KF, BP, 128)
            return carry

        lax.fori_loop(0, slots, finish_keys, 0)


def attend(block_table, brain_mask, held, tm_size):
    slots = held.shape[0]
    smem = pl.BlockSpec(memory_space=pltpu.SMEM)
    vmem = pl.BlockSpec(memory_space=pltpu.VMEM)
    hbm = pl.BlockSpec(memory_space=pltpu.HBM)
    store = (PAIRS + UNROLL, KR, QR)
    return pl.pallas_call(
        functools.partial(attend_kernel, tm_size),
        out_shape=(
            jax.ShapeDtypeStruct((slots, 2, BP, 128), jnp.bfloat16),
            jax.ShapeDtypeStruct((slots, KF, BP, 128), jnp.bfloat16),
        ),
        in_specs=[smem, smem, hbm, hbm],
        out_specs=(vmem, vmem),
        scratch_shapes=[
            pltpu.VMEM(held.shape, jnp.bfloat16),
            pltpu.VMEM((slots, 128, KR), jnp.bfloat16),
            pltpu.VMEM((10, KR, QR), jnp.float32),
            pltpu.VMEM((slots, KR, 128), jnp.float32),
            pltpu.VMEM(store, jnp.float32),
            pltpu.VMEM(store, jnp.float32),
            pltpu.VMEM((slots, 128, 2 * QR), jnp.bfloat16),
            pltpu.VMEM((slots, 2 * QR, 128), jnp.bfloat16),
            pltpu.VMEM((slots, 8, QR), jnp.float32),
            pltpu.VMEM((slots, 8, QR), jnp.float32),
            pltpu.VMEM((slots, 8, QR), jnp.float32),
            pltpu.VMEM((slots, HD, QR), jnp.float32),
            pltpu.VMEM((slots, HD, QR), jnp.float32),
            pltpu.SMEM((16,), jnp.int32),
            pltpu.SMEM((17,), jnp.int32),
            pltpu.SMEM((PAIRS + UNROLL,), jnp.int32),
            pltpu.SMEM((PAIRS + UNROLL,), jnp.int32),
            pltpu.SMEM((PAIRS + UNROLL,), jnp.int32),
            pltpu.SemaphoreType.DMA((2,)),
        ],
        compiler_params=pltpu.CompilerParams(vmem_limit_bytes=51 << 20),
        name="attend",
    )(block_table, brain_mask, held, jnp.asarray(window_bias()))


ROWS = 9216
KEYS_AT = 6 * D
STARTS = (0, 4096)
HALVES = (2048, 2560)
PIECES = (32, 40)
PARTS = 8
FIRST = (8, 4)
SECOND = (8, 16)


def finish_kernel(
    slots, tm_size, res_q, res_kv, tok_hbm, gout_hbm, wqkv_hbm, tg_ref, out,
    got_q, got_kv, got_halo, pair_in, summed, tok, gout, wqkv, grads, att, src, early, late,
    lsem, psem, cq, cs, ch, cqr, cr, crh, ss0, r0, ss1, r1, ss2, r2, ss3, r3, ss4, r4, ss5, r5,
):
    s = lax.axis_index("space")
    t = lax.axis_index("tm")
    core = s % 2
    chip = s // 2
    is_worker, worker = worker_of(s)
    head = worker // 2
    half = worker % 2
    other = lax.rem(t + tm_size + 2 * half - 1, tm_size)
    after = lax.rem(t + 1, tm_size)
    before = lax.rem(t + tm_size - 1, tm_size)
    sibling = {"space": s + 1 - 2 * core, "tm": t}

    def rank1(c):
        return t // 2 if c else chip

    def rank2(c):
        return 2 * chip + t % 2 if c else t

    def peer1(c, i):
        return {"space": s, "tm": 2 * i + t % 2} if c else {"space": 2 * i, "tm": t}

    def peer2(c, j):
        return {"space": 2 * (j // 2) + 1, "tm": 2 * (t // 2) + j % 2} if c else {"space": s, "tm": j}

    loads = [
        pltpu.make_async_copy(tok_hbm, tok, lsem.at[0]),
        pltpu.make_async_copy(gout_hbm, gout, lsem.at[1]),
        pltpu.make_async_copy(wqkv_hbm, wqkv, lsem.at[2]),
    ]
    for load in loads:
        load.start()

    barrier = pltpu.get_barrier_semaphore()

    def greet(i, carry):
        w = lax.rem(i + s, WORKERS)

        @pl.when(worker_space(w) != s)
        def _():
            signal(barrier, worker_space(w), t)

        signal(barrier, worker_space(w), (1 - w % 2) * after + (w % 2) * before)
        return carry

    lax.fori_loop(0, WORKERS, greet, 0)
    signal(barrier, sibling["space"], t)
    for c in range(2):

        @pl.when(core == c)
        def _(c=c):
            def greet1(n, carry):
                peer = peer1(c, (rank1(c) + n) % FIRST[c])
                signal(barrier, peer["space"], peer["tm"])
                return carry

            def greet2(n, carry):
                peer = peer2(c, (rank2(c) + n) % SECOND[c])
                signal(barrier, peer["space"], peer["tm"])
                return carry

            lax.fori_loop(1, FIRST[c], greet1, 0)
            lax.fori_loop(1, SECOND[c], greet2, 0)

    pl.semaphore_wait(barrier, is_worker * (2 * slots - 1) + 15 + 4 * core)

    each = slots // 2
    pair_copy = remote(
        res_kv.at[pl.ds(each * (1 - half), each), pl.ds(2 - 2 * half, 4)], pair_in,
        psem.at[0], psem.at[1], sibling,
    )

    def query_refs(i):
        return res_q.at[i], got_q.at[half, head]

    def key_refs(i):
        return summed.at[i % each], got_kv.at[head]

    def query_copy(i):
        a, b = query_refs(i)
        return remote(a, b, cq.at[i], cqr, {"space": i, "tm": t})

    def key_copy(i):
        a, b = key_refs(i)
        return remote(a, b, cs.at[i], cr, {"space": i, "tm": t})

    def halo_copy(i):
        return remote(
            res_kv.at[i, pl.ds(4 * half, 2)], got_halo.at[half, head], ch.at[i], crh,
            {"space": i, "tm": other},
        )

    @pl.when(is_worker == 1)
    def _():
        def send_queries(i, carry):
            to = lax.rem(i + s, slots)

            @pl.when(to != s)
            def _():
                query_copy(to).start()

            @pl.when(to == s)
            def _():
                a, b = query_refs(to)
                pltpu.make_async_copy(a, b, cqr).start()

            return carry

        def send_halo(i, carry):
            halo_copy(lax.rem(i + s, slots)).start()
            return carry

        def send_keys(i, carry):
            at = lax.rem(i + s, each)
            to = each * half + at
            mine = res_kv[to, pl.ds(2 - 2 * half, 4)].astype(jnp.float32)
            summed[at] = (mine + pair_in[at].astype(jnp.float32)).astype(jnp.bfloat16)

            @pl.when(to != s)
            def _():
                key_copy(to).start()

            @pl.when(to == s)
            def _():
                a, b = key_refs(to)
                pltpu.make_async_copy(a, b, cr).start()

            return carry

        pair_copy.start()
        lax.fori_loop(0, slots, send_queries, 0)
        lax.fori_loop(0, slots, send_halo, 0)
        pair_copy.wait_recv()
        lax.fori_loop(0, each, send_keys, 0)

    for load in loads:
        load.wait()
    tok_t = tok[...].T

    def pair(a, b):
        low = where_lane(a, pltpu.roll(b, HD, 1))
        high = where_lane(pltpu.roll(a, HD, 1), b)
        return low.astype(jnp.bfloat16), high.astype(jnp.bfloat16)

    def query_terms():
        pltpu.make_async_copy(got_q, got_q, cqr).wait()
        for i in range(HEADS // 2):
            at = 128 * i
            both = []
            for h in (2 * i, 2 * i + 1):
                rows = jnp.concatenate([got_q[0, h], got_q[1, h]], axis=0).astype(jnp.float32)
                both.append(rows.reshape(LF * BP, 128))
            dq, da = pair(*both)
            grads[:, at : at + 128] = dq
            att[:, at : at + 128] = da
            src[D * i : D * (i + 1), :] = jnp.dot(
                tok_t, dq, preferred_element_type=jnp.float32
            ).astype(jnp.bfloat16)
        att_t = att[...].T
        for i in range(6):
            start = 3 * D + HW * i
            src[start : start + HW, :] = jnp.dot(
                att_t, gout[:, 128 * i : 128 * (i + 1)], preferred_element_type=jnp.float32
            ).astype(jnp.bfloat16)

    def key_terms():
        pltpu.make_async_copy(got_halo, got_halo, crh).wait()
        pltpu.make_async_copy(got_kv, got_kv, cr).wait()
        for i in range(HEADS // 2):
            both = []
            for h in (2 * i, 2 * i + 1):
                edge = jnp.concatenate([got_halo[1, h], got_halo[0, h]], axis=0).astype(jnp.float32)
                both.append((got_kv[h].astype(jnp.float32) + edge).reshape(LF * BP, 128))
            for k, value in enumerate(pair(*both)):
                at = (1 + k) * HW + 128 * i
                grads[:, at : at + 128] = value
                start = KEYS_AT + D * (3 * k + i)
                src[start : start + D, :] = jnp.dot(
                    tok_t, value, preferred_element_type=jnp.float32
                ).astype(jnp.bfloat16)

    def token_grads():
        tg_ref[...] = lax.dot_general(
            grads[...], wqkv[...], (((1,), (1,)), ((), ())), preferred_element_type=jnp.float32
        ).astype(jnp.bfloat16)

    def stages(c, p):
        b0, hs, b1, s1, h2, b2, b3 = (early, late)[p]
        first, second = FIRST[c], SECOND[c]
        half_rows, piece = HALVES[p], PIECES[p]
        length = half_rows // first
        step = half_rows // PARTS
        parts = PARTS // first
        pieces = step // piece
        base = STARTS[p] + c * half_rows
        far = STARTS[p] + (1 - c) * half_rows
        here1, here2 = rank1(c), rank2(c)

        def rows(start, index, size):
            return pl.ds(pl.multiple_of(start + index * size, 64), size)

        def copy0(k):
            return remote(
                src.at[rows(far, k, step)], b0.at[rows(0, k, step)], ss0.at[p, k], r0.at[p, k], sibling
            )

        def copy1(i, slot):
            return remote(
                hs.at[rows(0, i, length)], b1.at[rows(0, slot, length)], ss1.at[p, i],
                r1.at[p, slot], peer1(c, i),
            )

        def copy2(j, slot):
            return remote(h2.at[j], b2.at[slot], ss2.at[p, j], r2.at[p, slot], peer2(c, j))

        def copy3(j, slot):
            return remote(b3.at[slot], b3.at[slot], ss3.at[p, j], r3.at[p, slot], peer2(c, j))

        def copy4(i, chunk):
            where = rows(base, chunk, length)
            return remote(out.at[where], out.at[where], ss4.at[p, i], r4.at[p, chunk], peer1(c, i))

        def copy5(chunk):
            where = rows(base, chunk, length)
            return remote(out.at[where], out.at[where], ss5.at[p, chunk], r5.at[p, chunk], sibling)

        def from_sibling(chunk):
            where = rows(far, chunk, half_rows // FIRST[1 - c])
            return remote(out.at[where], out.at[where], ss5.at[p, chunk], r5.at[p, chunk], sibling)

        def loop(low, high, body):
            def run(n, carry):
                body(n)
                return carry

            lax.fori_loop(low, high, run, 0)

        def send_pair():
            begin = ((rank1(1 - c) + 1) % FIRST[1 - c]) * (PARTS // FIRST[1 - c])
            loop(0, PARTS, lambda n: copy0((begin + n) % PARTS).start())

        def both(k):
            copy0(k).wait_recv()
            mine = src[rows(base, k, step), :].astype(jnp.float32)
            return mine + b0[rows(0, k, step), :].astype(jnp.float32)

        def send_first():
            def one(n):
                i = (here1 + n) % first
                for e in range(parts):
                    k = i * parts + e
                    hs[rows(0, k, step), :] = both(k).astype(jnp.bfloat16)
                copy1(i, here1).start()

            loop(1, first, one)
            for e in range(parts):
                own = both(here1 * parts + e)
                s1[e * pieces : (e + 1) * pieces] = own.reshape(pieces, piece, 128)

        def send_second():
            def one(n):
                i = (here1 + first - n) % first
                copy1(i, i).wait_recv()
                more = b1[rows(0, i, length), :].astype(jnp.float32)
                s1[0:second] += more.reshape(second, piece, 128)

            loop(1, first, one)
            h2[0:second] = s1[0:second].astype(jnp.bfloat16)
            loop(1, second, lambda n: copy2((here2 + n) % second, here2).start())

        def send_third():
            def one(n, sum_so_far):
                j = (here2 + second - n) % second
                copy2(j, j).wait_recv()
                return sum_so_far + b2[j].astype(jnp.float32)

            b3[here2] = lax.fori_loop(1, second, one, s1[here2]).astype(jnp.bfloat16)
            loop(1, second, lambda n: copy3((here2 + n) % second, here2).start())

        def send_fourth():
            def one(n):
                j = (here2 + second - n) % second
                copy3(j, j).wait_recv()

            loop(1, second, one)
            whole = b3[0:second].astype(jnp.float32).reshape(length, 128)
            out[rows(base, here1, length), :] = whole.astype(jnp.bfloat16)
            loop(1, first, lambda n: copy4((here1 + n) % first, here1).start())
            copy5(here1).start()

        def send_fifth():
            def one(n):
                i = (here1 + first - n) % first
                copy4(i, i).wait_recv()
                copy5(i).start()

            loop(1, first, one)

        def end():
            loop(0, FIRST[1 - c], lambda n: from_sibling(n).wait_recv())
            loop(0, PARTS, lambda n: copy0(n).wait_send())

            def one(n):
                i = (here1 + n) % first
                copy1(i, here1).wait_send()
                copy4(i, here1).wait_send()
                copy5(i).wait_send()

            loop(1, first, one)
            copy5(here1).wait_send()

            def two(n):
                j = (here2 + n) % second
                copy2(j, here2).wait_send()
                copy3(j, here2).wait_send()

            loop(1, second, two)

        return send_pair, send_first, send_second, send_third, send_fourth, send_fifth, end

    def sum_all(c):
        a, b = stages(c, 0), stages(c, 1)
        query_terms()
        a[0]()
        key_terms()
        b[0]()
        a[1]()
        b[1]()
        a[2]()
        b[2]()
        a[3]()
        token_grads()
        b[3]()
        a[4]()
        b[4]()
        a[5]()
        b[5]()
        a[6]()
        b[6]()

    for c in range(2):
        pl.when(core == c)(functools.partial(sum_all, c))

    @pl.when(is_worker == 1)
    def _():
        def finish(i, carry):
            halo_copy(i).wait_send()

            @pl.when(i != s)
            def _():
                query_copy(i).wait_send()

            return carry

        def finish_keys(i, carry):
            to = each * half + i

            @pl.when(to != s)
            def _():
                key_copy(to).wait_send()

            return carry

        lax.fori_loop(0, slots, finish, 0)
        lax.fori_loop(0, each, finish_keys, 0)
        pair_copy.wait_send()


def finish(res_q, res_kv, tokens, grad_out, w_qkv, slots, tm_size):
    hbm = pl.BlockSpec(memory_space=pltpu.HBM)
    vmem = pl.BlockSpec(memory_space=pltpu.VMEM)
    dma = pltpu.SemaphoreType.DMA
    sums = [
        [pltpu.VMEM((HALVES[p], 128), jnp.bfloat16)] * 3
        + [pltpu.VMEM((16, PIECES[p], 128), jnp.float32)]
        + [pltpu.VMEM((16, PIECES[p], 128), jnp.bfloat16)] * 3
        for p in range(2)
    ]
    return pl.pallas_call(
        functools.partial(finish_kernel, slots, tm_size),
        out_shape=(
            jax.ShapeDtypeStruct((LF * BP, D), jnp.bfloat16),
            jax.ShapeDtypeStruct((ROWS, 128), jnp.bfloat16),
        ),
        in_specs=[vmem, vmem] + [hbm] * 3,
        out_specs=(vmem, vmem),
        scratch_shapes=[
            pltpu.VMEM((2, HEADS, 2, BP, 128), jnp.bfloat16),
            pltpu.VMEM((HEADS, LF, BP, 128), jnp.bfloat16),
            pltpu.VMEM((2, HEADS, 2, BP, 128), jnp.bfloat16),
            pltpu.VMEM((slots // 2, LF, BP, 128), jnp.bfloat16),
            pltpu.VMEM((slots // 2, LF, BP, 128), jnp.bfloat16),
            pltpu.VMEM(tokens.shape, jnp.bfloat16),
            pltpu.VMEM(grad_out.shape, jnp.bfloat16),
            pltpu.VMEM(w_qkv.shape, jnp.bfloat16),
            pltpu.VMEM((LF * BP, 3 * HW), jnp.bfloat16),
            pltpu.VMEM((LF * BP, HW), jnp.bfloat16),
            pltpu.VMEM((ROWS, 128), jnp.bfloat16),
            *sums,
            dma((3,)), dma((2,)), dma((slots,)), dma((slots,)), dma((slots,)), dma, dma, dma,
            *[dma((2, size)) for size in (8, 8, 8, 8, 16, 16, 16, 16, 8, 8, 8, 8)],
        ],
        compiler_params=pltpu.CompilerParams(
            has_side_effects=True, collective_id=2, vmem_limit_bytes=32 << 20
        ),
        name="finish",
    )(res_q, res_kv, tokens, grad_out, w_qkv)


def widen_kernel(src, tg, qkv, out, tg_out, wide, wide_out, sem):
    step = 96
    copies = [pltpu.make_async_copy(tg, tg_out, sem.at[0])]
    copies[0].start()
    for k in range(D // step):
        rows = pl.ds(step * k, step)
        for i in range(9):
            start = D * i if i < 3 else KEYS_AT + D * (i - 3)
            part = src[start + step * k : start + step * (k + 1), :]
            wide[rows, 128 * i : 128 * (i + 1)] = part.astype(jnp.float32)
        copies.append(pltpu.make_async_copy(wide.at[rows], qkv.at[rows], sem.at[len(copies)]))
        copies[-1].start()
    for k in range(HW // step):
        rows = pl.ds(step * k, step)
        for i in range(6):
            start = 3 * D + HW * i
            part = src[start + step * k : start + step * (k + 1), :]
            wide_out[rows, 128 * i : 128 * (i + 1)] = part.astype(jnp.float32)
        copies.append(pltpu.make_async_copy(wide_out.at[rows], out.at[rows], sem.at[len(copies)]))
        copies[-1].start()
    for copy in copies:
        copy.wait()


def widen(terms, token_grads):
    vmem = pl.BlockSpec(memory_space=pltpu.VMEM)
    hbm = pl.BlockSpec(memory_space=pltpu.HBM)
    return pl.pallas_call(
        widen_kernel,
        out_shape=(
            jax.ShapeDtypeStruct((D, 3 * HW), jnp.float32),
            jax.ShapeDtypeStruct((HW, D), jnp.float32),
            jax.ShapeDtypeStruct(token_grads.shape, jnp.bfloat16),
        ),
        in_specs=[vmem, vmem],
        out_specs=(hbm, hbm, hbm),
        scratch_shapes=[
            pltpu.VMEM((D, 3 * HW), jnp.float32),
            pltpu.VMEM((HW, D), jnp.float32),
            pltpu.SemaphoreType.DMA((1 + (D + HW) // 96,)),
        ],
        compiler_params=pltpu.CompilerParams(vmem_limit_bytes=32 << 20),
        name="widen",
    )(terms, token_grads)


def shards(tokens, grad_out, w_qkv, w_out, brain_mask, block_table):
    slots = lax.axis_size("space")
    tm_size = lax.axis_size("tm")
    flat_tokens = tokens.reshape(-1, D)
    flat_grad = grad_out.reshape(-1, D)
    held = spread(flat_tokens, flat_grad, w_qkv, w_out, slots, tm_size)
    res_q, res_kv = attend(block_table, brain_mask, held, tm_size)
    token_grads, terms = finish(res_q, res_kv, flat_tokens, flat_grad, w_qkv, slots, tm_size)
    qkv_grads, out_grads, token_grads = widen(terms, token_grads)
    return (token_grads.reshape(tokens.shape), qkv_grads, out_grads)


def solution(mesh):
    in_specs = (P("space", "tm", None, None), P("space", "tm", None, None), P(), P(), P(), P())
    out_specs = (P("space", "tm", None, None), P(), P())
    return jax.shard_map(shards, mesh=mesh, in_specs=in_specs, out_specs=out_specs, check_vma=False)
```

```python
import functools

import numpy as np
import jax
import jax.numpy as jnp
from jax import lax
from jax.experimental import pallas as pl
from jax.experimental.pallas import tpu as pltpu
from jax.sharding import PartitionSpec as P

D = 768
HEADS = 6
HD = 64
SIDE = 4
BP = 64
RAD_S = 3
RAD_T = 2
HW = HEADS * HD
LF = 4
KF = 6
KR = KF * BP
QR = 2 * BP
WORKERS = 2 * HEADS


def where_lane(low, high):
    lane = lax.broadcasted_iota(jnp.int32, low.shape, low.ndim - 1)
    return jnp.where(lane < HD, low, high)


MESH = pl.DeviceIdType.MESH


def worker_space(w):
    return w


def worker_of(space):
    return 1 - space // WORKERS, space


def signal(semaphore, space, tm):
    pl.semaphore_signal(semaphore, inc=1, device_id={"space": space, "tm": tm}, device_id_type=MESH)


def remote(src, dst, send, recv, device):
    return pltpu.make_async_remote_copy(
        src_ref=src, dst_ref=dst, send_sem=send, recv_sem=recv, device_id=device, device_id_type=MESH
    )


def spread_kernel(
    slots, tm_size, tok_hbm, gout_hbm, wqkv_hbm, wout_hbm, held,
    tok, gout, wqkv, wout, packed, lsem, ssem, hsem, rsem,
):
    me = lax.axis_index("space")
    t = lax.axis_index("tm")
    after = lax.rem(t + 1, tm_size)
    before = lax.rem(t + tm_size - 1, tm_size)
    is_worker, worker = worker_of(me)
    loads = [
        pltpu.make_async_copy(wqkv_hbm, wqkv, lsem.at[0]),
        pltpu.make_async_copy(tok_hbm, tok, lsem.at[1]),
        pltpu.make_async_copy(wout_hbm, wout, lsem.at[2]),
        pltpu.make_async_copy(gout_hbm, gout, lsem.at[3]),
    ]
    for load in loads:
        load.start()

    barrier = pltpu.get_barrier_semaphore()

    @pl.when(is_worker == 1)
    def _():
        half = worker % 2
        source = lax.rem(t + tm_size - 1 + 2 * half, tm_size)

        def greet(i, carry):
            signal(barrier, lax.rem(me + i, slots), t)
            return carry

        def greet_halo(i, carry):
            signal(barrier, i, source)
            return carry

        lax.fori_loop(1, slots, greet, 0)
        lax.fori_loop(0, slots, greet_halo, 0)

    for load in loads:
        load.wait()

    def pair(low, high):
        first = where_lane(low, pltpu.roll(high, HD, 1)).astype(jnp.bfloat16)
        second = where_lane(pltpu.roll(low, HD, 1), high).astype(jnp.bfloat16)
        return first.reshape(LF, BP, 128), second.reshape(LF, BP, 128)

    def main_refs(w):
        start = 2 - 2 * (w % 2)
        return packed.at[w // 2, pl.ds(start, 6)], held.at[me, pl.ds(start, 6)]

    def main_copy(w):
        src, dst = main_refs(w)
        return remote(src, dst, ssem.at[w], rsem, {"space": worker_space(w), "tm": t})

    def halo_copy(h, half):
        return remote(
            packed.at[h, pl.ds(4 - 2 * half, 2)], held.at[me, pl.ds(6 * half, 2)],
            hsem.at[2 * h + half], rsem,
            {"space": worker_space(2 * h + half), "tm": before if half else after},
        )

    for turn in range(HEADS // 2):
        i = (me + turn) % (HEADS // 2)

        def columns(start):
            return pl.ds(pl.multiple_of(start + 128 * i, 128), 128)

        def product(start):
            return jnp.dot(tok[...], wqkv[:, columns(start)], preferred_element_type=jnp.float32)

        gatt = lax.dot_general(
            gout[...], wout[columns(0), :], (((1,), (1,)), ((), ())),
            preferred_element_type=jnp.float32,
        )
        keys = pair(product(HW), product(2 * HW))
        queries = pair(product(0), gatt)
        for j in range(2):
            packed[2 * i + j, 0:2] = queries[j][2:4]
            packed[2 * i + j, 2:6] = keys[j]
            packed[2 * i + j, 6:8] = queries[j][0:2]
        if turn == 0:
            pl.semaphore_wait(barrier, 2 * WORKERS - is_worker)

        def send(k, carry):
            w = 4 * i + (k + me) % 4

            @pl.when(worker_space(w) != me)
            def _():
                main_copy(w).start()

            @pl.when(worker_space(w) == me)
            def _():
                src, dst = main_refs(w)
                pltpu.make_async_copy(src, dst, rsem).start()

            return carry

        for j in range(2):
            halo_copy(2 * i + j, 0).start()
            halo_copy(2 * i + j, 1).start()
        lax.fori_loop(0, 4, send, 0)

    def finish(w, carry):
        @pl.when(worker_space(w) != me)
        def _():
            main_copy(w).wait_send()

        return carry

    def finish_halo(h, carry):
        halo_copy(h, 0).wait_send()
        halo_copy(h, 1).wait_send()
        return carry

    @pl.when(is_worker == 1)
    def _():
        pltpu.make_async_copy(held, held, rsem).wait()

    lax.fori_loop(0, HEADS, finish_halo, 0)
    lax.fori_loop(0, WORKERS, finish, 0)


def spread(tokens, grad_out, w_qkv, w_out, slots, tm_size):
    hbm = pl.BlockSpec(memory_space=pltpu.HBM)
    return pl.pallas_call(
        functools.partial(spread_kernel, slots, tm_size),
        out_shape=jax.ShapeDtypeStruct((slots, 8, BP, 128), jnp.bfloat16),
        in_specs=[hbm] * 4,
        out_specs=hbm,
        scratch_shapes=[
            pltpu.VMEM(tokens.shape, jnp.bfloat16),
            pltpu.VMEM(grad_out.shape, jnp.bfloat16),
            pltpu.VMEM(w_qkv.shape, jnp.bfloat16),
            pltpu.VMEM(w_out.shape, jnp.bfloat16),
            pltpu.VMEM((HEADS, 8, BP, 128), jnp.bfloat16),
            pltpu.SemaphoreType.DMA((4,)),
            pltpu.SemaphoreType.DMA((WORKERS,)),
            pltpu.SemaphoreType.DMA((WORKERS,)),
            pltpu.SemaphoreType.DMA,
        ],
        compiler_params=pltpu.CompilerParams(
            has_side_effects=True, collective_id=1, vmem_limit_bytes=60 << 20
        ),
        name="spread",
    )(tokens, grad_out, w_qkv, w_out)


UNROLL = 12
MOST = 12
PAIRS = 72


def window_bias():
    patch = np.arange(BP)
    px, py = patch // 16, patch // 4 % 4
    out = np.full((10, KF, BP, 2, BP), -np.inf, np.float32)
    for n in range(9):
        dr, dc = n // 3 - 1, n % 3 - 1
        near_x = np.abs(px[:, None] + 4 * dr - px[None, :]) <= RAD_S
        near_y = np.abs(py[:, None] + 4 * dc - py[None, :]) <= RAD_S
        for j in range(KF):
            for i in range(2):
                near = near_x & near_y & (abs(j - RAD_T - i) <= RAD_T)
                out[n, j, :, i, :] = np.where(near, 0.0, -np.inf)
    return out.reshape(10, KR, QR)


def attend_kernel(
    tm_size, table, mask, held_hbm, bias_hbm, res_q, res_kv,
    held, kvt, bias, acc, scores, dots, rhs_a, rhs_d, total, inverse, delta, att, dq,
    slot_of, brain, pair_q, pair_k, pair_off, sem,
):
    me = lax.axis_index("space")
    t = lax.axis_index("tm")
    is_worker, worker = worker_of(me)
    half = worker % 2
    slots = held.shape[0]
    scaling = HD ** (-0.5)

    def keys_of(slot):
        return held[slot, pl.ds(2 * half, KF)].reshape(KR, 128)

    @pl.when(is_worker == 1)
    def _():
        loads = [
            pltpu.make_async_copy(held_hbm, held, sem.at[0]),
            pltpu.make_async_copy(bias_hbm, bias, sem.at[1]),
        ]
        for load in loads:
            load.start()

        def place(s, carry):
            slot_of[table[s]] = s
            return carry

        lax.fori_loop(0, slots, place, 0)

        def list_block(g, carry):
            blocks, pairs = carry

            def add(g, blocks, pairs):
                slot = slot_of[g]
                brain[blocks] = slot
                row = g // SIDE
                col = g % SIDE
                for n in range(9):
                    nr = row + (n // 3 - 1)
                    nc = col + (n % 3 - 1)
                    inside = (nr >= 0) & (nr < SIDE) & (nc >= 0) & (nc < SIDE)
                    nb = jnp.clip(nr, 0, SIDE - 1) * SIDE + jnp.clip(nc, 0, SIDE - 1)
                    valid = inside & (mask[nb] == 1)
                    pair_q[pairs] = slot
                    pair_k[pairs] = slot_of[nb]
                    pair_off[pairs] = n
                    pairs = jnp.minimum(pairs + valid.astype(jnp.int32), PAIRS)
                return (blocks + 1, pairs)

            return lax.cond(
                mask[g] == 1, functools.partial(add, g, blocks, pairs), lambda: (blocks, pairs)
            )

        blocks, pairs = lax.fori_loop(0, slots, list_block, (jnp.int32(0), jnp.int32(0)))
        for n in range(UNROLL):
            pair_q[pairs + n] = brain[0]
            pair_k[pairs + n] = brain[0]
            pair_off[pairs + n] = 9
        steps = (pairs + (UNROLL - 1)) // UNROLL

        acc[...] = jnp.zeros_like(acc)
        res_q[...] = jnp.zeros_like(res_q)
        total[...] = jnp.zeros_like(total)
        att[...] = jnp.zeros_like(att)
        dq[...] = jnp.zeros_like(dq)

        def prepare(b, carry):
            slot = brain[b]
            kvt[slot] = keys_of(slot).T
            rows = held[slot, pl.ds(6 - 6 * half, 2)].reshape(QR, 128)
            cols = rows.T
            zero = jnp.zeros_like(cols)
            first = lax.broadcasted_iota(jnp.int32, cols.shape, 0) < HD
            left = lax.broadcasted_iota(jnp.int32, cols.shape, 1) < HD
            rhs_a[slot, :, :QR] = jnp.where(first, cols * scaling, zero)
            rhs_a[slot, :, QR:] = jnp.where(first, zero, cols)
            rhs_d[slot, :QR, :] = jnp.where(left, rows, zero)
            rhs_d[slot, QR:, :] = jnp.where(left, zero, rows)
            return carry

        loads[0].wait()
        lax.fori_loop(0, blocks, prepare, 0)
        loads[1].wait()

        @pl.when((t == 0) & (half == 0))
        def _():
            bias[:, 0 : 2 * BP, :] = jnp.full((10, 2 * BP, QR), -jnp.inf, jnp.float32)

        @pl.when((t == tm_size - 1) & (half == 1))
        def _():
            bias[:, 4 * BP : 6 * BP, :] = jnp.full((10, 2 * BP, QR), -jnp.inf, jnp.float32)

        def by_rows(x):
            return x.reshape(KR // 8, 8, QR)

        def score(step, carry):
            for u in range(UNROLL):
                p = step * UNROLL + u
                keys = keys_of(pair_k[p])
                both = jnp.dot(keys, rhs_a[pair_q[p]], preferred_element_type=jnp.float32)
                e = jnp.exp(both[:, :QR] + bias[pair_off[p]])
                scores[p] = e
                dots[p] = both[:, QR:]
                total[pair_q[p]] += jnp.sum(by_rows(e), axis=0)
            return carry

        lax.fori_loop(0, steps, score, 0)

        def invert(b, carry):
            slot = brain[b]
            whole = jnp.sum(total[slot], axis=0, keepdims=True)
            inverse[slot] = jnp.broadcast_to(1.0 / whole, (8, QR))
            return carry

        lax.fori_loop(0, blocks, invert, 0)

        def weigh(step, carry):
            for u in range(UNROLL):
                p = step * UNROLL + u
                w = by_rows(scores[p]) * inverse[pair_q[p]][None]
                w = w.reshape(KR, QR).astype(jnp.bfloat16)
                att[pair_q[p]] += jnp.dot(
                    kvt[pair_k[p], HD:, :], w, preferred_element_type=jnp.float32
                )
            return carry

        lax.fori_loop(0, steps, weigh, 0)

        def rest(b, carry):
            slot = brain[b]
            rounded = att[slot].astype(jnp.bfloat16).astype(jnp.float32)
            att[slot] = rounded
            grad = rhs_a[slot, HD:, QR:].astype(jnp.float32)
            one = jnp.sum(grad * rounded, axis=0, keepdims=True)
            delta[slot] = jnp.broadcast_to(one, (8, QR))
            return carry

        lax.fori_loop(0, blocks, rest, 0)

        def spread_grad(step, carry):
            for u in range(UNROLL):
                p = step * UNROLL + u
                qs = pair_q[p]
                w = by_rows(scores[p]) * inverse[qs][None]
                ds = w * (by_rows(dots[p]) - delta[qs][None])
                ds = ds.reshape(KR, QR).astype(jnp.bfloat16)
                lhs = jnp.concatenate([ds, w.reshape(KR, QR).astype(jnp.bfloat16)], axis=1)
                acc[pair_k[p]] += jnp.dot(lhs, rhs_d[qs], preferred_element_type=jnp.float32)
                dq[qs] += jnp.dot(kvt[pair_k[p], :HD, :], ds, preferred_element_type=jnp.float32)
            return carry

        lax.fori_loop(0, steps, spread_grad, 0)

        def give(b, carry):
            slot = brain[b]
            both = jnp.concatenate([dq[slot] * scaling, att[slot]], axis=0).T
            res_q[slot] = both.astype(jnp.bfloat16).reshape(2, BP, 128)
            return carry

        lax.fori_loop(0, blocks, give, 0)

        def finish_keys(s, carry):
            whole = acc[s]
            res_kv[s] = where_lane(whole * scaling, whole).astype(jnp.bfloat16).reshape(KF, BP, 128)
            return carry

        lax.fori_loop(0, slots, finish_keys, 0)


def attend(block_table, brain_mask, held, tm_size):
    slots = held.shape[0]
    smem = pl.BlockSpec(memory_space=pltpu.SMEM)
    vmem = pl.BlockSpec(memory_space=pltpu.VMEM)
    hbm = pl.BlockSpec(memory_space=pltpu.HBM)
    store = (PAIRS + UNROLL, KR, QR)
    return pl.pallas_call(
        functools.partial(attend_kernel, tm_size),
        out_shape=(
            jax.ShapeDtypeStruct((slots, 2, BP, 128), jnp.bfloat16),
            jax.ShapeDtypeStruct((slots, KF, BP, 128), jnp.bfloat16),
        ),
        in_specs=[smem, smem, hbm, hbm],
        out_specs=(vmem, vmem),
        scratch_shapes=[
            pltpu.VMEM(held.shape, jnp.bfloat16),
            pltpu.VMEM((slots, 128, KR), jnp.bfloat16),
            pltpu.VMEM((10, KR, QR), jnp.float32),
            pltpu.VMEM((slots, KR, 128), jnp.float32),
            pltpu.VMEM(store, jnp.float32),
            pltpu.VMEM(store, jnp.float32),
            pltpu.VMEM((slots, 128, 2 * QR), jnp.bfloat16),
            pltpu.VMEM((slots, 2 * QR, 128), jnp.bfloat16),
            pltpu.VMEM((slots, 8, QR), jnp.float32),
            pltpu.VMEM((slots, 8, QR), jnp.float32),
            pltpu.VMEM((slots, 8, QR), jnp.float32),
            pltpu.VMEM((slots, HD, QR), jnp.float32),
            pltpu.VMEM((slots, HD, QR), jnp.float32),
            pltpu.SMEM((16,), jnp.int32),
            pltpu.SMEM((17,), jnp.int32),
            pltpu.SMEM((PAIRS + UNROLL,), jnp.int32),
            pltpu.SMEM((PAIRS + UNROLL,), jnp.int32),
            pltpu.SMEM((PAIRS + UNROLL,), jnp.int32),
            pltpu.SemaphoreType.DMA((2,)),
        ],
        compiler_params=pltpu.CompilerParams(vmem_limit_bytes=51 << 20),
        name="attend",
    )(block_table, brain_mask, held, jnp.asarray(window_bias()))


ROWS = 9216
KEYS_AT = 6 * D
STARTS = (0, 4096)
HALVES = (2048, 2560)
PIECES = (32, 40)
PARTS = 8
FIRST = (8, 4)
SECOND = (8, 16)


def finish_kernel(
    slots, tm_size, res_q, res_kv, tok_hbm, gout_hbm, wqkv_hbm, tg_ref, out,
    got_q, got_kv, got_halo, pair_in, summed, tok, gout, wqkv, grads, att, src, early, late,
    lsem, psem, cq, cs, ch, cqr, cr, crh, ss0, r0, ss1, r1, ss2, r2, ss3, r3, ss4, r4, ss5, r5,
):
    s = lax.axis_index("space")
    t = lax.axis_index("tm")
    core = s % 2
    chip = s // 2
    is_worker, worker = worker_of(s)
    head = worker // 2
    half = worker % 2
    other = lax.rem(t + tm_size + 2 * half - 1, tm_size)
    after = lax.rem(t + 1, tm_size)
    before = lax.rem(t + tm_size - 1, tm_size)
    sibling = {"space": s + 1 - 2 * core, "tm": t}

    def rank1(c):
        return t // 2 if c else chip

    def rank2(c):
        return 2 * chip + t % 2 if c else t

    def peer1(c, i):
        return {"space": s, "tm": 2 * i + t % 2} if c else {"space": 2 * i, "tm": t}

    def peer2(c, j):
        return {"space": 2 * (j // 2) + 1, "tm": 2 * (t // 2) + j % 2} if c else {"space": s, "tm": j}

    loads = [
        pltpu.make_async_copy(tok_hbm, tok, lsem.at[0]),
        pltpu.make_async_copy(gout_hbm, gout, lsem.at[1]),
        pltpu.make_async_copy(wqkv_hbm, wqkv, lsem.at[2]),
    ]
    for load in loads:
        load.start()

    barrier = pltpu.get_barrier_semaphore()

    def greet(i, carry):
        w = lax.rem(i + s, WORKERS)

        @pl.when(worker_space(w) != s)
        def _():
            signal(barrier, worker_space(w), t)

        signal(barrier, worker_space(w), (1 - w % 2) * after + (w % 2) * before)
        return carry

    lax.fori_loop(0, WORKERS, greet, 0)
    signal(barrier, sibling["space"], t)
    for c in range(2):

        @pl.when(core == c)
        def _(c=c):
            def greet1(n, carry):
                peer = peer1(c, (rank1(c) + n) % FIRST[c])
                signal(barrier, peer["space"], peer["tm"])
                return carry

            def greet2(n, carry):
                peer = peer2(c, (rank2(c) + n) % SECOND[c])
                signal(barrier, peer["space"], peer["tm"])
                return carry

            lax.fori_loop(1, FIRST[c], greet1, 0)
            lax.fori_loop(1, SECOND[c], greet2, 0)

    pl.semaphore_wait(barrier, is_worker * (2 * slots - 1) + 15 + 4 * core)

    each = slots // 2
    pair_copy = remote(
        res_kv.at[pl.ds(each * (1 - half), each), pl.ds(2 - 2 * half, 4)], pair_in,
        psem.at[0], psem.at[1], sibling,
    )

    def query_refs(i):
        return res_q.at[i], got_q.at[half, head]

    def key_refs(i):
        return summed.at[i % each], got_kv.at[head]

    def query_copy(i):
        a, b = query_refs(i)
        return remote(a, b, cq.at[i], cqr, {"space": i, "tm": t})

    def key_copy(i):
        a, b = key_refs(i)
        return remote(a, b, cs.at[i], cr, {"space": i, "tm": t})

    def halo_copy(i):
        return remote(
            res_kv.at[i, pl.ds(4 * half, 2)], got_halo.at[half, head], ch.at[i], crh,
            {"space": i, "tm": other},
        )

    @pl.when(is_worker == 1)
    def _():
        def send_queries(i, carry):
            to = lax.rem(i + s, slots)

            @pl.when(to != s)
            def _():
                query_copy(to).start()

            @pl.when(to == s)
            def _():
                a, b = query_refs(to)
                pltpu.make_async_copy(a, b, cqr).start()

            return carry

        def send_halo(i, carry):
            halo_copy(lax.rem(i + s, slots)).start()
            return carry

        def send_keys(i, carry):
            at = lax.rem(i + s, each)
            to = each * half + at
            mine = res_kv[to, pl.ds(2 - 2 * half, 4)].astype(jnp.float32)
            summed[at] = (mine + pair_in[at].astype(jnp.float32)).astype(jnp.bfloat16)

            @pl.when(to != s)
            def _():
                key_copy(to).start()

            @pl.when(to == s)
            def _():
                a, b = key_refs(to)
                pltpu.make_async_copy(a, b, cr).start()

            return carry

        pair_copy.start()
        lax.fori_loop(0, slots, send_queries, 0)
        lax.fori_loop(0, slots, send_halo, 0)
        pair_copy.wait_recv()
        lax.fori_loop(0, each, send_keys, 0)

    for load in loads:
        load.wait()
    tok_t = tok[...].T

    def pair(a, b):
        low = where_lane(a, pltpu.roll(b, HD, 1))
        high = where_lane(pltpu.roll(a, HD, 1), b)
        return low.astype(jnp.bfloat16), high.astype(jnp.bfloat16)

    def query_terms():
        pltpu.make_async_copy(got_q, got_q, cqr).wait()
        for i in range(HEADS // 2):
            at = 128 * i
            both = []
            for h in (2 * i, 2 * i + 1):
                rows = jnp.concatenate([got_q[0, h], got_q[1, h]], axis=0).astype(jnp.float32)
                both.append(rows.reshape(LF * BP, 128))
            dq, da = pair(*both)
            grads[:, at : at + 128] = dq
            att[:, at : at + 128] = da
            src[D * i : D * (i + 1), :] = jnp.dot(
                tok_t, dq, preferred_element_type=jnp.float32
            ).astype(jnp.bfloat16)
        att_t = att[...].T
        for i in range(6):
            start = 3 * D + HW * i
            src[start : start + HW, :] = jnp.dot(
                att_t, gout[:, 128 * i : 128 * (i + 1)], preferred_element_type=jnp.float32
            ).astype(jnp.bfloat16)

    def key_terms():
        pltpu.make_async_copy(got_halo, got_halo, crh).wait()
        pltpu.make_async_copy(got_kv, got_kv, cr).wait()
        for i in range(HEADS // 2):
            both = []
            for h in (2 * i, 2 * i + 1):
                edge = jnp.concatenate([got_halo[1, h], got_halo[0, h]], axis=0).astype(jnp.float32)
                both.append((got_kv[h].astype(jnp.float32) + edge).reshape(LF * BP, 128))
            for k, value in enumerate(pair(*both)):
                at = (1 + k) * HW + 128 * i
                grads[:, at : at + 128] = value
                start = KEYS_AT + D * (3 * k + i)
                src[start : start + D, :] = jnp.dot(
                    tok_t, value, preferred_element_type=jnp.float32
                ).astype(jnp.bfloat16)

    def token_grads():
        tg_ref[...] = lax.dot_general(
            grads[...], wqkv[...], (((1,), (1,)), ((), ())), preferred_element_type=jnp.float32
        ).astype(jnp.bfloat16)

    def stages(c, p):
        b0, hs, b1, s1, h2, b2, b3 = (early, late)[p]
        first, second = FIRST[c], SECOND[c]
        half_rows, piece = HALVES[p], PIECES[p]
        length = half_rows // first
        step = half_rows // PARTS
        parts = PARTS // first
        pieces = step // piece
        base = STARTS[p] + c * half_rows
        far = STARTS[p] + (1 - c) * half_rows
        here1, here2 = rank1(c), rank2(c)

        def rows(start, index, size):
            return pl.ds(pl.multiple_of(start + index * size, 64), size)

        def copy0(k):
            return remote(
                src.at[rows(far, k, step)], b0.at[rows(0, k, step)], ss0.at[p, k], r0.at[p, k], sibling
            )

        def copy1(i, slot):
            return remote(
                hs.at[rows(0, i, length)], b1.at[rows(0, slot, length)], ss1.at[p, i],
                r1.at[p, slot], peer1(c, i),
            )

        def copy2(j, slot):
            return remote(h2.at[j], b2.at[slot], ss2.at[p, j], r2.at[p, slot], peer2(c, j))

        def copy3(j, slot):
            return remote(b3.at[slot], b3.at[slot], ss3.at[p, j], r3.at[p, slot], peer2(c, j))

        def copy4(i, chunk):
            where = rows(base, chunk, length)
            return remote(out.at[where], out.at[where], ss4.at[p, i], r4.at[p, chunk], peer1(c, i))

        def copy5(chunk):
            where = rows(base, chunk, length)
            return remote(out.at[where], out.at[where], ss5.at[p, chunk], r5.at[p, chunk], sibling)

        def from_sibling(chunk):
            where = rows(far, chunk, half_rows // FIRST[1 - c])
            return remote(out.at[where], out.at[where], ss5.at[p, chunk], r5.at[p, chunk], sibling)

        def loop(low, high, body):
            def run(n, carry):
                body(n)
                return carry

            lax.fori_loop(low, high, run, 0)

        def send_pair():
            begin = ((rank1(1 - c) + 1) % FIRST[1 - c]) * (PARTS // FIRST[1 - c])
            loop(0, PARTS, lambda n: copy0((begin + n) % PARTS).start())

        def both(k):
            copy0(k).wait_recv()
            mine = src[rows(base, k, step), :].astype(jnp.float32)
            return mine + b0[rows(0, k, step), :].astype(jnp.float32)

        def send_first():
            def one(n):
                i = (here1 + n) % first
                for e in range(parts):
                    k = i * parts + e
                    hs[rows(0, k, step), :] = both(k).astype(jnp.bfloat16)
                copy1(i, here1).start()

            loop(1, first, one)
            for e in range(parts):
                own = both(here1 * parts + e)
                s1[e * pieces : (e + 1) * pieces] = own.reshape(pieces, piece, 128)

        def send_second():
            def one(n):
                i = (here1 + first - n) % first
                copy1(i, i).wait_recv()
                more = b1[rows(0, i, length), :].astype(jnp.float32)
                s1[0:second] += more.reshape(second, piece, 128)

            loop(1, first, one)
            h2[0:second] = s1[0:second].astype(jnp.bfloat16)
            loop(1, second, lambda n: copy2((here2 + n) % second, here2).start())

        def send_third():
            def one(n, sum_so_far):
                j = (here2 + second - n) % second
                copy2(j, j).wait_recv()
                return sum_so_far + b2[j].astype(jnp.float32)

            b3[here2] = lax.fori_loop(1, second, one, s1[here2]).astype(jnp.bfloat16)
            loop(1, second, lambda n: copy3((here2 + n) % second, here2).start())

        def send_fourth():
            def one(n):
                j = (here2 + second - n) % second
                copy3(j, j).wait_recv()

            loop(1, second, one)
            whole = b3[0:second].astype(jnp.float32).reshape(length, 128)
            out[rows(base, here1, length), :] = whole.astype(jnp.bfloat16)
            loop(1, first, lambda n: copy4((here1 + n) % first, here1).start())
            copy5(here1).start()

        def send_fifth():
            def one(n):
                i = (here1 + first - n) % first
                copy4(i, i).wait_recv()
                copy5(i).start()

            loop(1, first, one)

        def end():
            loop(0, FIRST[1 - c], lambda n: from_sibling(n).wait_recv())
            loop(0, PARTS, lambda n: copy0(n).wait_send())

            def one(n):
                i = (here1 + n) % first
                copy1(i, here1).wait_send()
                copy4(i, here1).wait_send()
                copy5(i).wait_send()

            loop(1, first, one)
            copy5(here1).wait_send()

            def two(n):
                j = (here2 + n) % second
                copy2(j, here2).wait_send()
                copy3(j, here2).wait_send()

            loop(1, second, two)

        return send_pair, send_first, send_second, send_third, send_fourth, send_fifth, end

    def sum_all(c):
        a, b = stages(c, 0), stages(c, 1)
        query_terms()
        a[0]()
        key_terms()
        b[0]()
        a[1]()
        b[1]()
        a[2]()
        b[2]()
        a[3]()
        token_grads()
        b[3]()
        a[4]()
        b[4]()
        a[5]()
        b[5]()
        a[6]()
        b[6]()

    for c in range(2):
        pl.when(core == c)(functools.partial(sum_all, c))

    @pl.when(is_worker == 1)
    def _():
        def finish(i, carry):
            halo_copy(i).wait_send()

            @pl.when(i != s)
            def _():
                query_copy(i).wait_send()

            return carry

        def finish_keys(i, carry):
            to = each * half + i

            @pl.when(to != s)
            def _():
                key_copy(to).wait_send()

            return carry

        lax.fori_loop(0, slots, finish, 0)
        lax.fori_loop(0, each, finish_keys, 0)
        pair_copy.wait_send()


def finish(res_q, res_kv, tokens, grad_out, w_qkv, slots, tm_size):
    hbm = pl.BlockSpec(memory_space=pltpu.HBM)
    vmem = pl.BlockSpec(memory_space=pltpu.VMEM)
    dma = pltpu.SemaphoreType.DMA
    sums = [
        [pltpu.VMEM((HALVES[p], 128), jnp.bfloat16)] * 3
        + [pltpu.VMEM((16, PIECES[p], 128), jnp.float32)]
        + [pltpu.VMEM((16, PIECES[p], 128), jnp.bfloat16)] * 3
        for p in range(2)
    ]
    return pl.pallas_call(
        functools.partial(finish_kernel, slots, tm_size),
        out_shape=(
            jax.ShapeDtypeStruct((LF * BP, D), jnp.bfloat16),
            jax.ShapeDtypeStruct((ROWS, 128), jnp.bfloat16),
        ),
        in_specs=[vmem, vmem] + [hbm] * 3,
        out_specs=(vmem, vmem),
        scratch_shapes=[
            pltpu.VMEM((2, HEADS, 2, BP, 128), jnp.bfloat16),
            pltpu.VMEM((HEADS, LF, BP, 128), jnp.bfloat16),
            pltpu.VMEM((2, HEADS, 2, BP, 128), jnp.bfloat16),
            pltpu.VMEM((slots // 2, LF, BP, 128), jnp.bfloat16),
            pltpu.VMEM((slots // 2, LF, BP, 128), jnp.bfloat16),
            pltpu.VMEM(tokens.shape, jnp.bfloat16),
            pltpu.VMEM(grad_out.shape, jnp.bfloat16),
            pltpu.VMEM(w_qkv.shape, jnp.bfloat16),
            pltpu.VMEM((LF * BP, 3 * HW), jnp.bfloat16),
            pltpu.VMEM((LF * BP, HW), jnp.bfloat16),
            pltpu.VMEM((ROWS, 128), jnp.bfloat16),
            *sums,
            dma((3,)), dma((2,)), dma((slots,)), dma((slots,)), dma((slots,)), dma, dma, dma,
            *[dma((2, size)) for size in (8, 8, 8, 8, 16, 16, 16, 16, 8, 8, 8, 8)],
        ],
        compiler_params=pltpu.CompilerParams(
            has_side_effects=True, collective_id=2, vmem_limit_bytes=32 << 20
        ),
        name="finish",
    )(res_q, res_kv, tokens, grad_out, w_qkv)


def widen_kernel(src, tg, qkv, out, tg_out, wide, wide_out, sem):
    step = 96
    copies = [pltpu.make_async_copy(tg, tg_out, sem.at[0])]
    copies[0].start()
    for k in range(D // step):
        rows = pl.ds(step * k, step)
        for i in range(9):
            start = D * i if i < 3 else KEYS_AT + D * (i - 3)
            part = src[start + step * k : start + step * (k + 1), :]
            wide[rows, 128 * i : 128 * (i + 1)] = part.astype(jnp.float32)
        copies.append(pltpu.make_async_copy(wide.at[rows], qkv.at[rows], sem.at[len(copies)]))
        copies[-1].start()
    for k in range(HW // step):
        rows = pl.ds(step * k, step)
        for i in range(6):
            start = 3 * D + HW * i
            part = src[start + step * k : start + step * (k + 1), :]
            wide_out[rows, 128 * i : 128 * (i + 1)] = part.astype(jnp.float32)
        copies.append(pltpu.make_async_copy(wide_out.at[rows], out.at[rows], sem.at[len(copies)]))
        copies[-1].start()
    for copy in copies:
        copy.wait()


def widen(terms, token_grads):
    vmem = pl.BlockSpec(memory_space=pltpu.VMEM)
    hbm = pl.BlockSpec(memory_space=pltpu.HBM)
    return pl.pallas_call(
        widen_kernel,
        out_shape=(
            jax.ShapeDtypeStruct((D, 3 * HW), jnp.float32),
            jax.ShapeDtypeStruct((HW, D), jnp.float32),
            jax.ShapeDtypeStruct(token_grads.shape, jnp.bfloat16),
        ),
        in_specs=[vmem, vmem],
        out_specs=(hbm, hbm, hbm),
        scratch_shapes=[
            pltpu.VMEM((D, 3 * HW), jnp.float32),
            pltpu.VMEM((HW, D), jnp.float32),
            pltpu.SemaphoreType.DMA((1 + (D + HW) // 96,)),
        ],
        compiler_params=pltpu.CompilerParams(vmem_limit_bytes=32 << 20),
        name="widen",
    )(terms, token_grads)


def shards(tokens, grad_out, w_qkv, w_out, brain_mask, block_table):
    slots = lax.axis_size("space")
    tm_size = lax.axis_size("tm")
    flat_tokens = tokens.reshape(-1, D)
    flat_grad = grad_out.reshape(-1, D)
    held = spread(flat_tokens, flat_grad, w_qkv, w_out, slots, tm_size)
    res_q, res_kv = attend(block_table, brain_mask, held, tm_size)
    token_grads, terms = finish(res_q, res_kv, flat_tokens, flat_grad, w_qkv, slots, tm_size)
    qkv_grads, out_grads, token_grads = widen(terms, token_grads)
    return (token_grads.reshape(tokens.shape), qkv_grads, out_grads)


def solution(mesh):
    in_specs = (P("space", "tm", None, None), P("space", "tm", None, None), P(), P(), P(), P())
    out_specs = (P("space", "tm", None, None), P(), P())
    return jax.shard_map(shards, mesh=mesh, in_specs=in_specs, out_specs=out_specs, check_vma=False)
```
